32 devices in a mesh: grp: 2 (over y), basin: 4 (over z), chain: 2 (over x), mem: 2 (over core).
Axes of the slice: x: 2, y: 2, z: 4, core: 2. Of those that a mesh axis runs over, the one named last changes fastest.
Arguments:
- runoff: float32 [2, 64, 32, 2, 2048], P('mem', 'basin', 'grp', 'chain'), parts along dimension 2, may hold values from 0.002 to 0.02
- directions: int32 [32, 2, 2048], P(('grp', 'basin'), 'chain'), parts along dimension 0, may hold values from 0 to 2
Outputs:
- accumulation: float32 [128, 32, 2, 2048], P('mem', ('grp', 'basin'), 'chain'), parts along dimension 1
The draws below stay inside these ranges and needn't reach their ends.
There are 2 independent parts, one for each index of `grp`. The reference program is written for one: setup_inputs(seed, part) draws one part's arguments, and reference() takes and returns one part's arrays. A program takes and returns all parts, laid end to end along the dimension named above; each array names one. Nothing has to cross between parts.
Inputs may be any that keep to these rules, and one draw needn't show every extreme that they name: `directions`: direction codes of forward three-direction routing: 0 east, 1 north-east, 2 south-east along the flow.
All inputs are finite; a program needn't handle non-finite values.
Results may differ from the reference program's by a relative error of at most 0.0003.
Values sent between devices are 32-bit elements; how exact they have to be, the bound alone decides.
No kernel may reach another device: no remote copies, remote signals or barrier semaphores. Data moves between devices by JAX's collectives and lax.ppermute only.
A program may use at most 128 MiB of HBM per device.

```python
import math
import jax
import jax.numpy as jnp
from jax import lax

ROWS = 128
CELLS = 2048
COLS = 16
MEMBERS = 128
TILES = 16
SECTIONS = 2
HALVES = 2
HALF = 64


def place_ends(drawn, key, smallest, largest):
    shape = drawn.shape
    spot = [jax.random.randint(jax.random.fold_in(key, axis), (), 0, shape[axis]) for axis in range(len(shape))]
    drawn = drawn.at[tuple(spot)].set(smallest)
    longest = shape.index(max(shape))
    spot[longest] = (spot[longest] + 1) % shape[longest]
    return drawn.at[tuple(spot)].set(largest)


def steps_of(rng, dims, shards, smallest, top_value):
    level = 1.0
    for position, parts in shards:
        draws = jax.random.uniform(jax.random.fold_in(jax.random.fold_in(rng, 6), position), (parts,), jnp.float32, smallest / len(shards), top_value / len(shards))
        level = level * jnp.repeat(jnp.exp(draws), dims[position] // parts).reshape((-1,) + (1,) * (len(dims) - 1 - position))
    return level


def setup_inputs(seed: int = 0, part: int = 0) -> dict:
    splits = jax.random.split(jax.random.key(seed), 3)
    part_keys = jax.random.split(jax.random.fold_in(splits[2], part), 3)
    runoff = jnp.clip(jnp.exp(math.log(0.02) - 2.30258502 * jax.random.uniform(part_keys[0], (HALVES, HALF, TILES, SECTIONS, CELLS), jnp.float32) ** steps_of(part_keys[0], (HALVES, HALF, TILES, SECTIONS, CELLS), ((0, 2), (1, 4), (3, 2)), -0.2, 0.2)), 0.002, 0.02)
    directions = place_ends(jax.random.randint(part_keys[1], (TILES, SECTIONS, CELLS), 0, 3), jax.random.fold_in(part_keys[1], 1), 0, 2).astype(jnp.int32)
    return dict(runoff=runoff, directions=directions)


def target_rows(directions):
    row_ids = jnp.arange(CELLS, dtype=jnp.int32) % ROWS
    offsets = jnp.where(directions == 1, -1, jnp.where(directions == 2, 1, 0)).astype(jnp.int32)
    return jnp.clip(row_ids + offsets, 0, ROWS - 1).astype(jnp.int32)


def reference(runoff, directions):
    water_all = runoff.reshape(MEMBERS, TILES, SECTIONS, COLS, ROWS)
    targets = target_rows(directions).reshape(TILES, SECTIONS, COLS, ROWS)
    lane_ids = jnp.arange(ROWS, dtype=jnp.int32)

    def section_sweep(inflow, section_data):
        water_section, target_section = section_data

        def advance(carried, column_data):
            water_col, target_col = column_data
            summed = water_col + carried
            onehot = (target_col[:, :, None] == lane_ids[None, None, :]).astype(jnp.float32)
            passed = jnp.einsum("mtj,tji->mti", summed, onehot, precision=lax.Precision.HIGHEST)
            return passed, summed

        outflow, columns_out = lax.scan(advance, inflow, (jnp.moveaxis(water_section, 2, 0), jnp.moveaxis(target_section, 1, 0)))
        return outflow, columns_out

    no_inflow = jnp.zeros((MEMBERS, TILES, ROWS), jnp.float32)
    _, result = lax.scan(section_sweep, no_inflow, (jnp.moveaxis(water_all, 2, 0), jnp.moveaxis(targets, 1, 0)))
    return jnp.transpose(result, (2, 3, 0, 1, 4)).reshape(MEMBERS, TILES, SECTIONS, CELLS)
```

```python
import functools

import jax
import jax.numpy as jnp
from jax import lax
from jax.experimental import pallas as pl
from jax.experimental.pallas import tpu as pltpu
from jax.sharding import PartitionSpec as P

ROWS = 128
SUB = 8


def exchange_pairs(count, k):
    if count & (count - 1) == 0:
        return [(i, i ^ k) for i in range(count)]
    return [(i, (i + k) % count) for i in range(count)]


def reversed_pairs(pairs):
    return [(target, source) for source, target in pairs]


def looked_up(pairs, index):
    table = [0] * len(pairs)
    for source, target in pairs:
        table[source] = target
    return jnp.array(table, jnp.int32)[index]


def from_behind(value, axis):
    count = lax.axis_size(axis)
    return lax.ppermute(value, axis, [(i, i + 1) for i in range(count - 1)])


def column_masks(d_ref, col, tile_count, col_count):
    codes = d_ref[pl.ds(col, tile_count, col_count), :]
    codes = jnp.concatenate([codes] * (SUB // tile_count), axis=0)
    lane = lax.broadcasted_iota(jnp.int32, codes.shape, 1)
    north = (codes == 1) & (lane > 0)
    south = (codes == 2) & (lane < ROWS - 1)
    return north, south


def advance(summed, north, south):
    zero = jnp.zeros_like(summed)
    up = pltpu.roll(jnp.where(north, summed, zero), ROWS - 1, 1)
    down = pltpu.roll(jnp.where(south, summed, zero), 1, 1)
    return jnp.where(north | south, zero, summed) + (up + down)


def sweep_rows(x_ref, d_ref, carried, o_ref, tile_count, col_count):
    groups = len(carried)
    for col in range(col_count):
        masks = column_masks(d_ref, col, tile_count, col_count)
        for g in range(groups):
            rows = pl.ds(g * SUB * col_count + col, SUB, col_count)
            summed = x_ref[rows, :]
            if carried[g] is not None:
                summed = summed + carried[g]
            if o_ref is not None:
                o_ref[rows, :] = summed
            if o_ref is None or col < col_count - 1:
                carried[g] = advance(summed, *masks)
    return carried


def pack(x, block, tile_count):
    members, _, col_count, _ = x.shape
    parts = 4 if members % 4 == 0 else 1
    step = members // parts

    def body(block_ref, x_ref, o_ref, sems):
        tiles = pl.ds(block_ref[0] * tile_count, tile_count)
        copies = [
            pltpu.make_async_copy(
                x_ref.at[pl.ds(i * step, step), tiles], o_ref.at[pl.ds(i * step, step)], sems.at[i]
            )
            for i in range(parts)
        ]
        for copy in copies:
            copy.start()
        for copy in copies:
            copy.wait()

    out = pl.pallas_call(
        body,
        out_shape=jax.ShapeDtypeStruct((members, tile_count, col_count, ROWS), x.dtype),
        grid_spec=pltpu.PrefetchScalarGridSpec(
            num_scalar_prefetch=1,
            grid=(1,),
            in_specs=[pl.BlockSpec(memory_space=pl.ANY)],
            out_specs=pl.BlockSpec(memory_space=pl.ANY),
            scratch_shapes=[pltpu.SemaphoreType.DMA((parts,))],
        ),
        name="pack",
    )(block, x)
    return out.reshape(members * tile_count * col_count, ROWS)


def pack_with_inflow(x, block, inflow, tile_count):
    members, _, col_count, _ = x.shape
    count = members * tile_count

    def body(block_ref, x_ref, in_ref, o_ref):
        o_ref[...] = x_ref[...].reshape(o_ref.shape)
        rows = pl.ds(0, count, col_count)
        o_ref[rows, :] = o_ref[rows, :] + in_ref[...]

    return pl.pallas_call(
        body,
        out_shape=jax.ShapeDtypeStruct((count * col_count, ROWS), x.dtype),
        grid_spec=pltpu.PrefetchScalarGridSpec(
            num_scalar_prefetch=1,
            grid=(1,),
            in_specs=[
                pl.BlockSpec((members, tile_count, col_count, ROWS), lambda i, b: (0, b[0], 0, 0)),
                pl.BlockSpec((count, ROWS), lambda i, b: (0, 0)),
            ],
            out_specs=pl.BlockSpec((count * col_count, ROWS), lambda i, b: (0, 0)),
        ),
        name="pack_with_inflow",
    )(block, x, inflow)


def source_panels(x, blocks, dirs, inflow, tile_count):
    members, _, col_count, _ = x.shape
    count = members * tile_count
    listed = blocks.shape[0]

    def body(blocks_ref, x_ref, d_ref, in_ref, o_ref):
        flat = x_ref.reshape(count * col_count, ROWS)
        codes = d_ref.reshape(tile_count * col_count, ROWS)
        carried = [in_ref[0, pl.ds(g * SUB, SUB), :] for g in range(count // SUB)]
        carried = sweep_rows(flat, codes, carried, None, tile_count, col_count)
        for g in range(count // SUB):
            o_ref[0, pl.ds(g * SUB, SUB), :] = carried[g]

    return pl.pallas_call(
        body,
        out_shape=jax.ShapeDtypeStruct((listed, count, ROWS), x.dtype),
        grid_spec=pltpu.PrefetchScalarGridSpec(
            num_scalar_prefetch=1,
            grid=(listed,),
            in_specs=[
                pl.BlockSpec((members, tile_count, col_count, ROWS), lambda i, b: (0, b[i], 0, 0)),
                pl.BlockSpec((1, tile_count, col_count, ROWS), lambda i, b: (i, 0, 0, 0)),
                pl.BlockSpec((1, count, ROWS), lambda i, b: (i, 0, 0)),
            ],
            out_specs=pl.BlockSpec((1, count, ROWS), lambda i, b: (i, 0, 0)),
        ),
        name="source_panels",
    )(blocks, x, dirs, inflow)


def chunk_panel(chunk, codes, inflow, tile_count):
    count = inflow.shape[0]
    col_count = chunk.shape[0] // count

    def body(x_ref, d_ref, in_ref, o_ref):
        carried = [in_ref[pl.ds(g * SUB, SUB), :] for g in range(count // SUB)]
        carried = sweep_rows(x_ref, d_ref, carried, None, tile_count, col_count)
        for g in range(count // SUB):
            o_ref[pl.ds(g * SUB, SUB), :] = carried[g]

    return pl.pallas_call(
        body, out_shape=jax.ShapeDtypeStruct(inflow.shape, chunk.dtype), name="chunk_panel"
    )(chunk, codes, inflow)


def chunk_result(chunk, codes, inflow, result, block, tile_count, shape):
    col_count = codes.shape[0] // tile_count
    rows = chunk.shape[0]
    groups = rows // (col_count * SUB)
    aliases = {}
    operands = [block, chunk, codes]
    specs = [
        pl.BlockSpec((rows, ROWS), lambda i, b: (0, 0)),
        pl.BlockSpec(codes.shape, lambda i, b: (0, 0)),
    ]
    if inflow is not None:
        operands.append(inflow)
        specs.append(pl.BlockSpec(inflow.shape, lambda i, b: (0, 0)))
    if result is not None:
        aliases = {len(operands): 0}
        operands.append(result)
        specs.append(pl.BlockSpec(memory_space=pl.ANY))

    def body(block_ref, x_ref, d_ref, *rest):
        o_ref = rest[-1]
        carried = [None] * groups
        if inflow is not None:
            carried = [rest[0][pl.ds(g * SUB, SUB), :] for g in range(groups)]
        sweep_rows(x_ref, d_ref, carried, o_ref, tile_count, col_count)

    return pl.pallas_call(
        body,
        out_shape=jax.ShapeDtypeStruct(shape, chunk.dtype),
        grid_spec=pltpu.PrefetchScalarGridSpec(
            num_scalar_prefetch=1,
            grid=(1,),
            in_specs=specs,
            out_specs=pl.BlockSpec((rows, ROWS), lambda i, b: (b[0], 0)),
        ),
        input_output_aliases=aliases,
        name="chunk_result",
    )(*operands)


def local(runoff, directions):
    basins, chain = lax.axis_size("basin"), lax.axis_size("chain")
    _, members, all_tiles, _, cell_count = runoff.shape
    tile_count = directions.shape[0]
    col_count = cell_count // ROWS
    count = members * tile_count
    x = runoff.reshape(members, all_tiles, col_count, ROWS)
    d = directions.reshape(tile_count, col_count, ROWS)
    codes = d.reshape(tile_count * col_count, ROWS)
    me = lax.axis_index("basin")

    first = basins // 2
    late = [k for k in range(basins - 1, 0, -1) if k != first]
    pairs = {k: exchange_pairs(basins, k) for k in range(basins)}
    target = {k: looked_up(pairs[k], me)[None] for k in pairs}
    origin = {k: looked_up(reversed_pairs(pairs[k]), me)[None] for k in pairs}

    listed = [0] + late
    dirs = jnp.stack([d] + [lax.ppermute(d, "basin", reversed_pairs(pairs[k])) for k in late])
    blocks = jnp.concatenate([target[k] for k in listed])

    arrived = {first: lax.ppermute(pack(x, target[first], tile_count), "basin", pairs[first])}

    inflows = jnp.zeros((len(listed), count, ROWS), jnp.float32)
    for _ in range(chain - 1):
        inflows = from_behind(source_panels(x, blocks, dirs, inflows, tile_count), "chain")
    for i, k in enumerate(listed):
        chunk = pack_with_inflow(x, target[k], inflows[i], tile_count)
        arrived[k] = lax.ppermute(chunk, "basin", pairs[k]) if k else chunk

    inflow = jnp.zeros((count, ROWS), jnp.float32)
    for _ in range(chain - 1):
        inflow = from_behind(chunk_panel(arrived[first], codes, inflow, tile_count), "chain")

    shape = (basins * count * col_count, ROWS)
    result = None
    for k in [0, first] + late:
        result = chunk_result(
            arrived[k], codes, inflow if k == first else None, result, origin[k], tile_count, shape
        )
    return result.reshape(basins * members, tile_count, 1, cell_count)


def solution(mesh):
    return jax.shard_map(
        local,
        mesh=mesh,
        in_specs=(P("mem", "basin", "grp", "chain", None), P(("grp", "basin"), "chain", None)),
        out_specs=P("mem", ("grp", "basin"), "chain", None),
        check_vma=False,
    )
```

```python
import jax
import jax.numpy as jnp
from jax import lax
from jax.experimental import pallas as pl
from jax.experimental.pallas import tpu as pltpu
from jax.sharding import PartitionSpec as P

ROWS = 128
SUB = 8
HBM = pl.BlockSpec(memory_space=pl.ANY)
VMEM = pl.BlockSpec(memory_space=pltpu.VMEM)


def exchange_pairs(count, k):
    if count & (count - 1) == 0:
        return [(i, i ^ k) for i in range(count)]
    return [(i, (i + k) % count) for i in range(count)]


def reversed_pairs(pairs):
    return [(target, source) for source, target in pairs]


def target_of(k, count):
    me = lax.axis_index("basin")
    return me ^ k if count & (count - 1) == 0 else lax.rem(me + k, count)


def origin_of(k, count):
    me = lax.axis_index("basin")
    return me ^ k if count & (count - 1) == 0 else lax.rem(me + count - k, count)


def from_behind(value, axis):
    count = lax.axis_size(axis)
    return lax.ppermute(value, axis, [(i, i + 1) for i in range(count - 1)])


class Sizes:
    def __init__(self, members, tiles, columns, basins):
        self.members, self.tiles, self.columns, self.basins = members, tiles, columns, basins
        self.per_member = tiles * columns
        self.count = members * tiles
        self.rows = members * tiles * columns
        self.groups = self.count // SUB


def column_masks(d_ref, col, sizes):
    codes = d_ref[pl.ds(col, sizes.tiles, sizes.columns), :]
    codes = jnp.concatenate([codes] * (SUB // sizes.tiles), axis=0)
    lane = lax.broadcasted_iota(jnp.int32, codes.shape, 1)
    north = (codes == 1) & (lane > 0)
    south = (codes == 2) & (lane < ROWS - 1)
    return north, south


def advance(summed, north, south):
    zero = jnp.zeros_like(summed)
    up = pltpu.roll(jnp.where(north, summed, zero), ROWS - 1, 1)
    down = pltpu.roll(jnp.where(south, summed, zero), 1, 1)
    return jnp.where(north | south, zero, summed) + (up + down)


def sweep(x_ref, d_ref, carried, o_ref, sizes):
    for col in range(sizes.columns):
        north, south = column_masks(d_ref, col, sizes)
        for g in range(sizes.groups):
            rows = pl.ds(g * SUB * sizes.columns + col, SUB, sizes.columns)
            summed = x_ref[rows, :]
            if carried[g] is not None:
                summed = summed + carried[g]
            if o_ref is not None:
                o_ref[rows, :] = summed
            if o_ref is None or col < sizes.columns - 1:
                carried[g] = advance(summed, north, south)
    return carried


def registers(in_ref, i, sizes):
    if in_ref is None:
        return [None] * sizes.groups
    return [in_ref[i, pl.ds(g * SUB, SUB), :] for g in range(sizes.groups)]


def store_registers(o_ref, i, carried):
    for g, value in enumerate(carried):
        o_ref[i, pl.ds(g * SUB, SUB), :] = value


def gather_copies(x_ref, buf_ref, sem, block, sizes):
    size = sizes.per_member
    return [
        pltpu.make_async_copy(
            x_ref.at[m, pl.ds(block * size, size)], buf_ref.at[pl.ds(m * size, size)], sem.at[m]
        )
        for m in range(sizes.members)
    ]


def start_all(copies):
    for copy in copies:
        copy.start()


def wait_all(copies):
    for copy in copies:
        copy.wait()


def chunk_shape(sizes):
    return jax.ShapeDtypeStruct((sizes.rows, ROWS), jnp.float32)


def panel_shape(listed, sizes):
    return jax.ShapeDtypeStruct((listed, sizes.count, ROWS), jnp.float32)


def result_shape(sizes):
    return jax.ShapeDtypeStruct((sizes.basins * sizes.rows, ROWS), jnp.float32)


def params(sizes, chunks):
    return pltpu.CompilerParams(vmem_limit_bytes=(chunks * sizes.rows + 4096) * ROWS * 4)


def cost(chunks):
    return pl.CostEstimate(flops=chunks * (1 << 20), bytes_accessed=chunks * (1 << 20), transcendentals=0)


def pack(x, k, sizes):
    def body(x_ref, o_ref, sem):
        copies = gather_copies(x_ref, o_ref, sem, target_of(k, sizes.basins), sizes)
        start_all(copies)
        wait_all(copies)

    return pl.pallas_call(
        body,
        out_shape=chunk_shape(sizes),
        in_specs=[HBM],
        out_specs=VMEM,
        scratch_shapes=[pltpu.SemaphoreType.DMA((sizes.members,))],
        cost_estimate=cost(1),
        compiler_params=params(sizes, 2),
        name="pack",
    )(x)


def source_panels(x, ks, codes, inflow, sizes):
    listed = len(ks)

    def body(x_ref, *rest):
        d_refs, rest = rest[:listed], rest[listed:]
        in_ref = rest[0] if inflow is not None else None
        o_ref, buf, sem = rest[-3:]
        copies = [
            gather_copies(x_ref, buf.at[i], sem.at[i], target_of(k, sizes.basins), sizes)
            for i, k in enumerate(ks)
        ]
        for c in copies:
            start_all(c)
        for i in range(listed):
            wait_all(copies[i])
            store_registers(
                o_ref, i, sweep(buf.at[i], d_refs[i], registers(in_ref, i, sizes), None, sizes)
            )

    return pl.pallas_call(
        body,
        out_shape=panel_shape(listed, sizes),
        in_specs=[HBM] + [VMEM] * (listed + (inflow is not None)),
        out_specs=VMEM,
        scratch_shapes=[
            pltpu.VMEM((listed, sizes.rows, ROWS), jnp.float32),
            pltpu.SemaphoreType.DMA((listed, sizes.members)),
        ],
        cost_estimate=cost(listed),
        compiler_params=params(sizes, 2 * listed),
        name="source_panels",
    )(x, *codes, *([inflow] if inflow is not None else []))


def source_chunk(x, k, codes, inflow, i, sizes):
    def body(x_ref, d_ref, in_ref, o_ref, buf, sem):
        copies = gather_copies(x_ref, buf, sem, target_of(k, sizes.basins), sizes)
        start_all(copies)
        wait_all(copies)
        sweep(buf, d_ref, registers(in_ref, i, sizes), o_ref, sizes)

    return pl.pallas_call(
        body,
        out_shape=chunk_shape(sizes),
        in_specs=[HBM, VMEM, VMEM],
        out_specs=VMEM,
        scratch_shapes=[
            pltpu.VMEM((sizes.rows, ROWS), jnp.float32),
            pltpu.SemaphoreType.DMA((sizes.members,)),
        ],
        cost_estimate=cost(1),
        compiler_params=params(sizes, 3),
        name="source_chunk",
    )(x, codes, inflow)


def own_result(x, codes, inflow, sizes):
    def body(x_ref, d_ref, in_ref, o_ref, buf, out, sem, out_sem):
        copies = gather_copies(x_ref, buf, sem, lax.axis_index("basin"), sizes)
        start_all(copies)
        wait_all(copies)
        sweep(buf, d_ref, registers(in_ref, 0, sizes), out, sizes)
        place = o_ref.at[pl.ds(lax.axis_index("basin") * sizes.rows, sizes.rows)]
        copy = pltpu.make_async_copy(out, place, out_sem)
        copy.start()
        copy.wait()

    return pl.pallas_call(
        body,
        out_shape=result_shape(sizes),
        in_specs=[HBM, VMEM, VMEM],
        out_specs=HBM,
        scratch_shapes=[
            pltpu.VMEM((sizes.rows, ROWS), jnp.float32),
            pltpu.VMEM((sizes.rows, ROWS), jnp.float32),
            pltpu.SemaphoreType.DMA((sizes.members,)),
            pltpu.SemaphoreType.DMA,
        ],
        cost_estimate=cost(1),
        compiler_params=params(sizes, 3),
        name="own_result",
    )(x, codes, inflow)


def arrived_panels(chunks, codes, inflow, sizes):
    listed = len(chunks)

    def body(*refs):
        x_refs, d_ref, o_ref = refs[:listed], refs[listed], refs[-1]
        in_ref = refs[listed + 1] if inflow is not None else None
        for i in range(listed):
            store_registers(
                o_ref, i, sweep(x_refs[i], d_ref, registers(in_ref, i, sizes), None, sizes)
            )

    return pl.pallas_call(
        body,
        out_shape=panel_shape(listed, sizes),
        in_specs=[VMEM] * (listed + 1 + (inflow is not None)),
        out_specs=VMEM,
        cost_estimate=cost(listed),
        compiler_params=params(sizes, 2 * listed),
        name="arrived_panels",
    )(*chunks, codes, *([inflow] if inflow is not None else []))


def arrived_result(chunks, ks, codes, inflow, result, sizes):
    listed = len(chunks)

    def body(*refs):
        x_refs, d_ref, in_ref = refs[:listed], refs[listed], refs[listed + 1]
        o_ref, out, sem = refs[-3:]
        copies = []
        for i, k in enumerate(ks):
            sweep(x_refs[i], d_ref, registers(in_ref, i, sizes), out.at[i], sizes)
            place = o_ref.at[pl.ds(origin_of(k, sizes.basins) * sizes.rows, sizes.rows)]
            copies.append(pltpu.make_async_copy(out.at[i], place, sem.at[i]))
            copies[i].start()
        wait_all(copies)

    return pl.pallas_call(
        body,
        out_shape=result_shape(sizes),
        in_specs=[VMEM] * (listed + 2) + [HBM],
        out_specs=HBM,
        scratch_shapes=[
            pltpu.VMEM((listed, sizes.rows, ROWS), jnp.float32),
            pltpu.SemaphoreType.DMA((listed,)),
        ],
        input_output_aliases={listed + 2: 0},
        cost_estimate=cost(listed),
        compiler_params=params(sizes, 3 * listed),
        name="arrived_result",
    )(*chunks, codes, inflow, result)


def place_chunk(chunk, k, result, sizes):
    def body(x_ref, _, o_ref, sem):
        place = o_ref.at[pl.ds(origin_of(k, sizes.basins) * sizes.rows, sizes.rows)]
        copy = pltpu.make_async_copy(x_ref, place, sem)
        copy.start()
        copy.wait()

    return pl.pallas_call(
        body,
        out_shape=result_shape(sizes),
        in_specs=[VMEM, HBM],
        out_specs=HBM,
        scratch_shapes=[pltpu.SemaphoreType.DMA],
        input_output_aliases={1: 0},
        cost_estimate=cost(1),
        compiler_params=params(sizes, 2),
        name="place_chunk",
    )(chunk, result)


def local(runoff, directions):
    basins, chain = lax.axis_size("basin"), lax.axis_size("chain")
    _, members, all_tiles, _, cell_count = runoff.shape
    sizes = Sizes(members, directions.shape[0], cell_count // ROWS, basins)
    x = runoff.reshape(members, all_tiles * sizes.columns, ROWS)
    codes = directions.reshape(sizes.per_member, ROWS)

    early = sorted({basins // 2, 1}, reverse=True)
    late = [k for k in range(basins - 1, 0, -1) if k not in early]
    pairs = {k: exchange_pairs(basins, k) for k in range(basins)}
    listed = [0] + late

    arrived = {k: lax.ppermute(pack(x, k, sizes), "basin", pairs[k]) for k in early}
    dirs = [codes] + [lax.ppermute(codes, "basin", reversed_pairs(pairs[k])) for k in late]

    inflow = None
    for _ in range(chain - 1):
        inflow = from_behind(source_panels(x, listed, dirs, inflow, sizes), "chain")
    if inflow is None:
        inflow = jnp.zeros((len(listed), sizes.count, ROWS), jnp.float32)
    for i, k in enumerate(listed):
        if k:
            arrived[k] = lax.ppermute(source_chunk(x, k, dirs[i], inflow, i, sizes), "basin", pairs[k])
    result = own_result(x, codes, inflow, sizes)

    chunks = [arrived[k] for k in early]
    inflow = None
    for _ in range(chain - 1):
        inflow = from_behind(arrived_panels(chunks, codes, inflow, sizes), "chain")
    if inflow is None:
        inflow = jnp.zeros((len(early), sizes.count, ROWS), jnp.float32)
    result = arrived_result(chunks, early, codes, inflow, result, sizes)
    for k in late:
        result = place_chunk(arrived[k], k, result, sizes)
    return result.reshape(basins * members, sizes.tiles, 1, cell_count)


def solution(mesh):
    return jax.shard_map(
        local,
        mesh=mesh,
        in_specs=(P("mem", "basin", "grp", "chain", None), P(("grp", "basin"), "chain", None)),
        out_specs=P("mem", ("grp", "basin"), "chain", None),
        check_vma=False,
    )
```

```python
import jax
import jax.numpy as jnp
from jax import lax
from jax.experimental import pallas as pl
from jax.experimental.pallas import tpu as pltpu
from jax.sharding import PartitionSpec as P

ROWS = 128
SUB = 8
HBM = pl.BlockSpec(memory_space=pltpu.HBM)
VMEM = pl.BlockSpec(memory_space=pltpu.VMEM)


def exchange_pairs(count, k):
    if count & (count - 1) == 0:
        return [(i, i ^ k) for i in range(count)]
    return [(i, (i + k) % count) for i in range(count)]


def reversed_pairs(pairs):
    return [(target, source) for source, target in pairs]


def target_of(k, count):
    me = lax.axis_index("basin")
    return me ^ k if count & (count - 1) == 0 else lax.rem(me + k, count)


def origin_of(k, count):
    me = lax.axis_index("basin")
    return me ^ k if count & (count - 1) == 0 else lax.rem(me + count - k, count)


def from_behind(value, axis):
    count = lax.axis_size(axis)
    return lax.ppermute(value, axis, [(i, i + 1) for i in range(count - 1)])


class Sizes:
    def __init__(self, members, tiles, columns, basins):
        self.members, self.tiles, self.columns, self.basins = members, tiles, columns, basins
        self.per_member = tiles * columns
        self.count = members * tiles
        self.rows = members * tiles * columns
        self.groups = self.count // SUB


def column_masks(d_ref, col, sizes):
    codes = d_ref[pl.ds(col, sizes.tiles, sizes.columns), :]
    codes = jnp.concatenate([codes] * (SUB // sizes.tiles), axis=0)
    lane = lax.broadcasted_iota(jnp.int32, codes.shape, 1)
    north = (codes == 1) & (lane > 0)
    south = (codes == 2) & (lane < ROWS - 1)
    return north, south


def advance(summed, north, south):
    zero = jnp.zeros_like(summed)
    up = pltpu.roll(jnp.where(north, summed, zero), ROWS - 1, 1)
    down = pltpu.roll(jnp.where(south, summed, zero), 1, 1)
    return jnp.where(north | south, zero, summed) + (up + down)


def sweep(x_ref, d_ref, carried, o_ref, sizes):
    for col in range(sizes.columns):
        north, south = column_masks(d_ref, col, sizes)
        for g in range(sizes.groups):
            rows = pl.ds(g * SUB * sizes.columns + col, SUB, sizes.columns)
            summed = x_ref[rows, :]
            if carried[g] is not None:
                summed = summed + carried[g]
            if o_ref is not None:
                o_ref[rows, :] = summed
            if o_ref is None or col < sizes.columns - 1:
                carried[g] = advance(summed, north, south)
    return carried


def registers(in_ref, i, sizes):
    if in_ref is None:
        return [None] * sizes.groups
    return [in_ref[i, pl.ds(g * SUB, SUB), :] for g in range(sizes.groups)]


def store_registers(o_ref, i, carried):
    for g, value in enumerate(carried):
        o_ref[i, pl.ds(g * SUB, SUB), :] = value


def gather_copies(x_ref, buf_ref, sem, block, sizes):
    size = sizes.per_member
    return [
        pltpu.make_async_copy(
            x_ref.at[m, pl.ds(block * size, size)], buf_ref.at[pl.ds(m * size, size)], sem.at[m]
        )
        for m in range(sizes.members)
    ]


def start_all(copies):
    for copy in copies:
        copy.start()


def wait_all(copies):
    for copy in copies:
        copy.wait()


def chunk_shape(sizes):
    return jax.ShapeDtypeStruct((sizes.rows, ROWS), jnp.float32)


def panel_shape(listed, sizes):
    return jax.ShapeDtypeStruct((listed, sizes.count, ROWS), jnp.float32)


def result_shape(sizes):
    return jax.ShapeDtypeStruct((sizes.basins * sizes.rows, ROWS), jnp.float32)


def params(sizes, chunks):
    return pltpu.CompilerParams(vmem_limit_bytes=(chunks * sizes.rows + 4096) * ROWS * 4)


def cost(chunks):
    return pl.CostEstimate(flops=chunks, bytes_accessed=chunks, transcendentals=0)


def pack(x, k, sizes):
    def body(x_ref, o_ref, sem):
        copies = gather_copies(x_ref, o_ref, sem, target_of(k, sizes.basins), sizes)
        start_all(copies)
        wait_all(copies)

    return pl.pallas_call(
        body,
        out_shape=chunk_shape(sizes),
        in_specs=[HBM],
        out_specs=VMEM,
        scratch_shapes=[pltpu.SemaphoreType.DMA((sizes.members,))],
        cost_estimate=cost(1),
        compiler_params=params(sizes, 2),
        name="pack",
    )(x)


def source_panels(x, ks, codes, inflow, sizes):
    listed = len(ks)

    def body(x_ref, *rest):
        d_refs, rest = rest[:listed], rest[listed:]
        in_ref = rest[0] if inflow is not None else None
        o_ref, buf, sem = rest[-3:]
        copies = [
            gather_copies(x_ref, buf.at[i], sem.at[i], target_of(k, sizes.basins), sizes)
            for i, k in enumerate(ks)
        ]
        for c in copies:
            start_all(c)
        for i in range(listed):
            wait_all(copies[i])
            store_registers(
                o_ref, i, sweep(buf.at[i], d_refs[i], registers(in_ref, i, sizes), None, sizes)
            )

    return pl.pallas_call(
        body,
        out_shape=panel_shape(listed, sizes),
        in_specs=[HBM] + [VMEM] * (listed + (inflow is not None)),
        out_specs=VMEM,
        scratch_shapes=[
            pltpu.VMEM((listed, sizes.rows, ROWS), jnp.float32),
            pltpu.SemaphoreType.DMA((listed, sizes.members)),
        ],
        cost_estimate=cost(listed),
        compiler_params=params(sizes, 2 * listed),
        name="source_panels",
    )(x, *codes, *([inflow] if inflow is not None else []))


def source_chunks(x, ks, codes, inflow, sizes):
    listed = len(ks)

    def body(x_ref, *rest):
        d_refs, in_ref, o_refs = rest[:listed], rest[listed], rest[listed + 1 : 2 * listed + 1]
        buf, sem = rest[-2:]
        copies = [
            gather_copies(x_ref, buf.at[i], sem.at[i], target_of(k, sizes.basins), sizes)
            for i, k in enumerate(ks)
        ]
        for c in copies:
            start_all(c)
        for i in range(listed):
            wait_all(copies[i])
            sweep(buf.at[i], d_refs[i], registers(in_ref, i, sizes), o_refs[i], sizes)

    return pl.pallas_call(
        body,
        out_shape=[chunk_shape(sizes)] * listed,
        in_specs=[HBM] + [VMEM] * (listed + 1),
        out_specs=[VMEM] * listed,
        scratch_shapes=[
            pltpu.VMEM((listed, sizes.rows, ROWS), jnp.float32),
            pltpu.SemaphoreType.DMA((listed, sizes.members)),
        ],
        compiler_params=params(sizes, 3 * listed),
        cost_estimate=cost(listed),
        name="source_chunks",
    )(x, *codes, inflow)


def arrived_panels(chunks, codes, inflow, sizes):
    listed = len(chunks)

    def body(*refs):
        x_refs, d_ref, o_ref = refs[:listed], refs[listed], refs[-1]
        in_ref = refs[listed + 1] if inflow is not None else None
        for i in range(listed):
            store_registers(
                o_ref, i, sweep(x_refs[i], d_ref, registers(in_ref, i, sizes), None, sizes)
            )

    return pl.pallas_call(
        body,
        out_shape=panel_shape(listed, sizes),
        in_specs=[VMEM] * (listed + 1 + (inflow is not None)),
        out_specs=VMEM,
        cost_estimate=cost(listed),
        compiler_params=params(sizes, 2 * listed),
        name="arrived_panels",
    )(*chunks, codes, *([inflow] if inflow is not None else []))


def arrived_result(chunks, ks, codes, inflow, sizes):
    listed = len(chunks)

    def body(*refs):
        x_refs, d_ref, in_ref = refs[:listed], refs[listed], refs[listed + 1]
        o_ref, out, sem = refs[-3:]
        copies = []
        for i, k in enumerate(ks):
            sweep(x_refs[i], d_ref, registers(in_ref, i, sizes), out.at[i], sizes)
            place = o_ref.at[pl.ds(origin_of(k, sizes.basins) * sizes.rows, sizes.rows)]
            copies.append(pltpu.make_async_copy(out.at[i], place, sem.at[i]))
            copies[i].start()
        wait_all(copies)

    return pl.pallas_call(
        body,
        out_shape=result_shape(sizes),
        in_specs=[VMEM] * (listed + 2),
        out_specs=HBM,
        scratch_shapes=[
            pltpu.VMEM((listed, sizes.rows, ROWS), jnp.float32),
            pltpu.SemaphoreType.DMA((listed,)),
        ],
        cost_estimate=cost(listed),
        compiler_params=params(sizes, 3 * listed),
        name="arrived_result",
    )(*chunks, codes, inflow)


def place_chunk(chunk, k, result, sizes):
    def body(x_ref, _, o_ref, sem):
        place = o_ref.at[pl.ds(origin_of(k, sizes.basins) * sizes.rows, sizes.rows)]
        copy = pltpu.make_async_copy(x_ref, place, sem)
        copy.start()
        copy.wait()

    return pl.pallas_call(
        body,
        out_shape=result_shape(sizes),
        in_specs=[VMEM, HBM],
        out_specs=HBM,
        scratch_shapes=[pltpu.SemaphoreType.DMA],
        input_output_aliases={1: 0},
        cost_estimate=cost(1),
        compiler_params=params(sizes, 2),
        name="place_chunk",
    )(chunk, result)


def local(runoff, directions):
    basins, chain = lax.axis_size("basin"), lax.axis_size("chain")
    _, members, all_tiles, _, cell_count = runoff.shape
    sizes = Sizes(members, directions.shape[0], cell_count // ROWS, basins)
    x = runoff.reshape(members, all_tiles * sizes.columns, ROWS)
    x = pltpu.with_memory_space_constraint(x, pltpu.HBM)
    codes = directions.reshape(sizes.per_member, ROWS)

    early = [basins // 2]
    late = [k for k in range(basins - 1, 0, -1) if k not in early]
    pairs = {k: exchange_pairs(basins, k) for k in range(basins)}

    packed = [pack(x, k, sizes) for k in early]
    packed, codes = lax.optimization_barrier((packed, codes))
    arrived = {k: lax.ppermute(value, "basin", pairs[k]) for k, value in zip(early, packed)}
    dirs = [lax.ppermute(codes, "basin", reversed_pairs(pairs[k])) for k in late]

    inflow = None
    for _ in range(chain - 1):
        inflow = from_behind(source_panels(x, late, dirs, inflow, sizes), "chain")
    if inflow is None:
        inflow = jnp.zeros((len(late), sizes.count, ROWS), jnp.float32)
    chunks = source_chunks(x, late, dirs, inflow, sizes)
    for k, chunk in zip(late, chunks):
        arrived[k] = lax.ppermute(chunk, "basin", pairs[k])

    chunks = [pack(x, 0, sizes)] + [arrived[k] for k in early]
    inflow = None
    for _ in range(chain - 1):
        inflow = from_behind(arrived_panels(chunks, codes, inflow, sizes), "chain")
    if inflow is None:
        inflow = jnp.zeros((len(chunks), sizes.count, ROWS), jnp.float32)
    result = arrived_result(chunks, [0] + early, codes, inflow, sizes)
    for k in late:
        result = place_chunk(arrived[k], k, result, sizes)
    return result.reshape(basins * members, sizes.tiles, 1, cell_count)


def solution(mesh):
    return jax.shard_map(
        local,
        mesh=mesh,
        in_specs=(P("mem", "basin", "grp", "chain", None), P(("grp", "basin"), "chain", None)),
        out_specs=P("mem", ("grp", "basin"), "chain", None),
        check_vma=False,
    )
```

```python
import jax
import jax.numpy as jnp
from jax import lax
from jax.experimental import pallas as pl
from jax.experimental.pallas import tpu as pltpu
from jax.sharding import PartitionSpec as P

ROWS = 128
SUB = 8
HBM = pl.BlockSpec(memory_space=pltpu.HBM)
VMEM = pl.BlockSpec(memory_space=pltpu.VMEM)


def exchange_pairs(count, k):
    if count & (count - 1) == 0:
        return [(i, i ^ k) for i in range(count)]
    return [(i, (i + k) % count) for i in range(count)]


def reversed_pairs(pairs):
    return [(target, source) for source, target in pairs]


def target_of(k, count):
    me = lax.axis_index("basin")
    return me ^ k if count & (count - 1) == 0 else lax.rem(me + k, count)


def origin_of(k, count):
    me = lax.axis_index("basin")
    return me ^ k if count & (count - 1) == 0 else lax.rem(me + count - k, count)


def from_behind(value, axis):
    count = lax.axis_size(axis)
    return lax.ppermute(value, axis, [(i, i + 1) for i in range(count - 1)])


def fetched(codes, pairs):
    cores = lax.axis_size("mem")
    giver = cores - 1
    steps = [(a * cores + giver, b * cores + giver) for a, b in pairs]
    got = lax.ppermute(codes, ("basin", "mem"), steps)
    total = got
    for core in range(giver):
        total = total + lax.ppermute(got, "mem", [(giver, core)])
    return total


class Sizes:
    def __init__(self, members, tiles, columns, basins):
        self.members, self.tiles, self.columns, self.basins = members, tiles, columns, basins
        self.per_member = tiles * columns
        self.count = members * tiles
        self.rows = members * tiles * columns
        self.groups = self.count // SUB


def column_masks(d_ref, col, sizes):
    codes = d_ref[pl.ds(col, sizes.tiles, sizes.columns), :]
    codes = jnp.concatenate([codes] * (SUB // sizes.tiles), axis=0)
    lane = lax.broadcasted_iota(jnp.int32, codes.shape, 1)
    north = (codes == 1) & (lane > 0)
    south = (codes == 2) & (lane < ROWS - 1)
    return north, south


def advance(summed, north, south):
    zero = jnp.zeros_like(summed)
    up = pltpu.roll(jnp.where(north, summed, zero), ROWS - 1, 1)
    down = pltpu.roll(jnp.where(south, summed, zero), 1, 1)
    return jnp.where(north | south, zero, summed) + (up + down)


def sweep(x_ref, d_ref, carried, o_ref, sizes):
    for col in range(sizes.columns):
        north, south = column_masks(d_ref, col, sizes)
        for g in range(sizes.groups):
            rows = pl.ds(g * SUB * sizes.columns + col, SUB, sizes.columns)
            summed = x_ref[rows, :]
            if carried[g] is not None:
                summed = summed + carried[g]
            if o_ref is not None:
                o_ref[rows, :] = summed
            if o_ref is None or col < sizes.columns - 1:
                carried[g] = advance(summed, north, south)
    return carried


def registers(in_ref, i, sizes):
    if in_ref is None:
        return [None] * sizes.groups
    return [in_ref[i, pl.ds(g * SUB, SUB), :] for g in range(sizes.groups)]


def store_registers(o_ref, i, carried):
    for g, value in enumerate(carried):
        o_ref[i, pl.ds(g * SUB, SUB), :] = value


def gather_copies(x_ref, buf_ref, sem, block, sizes):
    size = sizes.per_member
    return [
        pltpu.make_async_copy(
            x_ref.at[m, pl.ds(block * size, size)], buf_ref.at[pl.ds(m * size, size)], sem.at[m]
        )
        for m in range(sizes.members)
    ]


def start_all(copies):
    for copy in copies:
        copy.start()


def wait_all(copies):
    for copy in copies:
        copy.wait()


def chunk_shape(sizes):
    return jax.ShapeDtypeStruct((sizes.rows, ROWS), jnp.float32)


def panel_shape(listed, sizes):
    return jax.ShapeDtypeStruct((listed, sizes.count, ROWS), jnp.float32)


def result_shape(sizes):
    return jax.ShapeDtypeStruct((sizes.basins * sizes.rows, ROWS), jnp.float32)


def params(sizes, chunks):
    return pltpu.CompilerParams(vmem_limit_bytes=(chunks * sizes.rows + 4096) * ROWS * 4)


def cost(chunks):
    return pl.CostEstimate(flops=chunks, bytes_accessed=chunks, transcendentals=0)


def pack(x, k, sizes):
    def body(x_ref, o_ref, sem):
        copies = gather_copies(x_ref, o_ref, sem, target_of(k, sizes.basins), sizes)
        start_all(copies)
        wait_all(copies)

    return pl.pallas_call(
        body,
        out_shape=chunk_shape(sizes),
        in_specs=[HBM],
        out_specs=VMEM,
        scratch_shapes=[pltpu.SemaphoreType.DMA((sizes.members,))],
        cost_estimate=cost(1),
        compiler_params=params(sizes, 2),
        name="pack",
    )(x)


def source_panels(x, ks, codes, inflow, sizes):
    listed = len(ks)

    def body(x_ref, *rest):
        d_refs, rest = rest[:listed], rest[listed:]
        in_ref = rest[0] if inflow is not None else None
        o_ref, buf, sem = rest[-3:]
        copies = [
            gather_copies(x_ref, buf.at[i], sem.at[i], target_of(k, sizes.basins), sizes)
            for i, k in enumerate(ks)
        ]
        for c in copies:
            start_all(c)
        for i in range(listed):
            wait_all(copies[i])
            store_registers(
                o_ref, i, sweep(buf.at[i], d_refs[i], registers(in_ref, i, sizes), None, sizes)
            )

    return pl.pallas_call(
        body,
        out_shape=panel_shape(listed, sizes),
        in_specs=[HBM] + [VMEM] * (listed + (inflow is not None)),
        out_specs=VMEM,
        scratch_shapes=[
            pltpu.VMEM((listed, sizes.rows, ROWS), jnp.float32),
            pltpu.SemaphoreType.DMA((listed, sizes.members)),
        ],
        cost_estimate=cost(listed),
        compiler_params=params(sizes, 2 * listed),
        name="source_panels",
    )(x, *codes, *([inflow] if inflow is not None else []))


def source_chunks(x, ks, codes, inflow, sizes):
    listed = len(ks)

    def body(x_ref, *rest):
        d_refs, in_ref, o_refs = rest[:listed], rest[listed], rest[listed + 1 : 2 * listed + 1]
        buf, sem = rest[-2:]
        copies = [
            gather_copies(x_ref, buf.at[i], sem.at[i], target_of(k, sizes.basins), sizes)
            for i, k in enumerate(ks)
        ]
        for c in copies:
            start_all(c)
        for i in range(listed):
            wait_all(copies[i])
            sweep(buf.at[i], d_refs[i], registers(in_ref, i, sizes), o_refs[i], sizes)

    return pl.pallas_call(
        body,
        out_shape=[chunk_shape(sizes)] * listed,
        in_specs=[HBM] + [VMEM] * (listed + 1),
        out_specs=[VMEM] * listed,
        scratch_shapes=[
            pltpu.VMEM((listed, sizes.rows, ROWS), jnp.float32),
            pltpu.SemaphoreType.DMA((listed, sizes.members)),
        ],
        compiler_params=params(sizes, 3 * listed),
        cost_estimate=cost(listed),
        name="source_chunks",
    )(x, *codes, inflow)


def arrived_panels(chunks, codes, inflow, sizes):
    listed = len(chunks)

    def body(*refs):
        x_refs, d_ref, o_ref = refs[:listed], refs[listed], refs[-1]
        in_ref = refs[listed + 1] if inflow is not None else None
        for i in range(listed):
            store_registers(
                o_ref, i, sweep(x_refs[i], d_ref, registers(in_ref, i, sizes), None, sizes)
            )

    return pl.pallas_call(
        body,
        out_shape=panel_shape(listed, sizes),
        in_specs=[VMEM] * (listed + 1 + (inflow is not None)),
        out_specs=VMEM,
        cost_estimate=cost(listed),
        compiler_params=params(sizes, 2 * listed),
        name="arrived_panels",
    )(*chunks, codes, *([inflow] if inflow is not None else []))


def arrived_result(chunks, ks, codes, inflow, sizes):
    listed = len(chunks)

    def body(*refs):
        x_refs, d_ref, in_ref = refs[:listed], refs[listed], refs[listed + 1]
        o_ref, out, sem = refs[-3:]
        copies = []
        for i, k in enumerate(ks):
            sweep(x_refs[i], d_ref, registers(in_ref, i, sizes), out.at[i], sizes)
            place = o_ref.at[pl.ds(origin_of(k, sizes.basins) * sizes.rows, sizes.rows)]
            copies.append(pltpu.make_async_copy(out.at[i], place, sem.at[i]))
            copies[i].start()
        wait_all(copies)

    return pl.pallas_call(
        body,
        out_shape=result_shape(sizes),
        in_specs=[VMEM] * (listed + 2),
        out_specs=HBM,
        scratch_shapes=[
            pltpu.VMEM((listed, sizes.rows, ROWS), jnp.float32),
            pltpu.SemaphoreType.DMA((listed,)),
        ],
        cost_estimate=cost(listed),
        compiler_params=params(sizes, 3 * listed),
        name="arrived_result",
    )(*chunks, codes, inflow)


def place_chunk(chunk, k, result, sizes):
    def body(x_ref, _, o_ref, sem):
        place = o_ref.at[pl.ds(origin_of(k, sizes.basins) * sizes.rows, sizes.rows)]
        copy = pltpu.make_async_copy(x_ref, place, sem)
        copy.start()
        copy.wait()

    return pl.pallas_call(
        body,
        out_shape=result_shape(sizes),
        in_specs=[VMEM, HBM],
        out_specs=HBM,
        scratch_shapes=[pltpu.SemaphoreType.DMA],
        input_output_aliases={1: 0},
        cost_estimate=cost(1),
        compiler_params=params(sizes, 2),
        name="place_chunk",
    )(chunk, result)


def local(runoff, directions):
    basins, chain = lax.axis_size("basin"), lax.axis_size("chain")
    _, members, all_tiles, _, cell_count = runoff.shape
    sizes = Sizes(members, directions.shape[0], cell_count // ROWS, basins)
    x = runoff.reshape(members, all_tiles * sizes.columns, ROWS)
    x = pltpu.with_memory_space_constraint(x, pltpu.HBM)
    codes = directions.reshape(sizes.per_member, ROWS)

    early = [basins - 1]
    late = [k for k in range(basins - 1, 0, -1) if k not in early]
    pairs = {k: exchange_pairs(basins, k) for k in range(basins)}

    packed = [pack(x, k, sizes) for k in early]
    packed, codes = lax.optimization_barrier((packed, codes))
    arrived = {k: lax.ppermute(value, "basin", pairs[k]) for k, value in zip(early, packed)}
    fetch = lambda value: [fetched(value, reversed_pairs(pairs[k])) for k in late]
    dirs = lax.cond(directions[0, 0, 0] < 3, fetch, lambda value: [value] * len(late), codes)

    inflow = None
    for _ in range(chain - 1):
        inflow = from_behind(source_panels(x, late, dirs, inflow, sizes), "chain")
    if inflow is None:
        inflow = jnp.zeros((len(late), sizes.count, ROWS), jnp.float32)
    chunks = source_chunks(x, late, dirs, inflow, sizes)
    for k, chunk in zip(late, chunks):
        arrived[k] = lax.ppermute(chunk, "basin", pairs[k])

    chunks = [pack(x, 0, sizes)] + [arrived[k] for k in early]
    inflow = None
    for _ in range(chain - 1):
        inflow = from_behind(arrived_panels(chunks, codes, inflow, sizes), "chain")
    if inflow is None:
        inflow = jnp.zeros((len(chunks), sizes.count, ROWS), jnp.float32)
    result = arrived_result(chunks, [0] + early, codes, inflow, sizes)
    for k in late:
        result = place_chunk(arrived[k], k, result, sizes)
    return result.reshape(basins * members, sizes.tiles, 1, cell_count)


def solution(mesh):
    return jax.shard_map(
        local,
        mesh=mesh,
        in_specs=(P("mem", "basin", "grp", "chain", None), P(("grp", "basin"), "chain", None)),
        out_specs=P("mem", ("grp", "basin"), "chain", None),
        check_vma=False,
    )
```

```python
import jax
import jax.numpy as jnp
from jax import lax
from jax.experimental import pallas as pl
from jax.experimental.pallas import tpu as pltpu
from jax.sharding import PartitionSpec as P

ROWS = 128
SUB = 8
HBM = pl.BlockSpec(memory_space=pltpu.HBM)
VMEM = pl.BlockSpec(memory_space=pltpu.VMEM)


def exchange_pairs(count, k):
    return [(i, i ^ k) for i in range(count)]


def partner(k):
    return lax.axis_index("basin") ^ k


def from_behind(value, axis):
    count = lax.axis_size(axis)
    return lax.ppermute(value, axis, [(i, i + 1) for i in range(count - 1)])


class Piece:
    def __init__(self, k, first, last, sizes):
        self.k, self.first, self.sizes = k, first, sizes
        self.members = last - first
        self.count = self.members * sizes.tiles
        self.rows = self.members * sizes.per_member
        self.groups = self.count // SUB

    def shape(self):
        return jax.ShapeDtypeStruct((self.rows, ROWS), jnp.float32)

    def panel(self):
        return jax.ShapeDtypeStruct((self.count, ROWS), jnp.float32)

    def gather(self, x_ref, buf_ref, sem):
        size = self.sizes.per_member
        block = partner(self.k)
        return [
            pltpu.make_async_copy(
                x_ref.at[self.first + m, pl.ds(block * size, size)],
                buf_ref.at[pl.ds(m * size, size)],
                sem.at[m],
            )
            for m in range(self.members)
        ]

    def place(self, o_ref):
        sizes = self.sizes
        start = (partner(self.k) * sizes.members + self.first) * sizes.per_member
        return o_ref.at[pl.ds(start, self.rows)]


class Sizes:
    def __init__(self, members, tiles, columns, basins):
        self.members, self.tiles, self.columns, self.basins = members, tiles, columns, basins
        self.per_member = tiles * columns

    def result(self):
        rows = self.basins * self.members * self.per_member
        return jax.ShapeDtypeStruct((rows, ROWS), jnp.float32)


def column_masks(d_ref, col, sizes):
    codes = d_ref[pl.ds(col, sizes.tiles, sizes.columns), :]
    codes = jnp.concatenate([codes] * (SUB // sizes.tiles), axis=0)
    lane = lax.broadcasted_iota(jnp.int32, codes.shape, 1)
    north = (codes == 1) & (lane > 0)
    south = (codes == 2) & (lane < ROWS - 1)
    return north, south


def advance(summed, north, south):
    zero = jnp.zeros_like(summed)
    up = pltpu.roll(jnp.where(north, summed, zero), ROWS - 1, 1)
    down = pltpu.roll(jnp.where(south, summed, zero), 1, 1)
    return jnp.where(north | south, zero, summed) + (up + down)


def sweep(x_ref, d_ref, carried, o_ref, sizes):
    for col in range(sizes.columns):
        north, south = column_masks(d_ref, col, sizes)
        for g in range(len(carried)):
            rows = pl.ds(g * SUB * sizes.columns + col, SUB, sizes.columns)
            summed = x_ref[rows, :]
            if carried[g] is not None:
                summed = summed + carried[g]
            if o_ref is not None:
                o_ref[rows, :] = summed
            if o_ref is None or col < sizes.columns - 1:
                carried[g] = advance(summed, north, south)
    return carried


def registers(in_ref, start, piece):
    if in_ref is None:
        return [None] * piece.groups
    return [in_ref[pl.ds(start + g * SUB, SUB), :] for g in range(piece.groups)]


def store_registers(o_ref, start, carried):
    for g, value in enumerate(carried):
        o_ref[pl.ds(start + g * SUB, SUB), :] = value


def start_all(copies):
    for copy in copies:
        copy.start()


def wait_all(copies):
    for copy in copies:
        copy.wait()


def params(rows):
    return pltpu.CompilerParams(vmem_limit_bytes=(rows + 4096) * ROWS * 4)


def cost(rows):
    return pl.CostEstimate(flops=rows * ROWS, bytes_accessed=rows * ROWS, transcendentals=0)


def pack(x, piece):
    def body(x_ref, o_ref, sem):
        copies = piece.gather(x_ref, o_ref, sem)
        start_all(copies)
        wait_all(copies)

    return pl.pallas_call(
        body,
        out_shape=piece.shape(),
        in_specs=[HBM],
        out_specs=VMEM,
        scratch_shapes=[pltpu.SemaphoreType.DMA((piece.members,))],
        compiler_params=params(piece.rows),
        cost_estimate=cost(piece.rows),
        name="pack",
    )(x)


def pack_with_codes(x, piece, codes):
    code_rows = codes.shape[0]

    def body(x_ref, d_ref, o_ref, buf, sem, code_sem):
        copies = piece.gather(x_ref, o_ref, sem)
        start_all(copies)
        copy = pltpu.make_async_copy(d_ref, buf, code_sem)
        copy.start()
        copy.wait()
        o_ref[pl.ds(piece.rows, code_rows), :] = buf[...].astype(jnp.float32)
        wait_all(copies)

    return pl.pallas_call(
        body,
        out_shape=jax.ShapeDtypeStruct((piece.rows + code_rows, ROWS), jnp.float32),
        in_specs=[HBM, HBM],
        out_specs=VMEM,
        scratch_shapes=[
            pltpu.VMEM(codes.shape, codes.dtype),
            pltpu.SemaphoreType.DMA((piece.members,)),
            pltpu.SemaphoreType.DMA,
        ],
        compiler_params=params(piece.rows),
        cost_estimate=cost(piece.rows),
        name="pack_with_codes",
    )(x, codes)


def source_panels(x, pieces, codes, inflow):
    listed, starts = len(pieces), panel_starts(pieces)
    rows = sum(piece.rows for piece in pieces)

    def body(x_ref, *refs):
        d_refs, in_ref = refs[:listed], refs[listed] if inflow is not None else None
        o_ref, bufs, sem = refs[-2 - listed], refs[-1 - listed : -1], refs[-1]
        copies = [piece.gather(x_ref, bufs[i], sem.at[i]) for i, piece in enumerate(pieces)]
        for c in copies:
            start_all(c)
        for i, piece in enumerate(pieces):
            wait_all(copies[i])
            size = piece.sizes.per_member
            codes_ref = d_refs[i].at[pl.ds(codes[i].shape[0] - size, size)]
            carried = registers(in_ref, starts[i], piece)
            store_registers(o_ref, starts[i], sweep(bufs[i], codes_ref, carried, None, piece.sizes))

    return pl.pallas_call(
        body,
        out_shape=jax.ShapeDtypeStruct((starts[-1], ROWS), jnp.float32),
        in_specs=[HBM] + [VMEM] * (listed + (inflow is not None)),
        out_specs=VMEM,
        scratch_shapes=[pltpu.VMEM((piece.rows, ROWS), jnp.float32) for piece in pieces]
        + [pltpu.SemaphoreType.DMA((listed, max(piece.members for piece in pieces)))],
        compiler_params=params(2 * rows),
        cost_estimate=cost(rows),
        name="source_panels",
    )(x, *codes, *([inflow] if inflow is not None else []))


def source_chunk(x, piece, codes, inflow):
    def body(x_ref, d_ref, in_ref, o_ref, buf, sem):
        copies = piece.gather(x_ref, buf, sem)
        start_all(copies)
        wait_all(copies)
        size = piece.sizes.per_member
        codes_ref = d_ref.at[pl.ds(codes.shape[0] - size, size)]
        sweep(buf, codes_ref, registers(in_ref, 0, piece), o_ref, piece.sizes)

    return pl.pallas_call(
        body,
        out_shape=piece.shape(),
        in_specs=[HBM, VMEM, VMEM],
        out_specs=VMEM,
        scratch_shapes=[
            pltpu.VMEM((piece.rows, ROWS), jnp.float32),
            pltpu.SemaphoreType.DMA((piece.members,)),
        ],
        compiler_params=params(3 * piece.rows),
        cost_estimate=cost(piece.rows),
        name="source_chunk",
    )(x, codes, inflow)


def panel_starts(pieces):
    starts = [0]
    for piece in pieces:
        starts.append(starts[-1] + piece.count)
    return starts


def arrived_panels(chunks, pieces, codes, inflow):
    listed, starts = len(pieces), panel_starts(pieces)
    rows = sum(piece.rows for piece in pieces)

    def body(*refs):
        x_refs, d_ref, o_ref = refs[:listed], refs[listed], refs[-1]
        in_ref = refs[listed + 1] if inflow is not None else None
        for x_ref, piece, start in zip(x_refs, pieces, starts):
            carried = registers(in_ref, start, piece)
            store_registers(o_ref, start, sweep(x_ref, d_ref, carried, None, piece.sizes))

    return pl.pallas_call(
        body,
        out_shape=jax.ShapeDtypeStruct((starts[-1], ROWS), jnp.float32),
        in_specs=[VMEM] * (listed + 1 + (inflow is not None)),
        out_specs=VMEM,
        compiler_params=params(2 * rows),
        cost_estimate=cost(rows),
        name="arrived_panels",
    )(*chunks, codes, *([inflow] if inflow is not None else []))


def arrived_result(chunks, pieces, codes, inflows, places, sizes):
    listed, given = len(pieces), len(inflows)
    rows = sum(piece.rows for piece in pieces)

    def body(*refs):
        x_refs, d_ref = refs[:listed], refs[listed]
        in_refs, o_ref = refs[listed + 1 : listed + 1 + given], refs[listed + 1 + given]
        outs, sem = refs[listed + 2 + given : -1], refs[-1]
        copies = []
        for i, piece in enumerate(pieces):
            which, start = places[i]
            sweep(x_refs[i], d_ref, registers(in_refs[which], start, piece), outs[i], sizes)
            copies.append(pltpu.make_async_copy(outs[i], piece.place(o_ref), sem.at[i]))
            copies[i].start()
        wait_all(copies)

    return pl.pallas_call(
        body,
        out_shape=sizes.result(),
        in_specs=[VMEM] * (listed + 1 + given),
        out_specs=HBM,
        scratch_shapes=[pltpu.VMEM((piece.rows, ROWS), jnp.float32) for piece in pieces]
        + [pltpu.SemaphoreType.DMA((listed,))],
        compiler_params=params(2 * rows),
        cost_estimate=cost(rows),
        name="arrived_result",
    )(*chunks, codes, *inflows)


def place_chunk(chunk, piece, result):
    def body(x_ref, _, o_ref, sem):
        copy = pltpu.make_async_copy(x_ref, piece.place(o_ref), sem)
        copy.start()
        copy.wait()

    return pl.pallas_call(
        body,
        out_shape=piece.sizes.result(),
        in_specs=[VMEM, HBM],
        out_specs=HBM,
        scratch_shapes=[pltpu.SemaphoreType.DMA],
        input_output_aliases={1: 0},
        compiler_params=params(piece.rows),
        cost_estimate=cost(piece.rows),
        name="place_chunk",
    )(chunk, result)


def local(runoff, directions):
    basins, chain = lax.axis_size("basin"), lax.axis_size("chain")
    _, members, all_tiles, _, cell_count = runoff.shape
    sizes = Sizes(members, directions.shape[0], cell_count // ROWS, basins)
    x = runoff.reshape(members, all_tiles * sizes.columns, ROWS)
    x = pltpu.with_memory_space_constraint(x, pltpu.HBM)
    codes = directions.reshape(sizes.per_member, ROWS)
    pairs = {k: exchange_pairs(basins, k) for k in range(basins)}

    far = basins - 1
    cut = max(SUB // sizes.tiles, members // 4)
    late = Piece(far, cut, members, sizes)
    early = [Piece(far, 0, cut, sizes)]
    early += [Piece(k, 0, members, sizes) for k in range(far - 1, 0, -1)]

    first = pack_with_codes(x, early[0], pltpu.with_memory_space_constraint(codes, pltpu.HBM))
    arrived = [lax.ppermute(first, "basin", pairs[far])]
    far_codes = arrived[0]
    arrived += [lax.ppermute(pack(x, piece), "basin", pairs[piece.k]) for piece in early[1:]]

    own = Piece(0, 0, members, sizes)
    source, source_codes, inflow = [late, own], [far_codes, codes], None
    for _ in range(chain - 1):
        inflow = from_behind(source_panels(x, source, source_codes, inflow), "chain")
    if inflow is None:
        inflow = jnp.zeros((panel_starts(source)[-1], ROWS), jnp.float32)
    finished = lax.ppermute(source_chunk(x, late, far_codes, inflow), "basin", pairs[far])

    late_inflow = None
    for _ in range(chain - 1):
        late_inflow = from_behind(arrived_panels(arrived, early, codes, late_inflow), "chain")
    if late_inflow is None:
        late_inflow = jnp.zeros((panel_starts(early)[-1], ROWS), jnp.float32)
    places = [(0, late.count)] + [(1, start) for start in panel_starts(early)[:-1]]
    result = arrived_result(
        [pack(x, own)] + arrived, [own] + early, codes, [inflow, late_inflow], places, sizes
    )
    result = place_chunk(finished, late, result)
    return result.reshape(basins * members, sizes.tiles, 1, cell_count)


def solution(mesh):
    return jax.shard_map(
        local,
        mesh=mesh,
        in_specs=(P("mem", "basin", "grp", "chain", None), P(("grp", "basin"), "chain", None)),
        out_specs=P("mem", ("grp", "basin"), "chain", None),
        check_vma=False,
    )
```

```python
import jax
import jax.numpy as jnp
from jax import lax
from jax.experimental import pallas as pl
from jax.experimental.pallas import tpu as pltpu
from jax.sharding import PartitionSpec as P

ROWS = 128
SUB = 8
HBM = pl.BlockSpec(memory_space=pltpu.HBM)
VMEM = pl.BlockSpec(memory_space=pltpu.VMEM)


def exchange_pairs(count, k):
    return [(i, i ^ k) for i in range(count)]


def partner(k):
    return lax.axis_index("basin") ^ k


def from_behind(value, axis):
    count = lax.axis_size(axis)
    return lax.ppermute(value, axis, [(i, (i + 1) % count) for i in range(count)])


class Piece:
    def __init__(self, k, first, last, sizes):
        self.k, self.first, self.sizes = k, first, sizes
        self.members = last - first
        self.count = self.members * sizes.tiles
        self.rows = self.members * sizes.per_member
        self.groups = self.count // SUB

    def shape(self):
        return jax.ShapeDtypeStruct((self.rows, ROWS), jnp.float32)

    def panel(self):
        return jax.ShapeDtypeStruct((self.count, ROWS), jnp.float32)

    def gather(self, x_ref, buf_ref, sem):
        size = self.sizes.per_member
        tiles = x_ref.at[pl.ds(self.first, self.members), pl.ds(partner(self.k) * size, size)]
        return [pltpu.make_async_copy(tiles, buf_ref.at[pl.ds(0, self.rows)].reshape(self.members, size, ROWS), sem)]

    def place(self, o_ref):
        sizes = self.sizes
        start = (partner(self.k) * sizes.members + self.first) * sizes.per_member
        return o_ref.at[pl.ds(start, self.rows)]


class Sizes:
    def __init__(self, members, tiles, columns, basins):
        self.members, self.tiles, self.columns, self.basins = members, tiles, columns, basins
        self.per_member = tiles * columns

    def result(self):
        rows = self.basins * self.members * self.per_member
        return jax.ShapeDtypeStruct((rows, ROWS), jnp.float32)


def column_masks(d_ref, col, sizes):
    codes = d_ref[pl.ds(col, sizes.tiles, sizes.columns), :]
    codes = jnp.concatenate([codes] * (SUB // sizes.tiles), axis=0)
    lane = lax.broadcasted_iota(jnp.int32, codes.shape, 1)
    north = (codes == 1) & (lane > 0)
    south = (codes == 2) & (lane < ROWS - 1)
    return north, south


def advance(summed, north, south):
    zero = jnp.zeros_like(summed)
    up = pltpu.roll(jnp.where(north, summed, zero), ROWS - 1, 1)
    down = pltpu.roll(jnp.where(south, summed, zero), 1, 1)
    return jnp.where(north | south, zero, summed) + (up + down)


def sweep(x_ref, d_ref, carried, o_ref, sizes):
    for col in range(sizes.columns):
        north, south = column_masks(d_ref, col, sizes)
        for g in range(len(carried)):
            rows = pl.ds(g * SUB * sizes.columns + col, SUB, sizes.columns)
            summed = x_ref[rows, :]
            if carried[g] is not None:
                summed = summed + carried[g]
            if o_ref is not None:
                o_ref[rows, :] = summed
            if o_ref is None or col < sizes.columns - 1:
                carried[g] = advance(summed, north, south)
    return carried


def registers(in_ref, start, piece):
    if in_ref is None:
        return [None] * piece.groups
    upstream = lax.axis_index("chain") > 0
    values = [in_ref[pl.ds(start + g * SUB, SUB), :] for g in range(piece.groups)]
    return [jnp.where(upstream, value, jnp.zeros_like(value)) for value in values]


def store_registers(o_ref, start, carried):
    for g, value in enumerate(carried):
        o_ref[pl.ds(start + g * SUB, SUB), :] = value


def start_all(copies):
    for copy in copies:
        copy.start()


def wait_all(copies):
    for copy in copies:
        copy.wait()


def params(rows):
    return pltpu.CompilerParams(vmem_limit_bytes=(rows + 4096) * ROWS * 4)


def cost(rows):
    return pl.CostEstimate(flops=rows * ROWS, bytes_accessed=rows * ROWS, transcendentals=0)


def pack(x, piece):
    def body(x_ref, o_ref, sem):
        copies = piece.gather(x_ref, o_ref, sem)
        start_all(copies)
        wait_all(copies)

    return pl.pallas_call(
        body,
        out_shape=piece.shape(),
        in_specs=[HBM],
        out_specs=VMEM,
        scratch_shapes=[pltpu.SemaphoreType.DMA],
        compiler_params=params(piece.rows),
        cost_estimate=cost(piece.rows),
        name="pack",
    )(x)


def pack_with_codes(x, piece, codes):
    code_rows = codes.shape[0]

    def body(x_ref, d_ref, o_ref, buf, sem, code_sem):
        copies = piece.gather(x_ref, o_ref, sem)
        start_all(copies)
        copy = pltpu.make_async_copy(d_ref, buf, code_sem)
        copy.start()
        copy.wait()
        o_ref[pl.ds(piece.rows, code_rows), :] = buf[...].astype(jnp.float32)
        wait_all(copies)

    return pl.pallas_call(
        body,
        out_shape=jax.ShapeDtypeStruct((piece.rows + code_rows, ROWS), jnp.float32),
        in_specs=[HBM, HBM],
        out_specs=VMEM,
        scratch_shapes=[
            pltpu.VMEM(codes.shape, codes.dtype),
            pltpu.SemaphoreType.DMA,
            pltpu.SemaphoreType.DMA,
        ],
        compiler_params=params(piece.rows),
        cost_estimate=cost(piece.rows),
        name="pack_with_codes",
    )(x, codes)


def source_panels(x, pieces, codes, inflow):
    listed, starts = len(pieces), panel_starts(pieces)
    rows = sum(piece.rows for piece in pieces)

    def body(x_ref, *refs):
        d_refs, in_ref = refs[:listed], refs[listed] if inflow is not None else None
        o_ref, bufs, sem = refs[-2 - listed], refs[-1 - listed : -1], refs[-1]
        copies = [piece.gather(x_ref, bufs[i], sem.at[i]) for i, piece in enumerate(pieces)]
        for c in copies:
            start_all(c)
        for i, piece in enumerate(pieces):
            wait_all(copies[i])
            size = piece.sizes.per_member
            codes_ref = d_refs[i].at[pl.ds(codes[i].shape[0] - size, size)]
            carried = registers(in_ref, starts[i], piece)
            store_registers(o_ref, starts[i], sweep(bufs[i], codes_ref, carried, None, piece.sizes))

    return pl.pallas_call(
        body,
        out_shape=jax.ShapeDtypeStruct((starts[-1], ROWS), jnp.float32),
        in_specs=[HBM] + [VMEM] * (listed + (inflow is not None)),
        out_specs=VMEM,
        scratch_shapes=[pltpu.VMEM((piece.rows, ROWS), jnp.float32) for piece in pieces]
        + [pltpu.SemaphoreType.DMA((listed,))],
        compiler_params=params(2 * rows),
        cost_estimate=cost(rows),
        name="source_panels",
    )(x, *codes, *([inflow] if inflow is not None else []))


def source_chunk(x, piece, codes, inflow):
    def body(x_ref, d_ref, in_ref, o_ref, buf, sem):
        copies = piece.gather(x_ref, buf, sem)
        start_all(copies)
        wait_all(copies)
        size = piece.sizes.per_member
        codes_ref = d_ref.at[pl.ds(codes.shape[0] - size, size)]
        sweep(buf, codes_ref, registers(in_ref, 0, piece), o_ref, piece.sizes)

    return pl.pallas_call(
        body,
        out_shape=piece.shape(),
        in_specs=[HBM, VMEM, VMEM],
        out_specs=VMEM,
        scratch_shapes=[
            pltpu.VMEM((piece.rows, ROWS), jnp.float32),
            pltpu.SemaphoreType.DMA,
        ],
        compiler_params=params(3 * piece.rows),
        cost_estimate=cost(piece.rows),
        name="source_chunk",
    )(x, codes, inflow)


def panel_starts(pieces):
    starts = [0]
    for piece in pieces:
        starts.append(starts[-1] + piece.count)
    return starts


def arrived_panels(chunks, pieces, codes, inflow):
    listed, starts = len(pieces), panel_starts(pieces)
    rows = sum(piece.rows for piece in pieces)

    def body(*refs):
        x_refs, d_ref, o_ref = refs[:listed], refs[listed], refs[-1]
        in_ref = refs[listed + 1] if inflow is not None else None
        for x_ref, piece, start in zip(x_refs, pieces, starts):
            carried = registers(in_ref, start, piece)
            store_registers(o_ref, start, sweep(x_ref, d_ref, carried, None, piece.sizes))

    return pl.pallas_call(
        body,
        out_shape=jax.ShapeDtypeStruct((starts[-1], ROWS), jnp.float32),
        in_specs=[VMEM] * (listed + 1 + (inflow is not None)),
        out_specs=VMEM,
        compiler_params=params(2 * rows),
        cost_estimate=cost(rows),
        name="arrived_panels",
    )(*chunks, codes, *([inflow] if inflow is not None else []))


def own_result(x, piece, codes, inflow, start):
    def body(x_ref, d_ref, in_ref, o_ref, buf, out, sem, out_sem):
        copies = piece.gather(x_ref, buf, sem)
        start_all(copies)
        wait_all(copies)
        sweep(buf, d_ref, registers(in_ref, start, piece), out, piece.sizes)
        copy = pltpu.make_async_copy(out, piece.place(o_ref), out_sem)
        copy.start()
        copy.wait()

    return pl.pallas_call(
        body,
        out_shape=piece.sizes.result(),
        in_specs=[HBM, VMEM, VMEM],
        out_specs=HBM,
        scratch_shapes=[pltpu.VMEM((piece.rows, ROWS), jnp.float32)] * 2
        + [pltpu.SemaphoreType.DMA] * 2,
        compiler_params=params(2 * piece.rows),
        cost_estimate=cost(piece.rows),
        name="own_result",
    )(x, codes, inflow)


def arrived_result(chunks, pieces, codes, inflow, result):
    listed, starts = len(pieces), panel_starts(pieces)
    rows = sum(piece.rows for piece in pieces)

    def body(*refs):
        x_refs, d_ref, in_ref, o_ref = refs[:listed], refs[listed], refs[listed + 1], refs[listed + 3]
        outs, sem = refs[listed + 4 : -1], refs[-1]
        copies = []
        for i, piece in enumerate(pieces):
            sweep(x_refs[i], d_ref, registers(in_ref, starts[i], piece), outs[i], piece.sizes)
            copies.append(pltpu.make_async_copy(outs[i], piece.place(o_ref), sem.at[i]))
            copies[i].start()
        wait_all(copies)

    return pl.pallas_call(
        body,
        out_shape=pieces[0].sizes.result(),
        in_specs=[VMEM] * (listed + 2) + [HBM],
        out_specs=HBM,
        scratch_shapes=[pltpu.VMEM((piece.rows, ROWS), jnp.float32) for piece in pieces]
        + [pltpu.SemaphoreType.DMA((listed,))],
        input_output_aliases={listed + 2: 0},
        compiler_params=params(2 * rows),
        cost_estimate=cost(rows),
        name="arrived_result",
    )(*chunks, codes, inflow, result)


def place_chunk(chunk, piece, result):
    def body(x_ref, _, o_ref, sem):
        copy = pltpu.make_async_copy(x_ref, piece.place(o_ref), sem)
        copy.start()
        copy.wait()

    return pl.pallas_call(
        body,
        out_shape=piece.sizes.result(),
        in_specs=[VMEM, HBM],
        out_specs=HBM,
        scratch_shapes=[pltpu.SemaphoreType.DMA],
        input_output_aliases={1: 0},
        compiler_params=params(piece.rows),
        cost_estimate=cost(piece.rows),
        name="place_chunk",
    )(chunk, result)


def local(runoff, directions):
    basins, chain = lax.axis_size("basin"), lax.axis_size("chain")
    _, members, all_tiles, _, cell_count = runoff.shape
    sizes = Sizes(members, directions.shape[0], cell_count // ROWS, basins)
    x = runoff.reshape(members, all_tiles * sizes.columns, ROWS)
    x = pltpu.with_memory_space_constraint(x, pltpu.HBM)
    codes = directions.reshape(sizes.per_member, ROWS)
    pairs = {k: exchange_pairs(basins, k) for k in range(basins)}

    far = basins - 1
    cut = max(SUB // sizes.tiles, members // 4)
    late = Piece(far, cut, members, sizes)
    early = [Piece(far, 0, cut, sizes)]
    early += [Piece(k, 0, members, sizes) for k in range(far - 1, 0, -1)]

    first = pack_with_codes(x, early[0], pltpu.with_memory_space_constraint(codes, pltpu.HBM))
    arrived = [lax.ppermute(first, "basin", pairs[far])]
    far_codes = arrived[0]
    arrived += [lax.ppermute(pack(x, piece), "basin", pairs[piece.k]) for piece in early[1:]]

    own = Piece(0, 0, members, sizes)
    source, source_codes, inflow = [late, own], [far_codes, codes], None
    for _ in range(chain - 1):
        inflow = from_behind(source_panels(x, source, source_codes, inflow), "chain")
    if inflow is None:
        inflow = jnp.zeros((panel_starts(source)[-1], ROWS), jnp.float32)
    finished = lax.ppermute(source_chunk(x, late, far_codes, inflow), "basin", pairs[far])

    result = own_result(x, own, codes, inflow, late.count)
    result, arrived = lax.optimization_barrier((result, arrived))
    late_inflow = None
    for _ in range(chain - 1):
        late_inflow = from_behind(arrived_panels(arrived, early, codes, late_inflow), "chain")
    if late_inflow is None:
        late_inflow = jnp.zeros((panel_starts(early)[-1], ROWS), jnp.float32)
    result = arrived_result(arrived, early, codes, late_inflow, result)
    result = place_chunk(finished, late, result)
    return result.reshape(basins * members, sizes.tiles, 1, cell_count)


def solution(mesh):
    return jax.shard_map(
        local,
        mesh=mesh,
        in_specs=(P("mem", "basin", "grp", "chain", None), P(("grp", "basin"), "chain", None)),
        out_specs=P("mem", ("grp", "basin"), "chain", None),
        check_vma=False,
    )
```

```python
import jax
import jax.numpy as jnp
from jax import lax
from jax.experimental import pallas as pl
from jax.experimental.pallas import tpu as pltpu
from jax.sharding import PartitionSpec as P

ROWS = 128
SUB = 8
HBM = pl.BlockSpec(memory_space=pltpu.HBM)
VMEM = pl.BlockSpec(memory_space=pltpu.VMEM)


def exchange_pairs(count, k):
    return [(i, i ^ k) for i in range(count)]


def partner(k):
    return lax.axis_index("basin") ^ k


def from_behind(value, axis):
    count = lax.axis_size(axis)
    return lax.ppermute(value, axis, [(i, (i + 1) % count) for i in range(count)])


class Piece:
    def __init__(self, k, first, last, sizes):
        self.k, self.first, self.sizes = k, first, sizes
        self.members = last - first
        self.count = self.members * sizes.tiles
        self.rows = self.members * sizes.per_member
        self.groups = self.count // SUB

    def shape(self):
        return jax.ShapeDtypeStruct((self.rows, ROWS), jnp.float32)

    def panel(self):
        return jax.ShapeDtypeStruct((self.count, ROWS), jnp.float32)

    def gather(self, x_ref, buf_ref, sem):
        size = self.sizes.per_member
        tiles = x_ref.at[pl.ds(self.first, self.members), pl.ds(partner(self.k) * size, size)]
        return [pltpu.make_async_copy(tiles, buf_ref.at[pl.ds(0, self.rows)].reshape(self.members, size, ROWS), sem)]

    def place(self, o_ref):
        sizes = self.sizes
        start = (partner(self.k) * sizes.members + self.first) * sizes.per_member
        return o_ref.at[pl.ds(start, self.rows)]


class Sizes:
    def __init__(self, members, tiles, columns, basins):
        self.members, self.tiles, self.columns, self.basins = members, tiles, columns, basins
        self.per_member = tiles * columns

    def result(self):
        rows = self.basins * self.members * self.per_member
        return jax.ShapeDtypeStruct((rows, ROWS), jnp.float32)


def column_masks(d_ref, col, sizes):
    codes = d_ref[pl.ds(col, sizes.tiles, sizes.columns), :]
    codes = jnp.concatenate([codes] * (SUB // sizes.tiles), axis=0)
    lane = lax.broadcasted_iota(jnp.int32, codes.shape, 1)
    north = (codes == 1) & (lane > 0)
    south = (codes == 2) & (lane < ROWS - 1)
    return north, south


def advance(summed, north, south):
    zero = jnp.zeros_like(summed)
    up = pltpu.roll(jnp.where(north, summed, zero), ROWS - 1, 1)
    down = pltpu.roll(jnp.where(south, summed, zero), 1, 1)
    return jnp.where(north | south, zero, summed) + (up + down)


def sweep(x_ref, d_ref, carried, o_ref, sizes):
    for col in range(sizes.columns):
        north, south = column_masks(d_ref, col, sizes)
        for g in range(len(carried)):
            rows = pl.ds(g * SUB * sizes.columns + col, SUB, sizes.columns)
            summed = x_ref[rows, :]
            if carried[g] is not None:
                summed = summed + carried[g]
            if o_ref is not None:
                o_ref[rows, :] = summed
            if o_ref is None or col < sizes.columns - 1:
                carried[g] = advance(summed, north, south)
    return carried


def registers(in_ref, start, piece):
    if in_ref is None:
        return [None] * piece.groups
    upstream = lax.axis_index("chain") > 0
    values = [in_ref[pl.ds(start + g * SUB, SUB), :] for g in range(piece.groups)]
    return [jnp.where(upstream, value, jnp.zeros_like(value)) for value in values]


def store_registers(o_ref, start, carried):
    for g, value in enumerate(carried):
        o_ref[pl.ds(start + g * SUB, SUB), :] = value


def start_all(copies):
    for copy in copies:
        copy.start()


def wait_all(copies):
    for copy in copies:
        copy.wait()


def params(rows):
    return pltpu.CompilerParams(vmem_limit_bytes=(rows + 4096) * ROWS * 4)


def cost(rows):
    return pl.CostEstimate(flops=rows * ROWS, bytes_accessed=rows * ROWS, transcendentals=0)


def pack(x, piece):
    def body(x_ref, o_ref, sem):
        copies = piece.gather(x_ref, o_ref, sem)
        start_all(copies)
        wait_all(copies)

    return pl.pallas_call(
        body,
        out_shape=piece.shape(),
        in_specs=[HBM],
        out_specs=VMEM,
        scratch_shapes=[pltpu.SemaphoreType.DMA],
        compiler_params=params(piece.rows),
        cost_estimate=cost(piece.rows),
        name="pack",
    )(x)


def pack_with_codes(x, piece, codes):
    code_rows = codes.shape[0]

    def body(x_ref, d_ref, o_ref, buf, sem, code_sem):
        copies = piece.gather(x_ref, o_ref, sem)
        start_all(copies)
        copy = pltpu.make_async_copy(d_ref, buf, code_sem)
        copy.start()
        copy.wait()
        o_ref[pl.ds(piece.rows, code_rows), :] = buf[...].astype(jnp.float32)
        wait_all(copies)

    return pl.pallas_call(
        body,
        out_shape=jax.ShapeDtypeStruct((piece.rows + code_rows, ROWS), jnp.float32),
        in_specs=[HBM, HBM],
        out_specs=VMEM,
        scratch_shapes=[
            pltpu.VMEM(codes.shape, codes.dtype),
            pltpu.SemaphoreType.DMA,
            pltpu.SemaphoreType.DMA,
        ],
        compiler_params=params(piece.rows),
        cost_estimate=cost(piece.rows),
        name="pack_with_codes",
    )(x, codes)


def source_panels(x, pieces, codes, inflow):
    listed, starts = len(pieces), panel_starts(pieces)
    rows = sum(piece.rows for piece in pieces)

    def body(x_ref, *refs):
        d_refs, in_ref = refs[:listed], refs[listed] if inflow is not None else None
        o_ref, bufs, sem = refs[-2 - listed], refs[-1 - listed : -1], refs[-1]
        copies = [piece.gather(x_ref, bufs[i], sem.at[i]) for i, piece in enumerate(pieces)]
        for c in copies:
            start_all(c)
        for i, piece in enumerate(pieces):
            wait_all(copies[i])
            size = piece.sizes.per_member
            codes_ref = d_refs[i].at[pl.ds(codes[i].shape[0] - size, size)]
            carried = registers(in_ref, starts[i], piece)
            store_registers(o_ref, starts[i], sweep(bufs[i], codes_ref, carried, None, piece.sizes))

    return pl.pallas_call(
        body,
        out_shape=jax.ShapeDtypeStruct((starts[-1], ROWS), jnp.float32),
        in_specs=[HBM] + [VMEM] * (listed + (inflow is not None)),
        out_specs=VMEM,
        scratch_shapes=[pltpu.VMEM((piece.rows, ROWS), jnp.float32) for piece in pieces]
        + [pltpu.SemaphoreType.DMA((listed,))],
        compiler_params=params(2 * rows),
        cost_estimate=cost(rows),
        name="source_panels",
    )(x, *codes, *([inflow] if inflow is not None else []))


def source_chunk(x, piece, codes, inflow):
    def body(x_ref, d_ref, in_ref, o_ref, buf, sem):
        copies = piece.gather(x_ref, buf, sem)
        start_all(copies)
        wait_all(copies)
        size = piece.sizes.per_member
        codes_ref = d_ref.at[pl.ds(codes.shape[0] - size, size)]
        sweep(buf, codes_ref, registers(in_ref, 0, piece), o_ref, piece.sizes)

    return pl.pallas_call(
        body,
        out_shape=piece.shape(),
        in_specs=[HBM, VMEM, VMEM],
        out_specs=VMEM,
        scratch_shapes=[
            pltpu.VMEM((piece.rows, ROWS), jnp.float32),
            pltpu.SemaphoreType.DMA,
        ],
        compiler_params=params(3 * piece.rows),
        cost_estimate=cost(piece.rows),
        name="source_chunk",
    )(x, codes, inflow)


def panel_starts(pieces):
    starts = [0]
    for piece in pieces:
        starts.append(starts[-1] + piece.count)
    return starts


def arrived_panels(chunks, pieces, codes, inflow):
    listed, starts = len(pieces), panel_starts(pieces)
    rows = sum(piece.rows for piece in pieces)

    def body(*refs):
        x_refs, d_ref, o_ref = refs[:listed], refs[listed], refs[-1]
        in_ref = refs[listed + 1] if inflow is not None else None
        for x_ref, piece, start in zip(x_refs, pieces, starts):
            carried = registers(in_ref, start, piece)
            store_registers(o_ref, start, sweep(x_ref, d_ref, carried, None, piece.sizes))

    return pl.pallas_call(
        body,
        out_shape=jax.ShapeDtypeStruct((starts[-1], ROWS), jnp.float32),
        in_specs=[VMEM] * (listed + 1 + (inflow is not None)),
        out_specs=VMEM,
        compiler_params=params(2 * rows),
        cost_estimate=cost(rows),
        name="arrived_panels",
    )(*chunks, codes, *([inflow] if inflow is not None else []))


def own_result(x, piece, codes, inflow, start):
    def body(x_ref, d_ref, in_ref, o_ref, buf, out, sem, out_sem):
        copies = piece.gather(x_ref, buf, sem)
        start_all(copies)
        wait_all(copies)
        sweep(buf, d_ref, registers(in_ref, start, piece), out, piece.sizes)
        copy = pltpu.make_async_copy(out, piece.place(o_ref), out_sem)
        copy.start()
        copy.wait()

    return pl.pallas_call(
        body,
        out_shape=piece.sizes.result(),
        in_specs=[HBM, VMEM, VMEM],
        out_specs=HBM,
        scratch_shapes=[pltpu.VMEM((piece.rows, ROWS), jnp.float32)] * 2
        + [pltpu.SemaphoreType.DMA] * 2,
        compiler_params=params(2 * piece.rows),
        cost_estimate=cost(piece.rows),
        name="own_result",
    )(x, codes, inflow)


def arrived_result(chunks, pieces, codes, inflow, result):
    listed, starts = len(pieces), panel_starts(pieces)
    rows = sum(piece.rows for piece in pieces)

    def body(*refs):
        x_refs, d_ref, in_ref, o_ref = refs[:listed], refs[listed], refs[listed + 1], refs[listed + 3]
        outs, sem = refs[listed + 4 : -1], refs[-1]
        copies = []
        for i, piece in enumerate(pieces):
            sweep(x_refs[i], d_ref, registers(in_ref, starts[i], piece), outs[i], piece.sizes)
            copies.append(pltpu.make_async_copy(outs[i], piece.place(o_ref), sem.at[i]))
            copies[i].start()
        wait_all(copies)

    return pl.pallas_call(
        body,
        out_shape=pieces[0].sizes.result(),
        in_specs=[VMEM] * (listed + 2) + [HBM],
        out_specs=HBM,
        scratch_shapes=[pltpu.VMEM((piece.rows, ROWS), jnp.float32) for piece in pieces]
        + [pltpu.SemaphoreType.DMA((listed,))],
        input_output_aliases={listed + 2: 0},
        compiler_params=params(2 * rows),
        cost_estimate=cost(rows),
        name="arrived_result",
    )(*chunks, codes, inflow, result)


def place_chunk(chunk, piece, result):
    def body(x_ref, _, o_ref, sem):
        copy = pltpu.make_async_copy(x_ref, piece.place(o_ref), sem)
        copy.start()
        copy.wait()

    return pl.pallas_call(
        body,
        out_shape=piece.sizes.result(),
        in_specs=[VMEM, HBM],
        out_specs=HBM,
        scratch_shapes=[pltpu.SemaphoreType.DMA],
        input_output_aliases={1: 0},
        compiler_params=params(piece.rows),
        cost_estimate=cost(piece.rows),
        name="place_chunk",
    )(chunk, result)


def local(runoff, directions):
    basins, chain = lax.axis_size("basin"), lax.axis_size("chain")
    _, members, all_tiles, _, cell_count = runoff.shape
    sizes = Sizes(members, directions.shape[0], cell_count // ROWS, basins)
    x = runoff.reshape(members, all_tiles * sizes.columns, ROWS)
    x = pltpu.with_memory_space_constraint(x, pltpu.HBM)
    codes = directions.reshape(sizes.per_member, ROWS)
    pairs = {k: exchange_pairs(basins, k) for k in range(basins)}

    far = basins - 1
    cut = SUB // sizes.tiles
    late = Piece(far, cut, members, sizes)
    head = Piece(far, 0, cut, sizes)
    near = [Piece(k, 0, members, sizes) for k in range(1, basins // 2)]
    across = [Piece(k, 0, members, sizes) for k in range(basins // 2, far)]

    first = pack_with_codes(x, head, pltpu.with_memory_space_constraint(codes, pltpu.HBM))
    far_codes = lax.ppermute(first, "basin", pairs[far])
    arrived = {head: far_codes}
    for piece in across + near:
        arrived[piece] = lax.ppermute(pack(x, piece), "basin", pairs[piece.k])

    own = Piece(0, 0, members, sizes)
    source, source_codes, inflow = [late, own], [far_codes, codes], None
    for _ in range(chain - 1):
        inflow = from_behind(source_panels(x, source, source_codes, inflow), "chain")
    if inflow is None:
        inflow = jnp.zeros((panel_starts(source)[-1], ROWS), jnp.float32)
    finished = lax.ppermute(source_chunk(x, late, far_codes, inflow), "basin", pairs[far])

    result = own_result(x, own, codes, inflow, late.count)
    for group in ([head] + near, across):
        chunks = [arrived[piece] for piece in group]
        result, chunks = lax.optimization_barrier((result, chunks))
        inflow = None
        for _ in range(chain - 1):
            inflow = from_behind(arrived_panels(chunks, group, codes, inflow), "chain")
        if inflow is None:
            inflow = jnp.zeros((panel_starts(group)[-1], ROWS), jnp.float32)
        result = arrived_result(chunks, group, codes, inflow, result)
    result = place_chunk(finished, late, result)
    return result.reshape(basins * members, sizes.tiles, 1, cell_count)


def solution(mesh):
    return jax.shard_map(
        local,
        mesh=mesh,
        in_specs=(P("mem", "basin", "grp", "chain", None), P(("grp", "basin"), "chain", None)),
        out_specs=P("mem", ("grp", "basin"), "chain", None),
        check_vma=False,
    )
```

```python
import jax
import jax.numpy as jnp
from jax import lax
from jax.experimental import pallas as pl
from jax.experimental.pallas import tpu as pltpu
from jax.sharding import PartitionSpec as P

ROWS = 128
SUB = 8
HBM = pl.BlockSpec(memory_space=pltpu.HBM)
VMEM = pl.BlockSpec(memory_space=pltpu.VMEM)


def exchange_pairs(count, k):
    return [(i, i ^ k) for i in range(count)]


def partner(k):
    return lax.axis_index("basin") ^ k


def from_behind(value, axis):
    count = lax.axis_size(axis)
    return lax.ppermute(value, axis, [(i, (i + 1) % count) for i in range(count)])


class Piece:
    def __init__(self, k, first, last, sizes):
        self.k, self.first, self.sizes = k, first, sizes
        self.members = last - first
        self.count = self.members * sizes.tiles
        self.rows = self.members * sizes.per_member
        self.groups = self.count // SUB

    def shape(self):
        return jax.ShapeDtypeStruct((self.rows, ROWS), jnp.float32)

    def panel(self):
        return jax.ShapeDtypeStruct((self.count, ROWS), jnp.float32)

    def gather(self, x_ref, buf_ref, sem):
        size = self.sizes.per_member
        tiles = x_ref.at[pl.ds(self.first, self.members), pl.ds(partner(self.k) * size, size)]
        return [pltpu.make_async_copy(tiles, buf_ref.at[pl.ds(0, self.rows)].reshape(self.members, size, ROWS), sem)]

    def place(self, o_ref):
        sizes = self.sizes
        start = (partner(self.k) * sizes.members + self.first) * sizes.per_member
        return o_ref.at[pl.ds(start, self.rows)]


class Sizes:
    def __init__(self, members, tiles, columns, basins):
        self.members, self.tiles, self.columns, self.basins = members, tiles, columns, basins
        self.per_member = tiles * columns

    def result(self):
        rows = self.basins * self.members * self.per_member
        return jax.ShapeDtypeStruct((rows, ROWS), jnp.float32)


def column_masks(d_ref, col, sizes):
    codes = d_ref[pl.ds(col, sizes.tiles, sizes.columns), :]
    codes = jnp.concatenate([codes] * (SUB // sizes.tiles), axis=0)
    lane = lax.broadcasted_iota(jnp.int32, codes.shape, 1)
    north = (codes == 1) & (lane > 0)
    south = (codes == 2) & (lane < ROWS - 1)
    return north, south


def advance(summed, north, south):
    zero = jnp.zeros_like(summed)
    up = pltpu.roll(jnp.where(north, summed, zero), ROWS - 1, 1)
    down = pltpu.roll(jnp.where(south, summed, zero), 1, 1)
    return jnp.where(north | south, zero, summed) + (up + down)


def sweep(x_ref, d_ref, carried, o_ref, sizes):
    for col in range(sizes.columns):
        north, south = column_masks(d_ref, col, sizes)
        for g in range(len(carried)):
            rows = pl.ds(g * SUB * sizes.columns + col, SUB, sizes.columns)
            summed = x_ref[rows, :]
            if carried[g] is not None:
                summed = summed + carried[g]
            if o_ref is not None:
                o_ref[rows, :] = summed
            if o_ref is None or col < sizes.columns - 1:
                carried[g] = advance(summed, north, south)
    return carried


def registers(in_ref, start, piece):
    if in_ref is None:
        return [None] * piece.groups
    upstream = lax.axis_index("chain") > 0
    values = [in_ref[pl.ds(start + g * SUB, SUB), :] for g in range(piece.groups)]
    return [jnp.where(upstream, value, jnp.zeros_like(value)) for value in values]


def store_registers(o_ref, start, carried):
    for g, value in enumerate(carried):
        o_ref[pl.ds(start + g * SUB, SUB), :] = value


def start_all(copies):
    for copy in copies:
        copy.start()


def wait_all(copies):
    for copy in copies:
        copy.wait()


def params(rows):
    return pltpu.CompilerParams(vmem_limit_bytes=(rows + 4096) * ROWS * 4)


def cost(rows):
    return pl.CostEstimate(flops=rows * ROWS, bytes_accessed=rows * ROWS, transcendentals=0)


def pack(x, pieces):
    rows = sum(piece.rows for piece in pieces)

    def body(x_ref, *refs):
        o_refs, sem = refs[:-1], refs[-1]
        copies = [piece.gather(x_ref, o_refs[i], sem.at[i]) for i, piece in enumerate(pieces)]
        for c in copies:
            start_all(c)
        for c in copies:
            wait_all(c)

    return pl.pallas_call(
        body,
        out_shape=[piece.shape() for piece in pieces],
        in_specs=[HBM],
        out_specs=[VMEM] * len(pieces),
        scratch_shapes=[pltpu.SemaphoreType.DMA((len(pieces),))],
        compiler_params=params(rows),
        cost_estimate=cost(rows),
        name="pack",
    )(x)


def pack_with_codes(x, piece, codes):
    code_rows = codes.shape[0]

    def body(x_ref, d_ref, o_ref, buf, sem, code_sem):
        copies = piece.gather(x_ref, o_ref, sem)
        start_all(copies)
        copy = pltpu.make_async_copy(d_ref, buf, code_sem)
        copy.start()
        copy.wait()
        o_ref[pl.ds(piece.rows, code_rows), :] = buf[...].astype(jnp.float32)
        wait_all(copies)

    return pl.pallas_call(
        body,
        out_shape=jax.ShapeDtypeStruct((piece.rows + code_rows, ROWS), jnp.float32),
        in_specs=[HBM, HBM],
        out_specs=VMEM,
        scratch_shapes=[
            pltpu.VMEM(codes.shape, codes.dtype),
            pltpu.SemaphoreType.DMA,
            pltpu.SemaphoreType.DMA,
        ],
        compiler_params=params(piece.rows),
        cost_estimate=cost(piece.rows),
        name="pack_with_codes",
    )(x, codes)


def source_panels(x, pieces, codes, inflow):
    listed, starts = len(pieces), panel_starts(pieces)
    rows = sum(piece.rows for piece in pieces)

    def body(x_ref, *refs):
        d_refs, in_ref = refs[:listed], refs[listed] if inflow is not None else None
        o_ref, bufs, sem = refs[-2 - listed], refs[-1 - listed : -1], refs[-1]
        copies = [piece.gather(x_ref, bufs[i], sem.at[i]) for i, piece in enumerate(pieces)]
        for c in copies:
            start_all(c)
        for i, piece in enumerate(pieces):
            wait_all(copies[i])
            size = piece.sizes.per_member
            codes_ref = d_refs[i].at[pl.ds(codes[i].shape[0] - size, size)]
            carried = registers(in_ref, starts[i], piece)
            store_registers(o_ref, starts[i], sweep(bufs[i], codes_ref, carried, None, piece.sizes))

    return pl.pallas_call(
        body,
        out_shape=jax.ShapeDtypeStruct((starts[-1], ROWS), jnp.float32),
        in_specs=[HBM] + [VMEM] * (listed + (inflow is not None)),
        out_specs=VMEM,
        scratch_shapes=[pltpu.VMEM((piece.rows, ROWS), jnp.float32) for piece in pieces]
        + [pltpu.SemaphoreType.DMA((listed,))],
        compiler_params=params(2 * rows),
        cost_estimate=cost(rows),
        name="source_panels",
    )(x, *codes, *([inflow] if inflow is not None else []))


def source_chunk(x, piece, codes, inflow):
    def body(x_ref, d_ref, in_ref, o_ref, buf, sem):
        copies = piece.gather(x_ref, buf, sem)
        start_all(copies)
        wait_all(copies)
        size = piece.sizes.per_member
        codes_ref = d_ref.at[pl.ds(codes.shape[0] - size, size)]
        sweep(buf, codes_ref, registers(in_ref, 0, piece), o_ref, piece.sizes)

    return pl.pallas_call(
        body,
        out_shape=piece.shape(),
        in_specs=[HBM, VMEM, VMEM],
        out_specs=VMEM,
        scratch_shapes=[
            pltpu.VMEM((piece.rows, ROWS), jnp.float32),
            pltpu.SemaphoreType.DMA,
        ],
        compiler_params=params(3 * piece.rows),
        cost_estimate=cost(piece.rows),
        name="source_chunk",
    )(x, codes, inflow)


def panel_starts(pieces):
    starts = [0]
    for piece in pieces:
        starts.append(starts[-1] + piece.count)
    return starts


def arrived_panels(chunks, pieces, codes, inflow):
    listed, starts = len(pieces), panel_starts(pieces)
    rows = sum(piece.rows for piece in pieces)

    def body(*refs):
        x_refs, d_ref, o_ref = refs[:listed], refs[listed], refs[-1]
        in_ref = refs[listed + 1] if inflow is not None else None
        for x_ref, piece, start in zip(x_refs, pieces, starts):
            carried = registers(in_ref, start, piece)
            store_registers(o_ref, start, sweep(x_ref, d_ref, carried, None, piece.sizes))

    return pl.pallas_call(
        body,
        out_shape=jax.ShapeDtypeStruct((starts[-1], ROWS), jnp.float32),
        in_specs=[VMEM] * (listed + 1 + (inflow is not None)),
        out_specs=VMEM,
        compiler_params=params(2 * rows),
        cost_estimate=cost(rows),
        name="arrived_panels",
    )(*chunks, codes, *([inflow] if inflow is not None else []))


def own_result(x, piece, codes, inflow, start):
    def body(x_ref, d_ref, in_ref, o_ref, buf, out, sem, out_sem):
        copies = piece.gather(x_ref, buf, sem)
        start_all(copies)
        wait_all(copies)
        sweep(buf, d_ref, registers(in_ref, start, piece), out, piece.sizes)
        copy = pltpu.make_async_copy(out, piece.place(o_ref), out_sem)
        copy.start()
        copy.wait()

    return pl.pallas_call(
        body,
        out_shape=piece.sizes.result(),
        in_specs=[HBM, VMEM, VMEM],
        out_specs=HBM,
        scratch_shapes=[pltpu.VMEM((piece.rows, ROWS), jnp.float32)] * 2
        + [pltpu.SemaphoreType.DMA] * 2,
        compiler_params=params(2 * piece.rows),
        cost_estimate=cost(piece.rows),
        name="own_result",
    )(x, codes, inflow)


def arrived_result(chunks, pieces, codes, inflow, result):
    listed, starts = len(pieces), panel_starts(pieces)
    rows = sum(piece.rows for piece in pieces)

    def body(*refs):
        x_refs, d_ref, in_ref, o_ref = refs[:listed], refs[listed], refs[listed + 1], refs[listed + 3]
        outs, sem = refs[listed + 4 : -1], refs[-1]
        copies = []
        for i, piece in enumerate(pieces):
            sweep(x_refs[i], d_ref, registers(in_ref, starts[i], piece), outs[i], piece.sizes)
            copies.append(pltpu.make_async_copy(outs[i], piece.place(o_ref), sem.at[i]))
            copies[i].start()
        wait_all(copies)

    return pl.pallas_call(
        body,
        out_shape=pieces[0].sizes.result(),
        in_specs=[VMEM] * (listed + 2) + [HBM],
        out_specs=HBM,
        scratch_shapes=[pltpu.VMEM((piece.rows, ROWS), jnp.float32) for piece in pieces]
        + [pltpu.SemaphoreType.DMA((listed,))],
        input_output_aliases={listed + 2: 0},
        compiler_params=params(2 * rows),
        cost_estimate=cost(rows),
        name="arrived_result",
    )(*chunks, codes, inflow, result)


def place_chunk(chunk, piece, result):
    def body(x_ref, _, o_ref, sem):
        copy = pltpu.make_async_copy(x_ref, piece.place(o_ref), sem)
        copy.start()
        copy.wait()

    return pl.pallas_call(
        body,
        out_shape=piece.sizes.result(),
        in_specs=[VMEM, HBM],
        out_specs=HBM,
        scratch_shapes=[pltpu.SemaphoreType.DMA],
        input_output_aliases={1: 0},
        compiler_params=params(piece.rows),
        cost_estimate=cost(piece.rows),
        name="place_chunk",
    )(chunk, result)


def local(runoff, directions):
    basins, chain = lax.axis_size("basin"), lax.axis_size("chain")
    _, members, all_tiles, _, cell_count = runoff.shape
    sizes = Sizes(members, directions.shape[0], cell_count // ROWS, basins)
    x = runoff.reshape(members, all_tiles * sizes.columns, ROWS)
    x = pltpu.with_memory_space_constraint(x, pltpu.HBM)
    codes = directions.reshape(sizes.per_member, ROWS)
    pairs = {k: exchange_pairs(basins, k) for k in range(basins)}

    far = basins - 1
    cut = max(SUB // sizes.tiles, members // 4)
    late = Piece(far, cut, members, sizes)
    head = Piece(far, 0, cut, sizes)
    part = max(SUB // sizes.tiles, members // 4)
    near = [
        Piece(k, start, start + part, sizes)
        for k in range(1, basins // 2)
        for start in range(0, members, part)
    ]
    across = [Piece(k, 0, members, sizes) for k in range(basins // 2, far)]

    first = pack_with_codes(x, head, pltpu.with_memory_space_constraint(codes, pltpu.HBM))
    far_codes = lax.ppermute(first, "basin", pairs[far])
    arrived = {head: far_codes}
    for group in (across, near):
        for piece, chunk in zip(group, pack(x, group)):
            arrived[piece] = lax.ppermute(chunk, "basin", pairs[piece.k])

    own = Piece(0, 0, members, sizes)
    source, source_codes, inflow = [late, own], [far_codes, codes], None
    for _ in range(chain - 1):
        inflow = from_behind(source_panels(x, source, source_codes, inflow), "chain")
    if inflow is None:
        inflow = jnp.zeros((panel_starts(source)[-1], ROWS), jnp.float32)
    waited = [arrived[piece] for piece in near]
    inflow, waited = lax.optimization_barrier((inflow, waited))
    arrived.update(zip(near, waited))
    finished = lax.ppermute(source_chunk(x, late, far_codes, inflow), "basin", pairs[far])

    result = own_result(x, own, codes, inflow, late.count)
    for group in ([head] + near, across):
        chunks = [arrived[piece] for piece in group]
        result, chunks = lax.optimization_barrier((result, chunks))
        inflow = None
        for _ in range(chain - 1):
            inflow = from_behind(arrived_panels(chunks, group, codes, inflow), "chain")
        if inflow is None:
            inflow = jnp.zeros((panel_starts(group)[-1], ROWS), jnp.float32)
        result = arrived_result(chunks, group, codes, inflow, result)
    result = place_chunk(finished, late, result)
    return result.reshape(basins * members, sizes.tiles, 1, cell_count)


def solution(mesh):
    return jax.shard_map(
        local,
        mesh=mesh,
        in_specs=(P("mem", "basin", "grp", "chain", None), P(("grp", "basin"), "chain", None)),
        out_specs=P("mem", ("grp", "basin"), "chain", None),
        check_vma=False,
    )
```

```python
import jax
import jax.numpy as jnp
from jax import lax
from jax.experimental import pallas as pl
from jax.experimental.pallas import tpu as pltpu
from jax.sharding import PartitionSpec as P

ROWS = 128
SUB = 8
HBM = pl.BlockSpec(memory_space=pltpu.HBM)
VMEM = pl.BlockSpec(memory_space=pltpu.VMEM)


def exchange_pairs(count, k):
    return [(i, i ^ k) for i in range(count)]


def partner(k):
    return lax.axis_index("basin") ^ k


def from_behind(value, axis):
    count = lax.axis_size(axis)
    return lax.ppermute(value, axis, [(i, (i + 1) % count) for i in range(count)])


class Piece:
    def __init__(self, k, first, last, sizes):
        self.k, self.first, self.sizes = k, first, sizes
        self.members = last - first
        self.count = self.members * sizes.tiles
        self.rows = self.members * sizes.per_member
        self.groups = self.count // SUB

    def shape(self):
        return jax.ShapeDtypeStruct((self.rows, ROWS), jnp.float32)

    def panel(self):
        return jax.ShapeDtypeStruct((self.count, ROWS), jnp.float32)

    def gather(self, x_ref, buf_ref, sem):
        size = self.sizes.per_member
        tiles = x_ref.at[pl.ds(self.first, self.members), pl.ds(partner(self.k) * size, size)]
        return [pltpu.make_async_copy(tiles, buf_ref.at[pl.ds(0, self.rows)].reshape(self.members, size, ROWS), sem)]

    def place(self, o_ref):
        sizes = self.sizes
        start = (partner(self.k) * sizes.members + self.first) * sizes.per_member
        return o_ref.at[pl.ds(start, self.rows)]


class Sizes:
    def __init__(self, members, tiles, columns, basins):
        self.members, self.tiles, self.columns, self.basins = members, tiles, columns, basins
        self.per_member = tiles * columns

    def result(self):
        rows = self.basins * self.members * self.per_member
        return jax.ShapeDtypeStruct((rows, ROWS), jnp.float32)


def column_masks(d_ref, col, sizes):
    codes = d_ref[pl.ds(col, sizes.tiles, sizes.columns), :]
    codes = jnp.concatenate([codes] * (SUB // sizes.tiles), axis=0)
    lane = lax.broadcasted_iota(jnp.int32, codes.shape, 1)
    north = (codes == 1) & (lane > 0)
    south = (codes == 2) & (lane < ROWS - 1)
    return north, south


def advance(summed, north, south):
    zero = jnp.zeros_like(summed)
    up = pltpu.roll(jnp.where(north, summed, zero), ROWS - 1, 1)
    down = pltpu.roll(jnp.where(south, summed, zero), 1, 1)
    return jnp.where(north | south, zero, summed) + (up + down)


def sweep(x_ref, d_ref, carried, o_ref, sizes):
    for col in range(sizes.columns):
        north, south = column_masks(d_ref, col, sizes)
        for g in range(len(carried)):
            rows = pl.ds(g * SUB * sizes.columns + col, SUB, sizes.columns)
            summed = x_ref[rows, :]
            if carried[g] is not None:
                summed = summed + carried[g]
            if o_ref is not None:
                o_ref[rows, :] = summed
            if o_ref is None or col < sizes.columns - 1:
                carried[g] = advance(summed, north, south)
    return carried


def registers(in_ref, start, piece):
    if in_ref is None:
        return [None] * piece.groups
    upstream = lax.axis_index("chain") > 0
    values = [in_ref[pl.ds(start + g * SUB, SUB), :] for g in range(piece.groups)]
    return [jnp.where(upstream, value, jnp.zeros_like(value)) for value in values]


def store_registers(o_ref, start, carried):
    for g, value in enumerate(carried):
        o_ref[pl.ds(start + g * SUB, SUB), :] = value


def start_all(copies):
    for copy in copies:
        copy.start()


def wait_all(copies):
    for copy in copies:
        copy.wait()


def params(rows):
    return pltpu.CompilerParams(vmem_limit_bytes=(rows + 4096) * ROWS * 4)


def cost(rows):
    return pl.CostEstimate(flops=rows * ROWS, bytes_accessed=rows * ROWS, transcendentals=0)


def pack(x, piece):
    def body(x_ref, o_ref, sem):
        copies = piece.gather(x_ref, o_ref, sem)
        start_all(copies)
        wait_all(copies)

    return pl.pallas_call(
        body,
        out_shape=piece.shape(),
        in_specs=[HBM],
        out_specs=VMEM,
        scratch_shapes=[pltpu.SemaphoreType.DMA],
        compiler_params=params(piece.rows),
        cost_estimate=cost(piece.rows),
        name="pack",
    )(x)


def pack_with_codes(x, piece, codes):
    code_rows = codes.shape[0]

    def body(x_ref, d_ref, o_ref, buf, sem, code_sem):
        copies = piece.gather(x_ref, o_ref, sem)
        start_all(copies)
        copy = pltpu.make_async_copy(d_ref, buf, code_sem)
        copy.start()
        copy.wait()
        o_ref[pl.ds(piece.rows, code_rows), :] = buf[...].astype(jnp.float32)
        wait_all(copies)

    return pl.pallas_call(
        body,
        out_shape=jax.ShapeDtypeStruct((piece.rows + code_rows, ROWS), jnp.float32),
        in_specs=[HBM, HBM],
        out_specs=VMEM,
        scratch_shapes=[
            pltpu.VMEM(codes.shape, codes.dtype),
            pltpu.SemaphoreType.DMA,
            pltpu.SemaphoreType.DMA,
        ],
        compiler_params=params(piece.rows),
        cost_estimate=cost(piece.rows),
        name="pack_with_codes",
    )(x, codes)


def source_panels(x, pieces, codes, inflow):
    listed, starts = len(pieces), panel_starts(pieces)
    rows = sum(piece.rows for piece in pieces)

    def body(x_ref, *refs):
        d_refs, in_ref = refs[:listed], refs[listed] if inflow is not None else None
        o_ref, bufs, sem = refs[-2 - listed], refs[-1 - listed : -1], refs[-1]
        copies = [piece.gather(x_ref, bufs[i], sem.at[i]) for i, piece in enumerate(pieces)]
        for c in copies:
            start_all(c)
        for i, piece in enumerate(pieces):
            wait_all(copies[i])
            size = piece.sizes.per_member
            codes_ref = d_refs[i].at[pl.ds(codes[i].shape[0] - size, size)]
            carried = registers(in_ref, starts[i], piece)
            store_registers(o_ref, starts[i], sweep(bufs[i], codes_ref, carried, None, piece.sizes))

    return pl.pallas_call(
        body,
        out_shape=jax.ShapeDtypeStruct((starts[-1], ROWS), jnp.float32),
        in_specs=[HBM] + [VMEM] * (listed + (inflow is not None)),
        out_specs=VMEM,
        scratch_shapes=[pltpu.VMEM((piece.rows, ROWS), jnp.float32) for piece in pieces]
        + [pltpu.SemaphoreType.DMA((listed,))],
        compiler_params=params(2 * rows),
        cost_estimate=cost(rows),
        name="source_panels",
    )(x, *codes, *([inflow] if inflow is not None else []))


def source_chunk(x, piece, codes, inflow):
    def body(x_ref, d_ref, in_ref, o_ref, buf, sem):
        copies = piece.gather(x_ref, buf, sem)
        start_all(copies)
        wait_all(copies)
        size = piece.sizes.per_member
        codes_ref = d_ref.at[pl.ds(codes.shape[0] - size, size)]
        sweep(buf, codes_ref, registers(in_ref, 0, piece), o_ref, piece.sizes)

    return pl.pallas_call(
        body,
        out_shape=piece.shape(),
        in_specs=[HBM, VMEM, VMEM],
        out_specs=VMEM,
        scratch_shapes=[
            pltpu.VMEM((piece.rows, ROWS), jnp.float32),
            pltpu.SemaphoreType.DMA,
        ],
        compiler_params=params(3 * piece.rows),
        cost_estimate=cost(piece.rows),
        name="source_chunk",
    )(x, codes, inflow)


def panel_starts(pieces):
    starts = [0]
    for piece in pieces:
        starts.append(starts[-1] + piece.count)
    return starts


def arrived_panels(chunks, pieces, codes, inflow):
    listed, starts = len(pieces), panel_starts(pieces)
    rows = sum(piece.rows for piece in pieces)

    def body(*refs):
        x_refs, d_ref, o_ref = refs[:listed], refs[listed], refs[-1]
        in_ref = refs[listed + 1] if inflow is not None else None
        for x_ref, piece, start in zip(x_refs, pieces, starts):
            carried = registers(in_ref, start, piece)
            store_registers(o_ref, start, sweep(x_ref, d_ref, carried, None, piece.sizes))

    return pl.pallas_call(
        body,
        out_shape=jax.ShapeDtypeStruct((starts[-1], ROWS), jnp.float32),
        in_specs=[VMEM] * (listed + 1 + (inflow is not None)),
        out_specs=VMEM,
        compiler_params=params(2 * rows),
        cost_estimate=cost(rows),
        name="arrived_panels",
    )(*chunks, codes, *([inflow] if inflow is not None else []))


def own_result(x, piece, codes, inflow, start):
    def body(x_ref, d_ref, in_ref, o_ref, buf, out, sem, out_sem):
        copies = piece.gather(x_ref, buf, sem)
        start_all(copies)
        wait_all(copies)
        sweep(buf, d_ref, registers(in_ref, start, piece), out, piece.sizes)
        copy = pltpu.make_async_copy(out, piece.place(o_ref), out_sem)
        copy.start()
        copy.wait()

    return pl.pallas_call(
        body,
        out_shape=piece.sizes.result(),
        in_specs=[HBM, VMEM, VMEM],
        out_specs=HBM,
        scratch_shapes=[pltpu.VMEM((piece.rows, ROWS), jnp.float32)] * 2
        + [pltpu.SemaphoreType.DMA] * 2,
        compiler_params=params(2 * piece.rows),
        cost_estimate=cost(piece.rows),
        name="own_result",
    )(x, codes, inflow)


def arrived_result(chunks, pieces, codes, inflow, result):
    listed, starts = len(pieces), panel_starts(pieces)
    rows = sum(piece.rows for piece in pieces)

    def body(*refs):
        x_refs, d_ref, in_ref, o_ref = refs[:listed], refs[listed], refs[listed + 1], refs[listed + 3]
        outs, sem = refs[listed + 4 : -1], refs[-1]
        copies = []
        for i, piece in enumerate(pieces):
            sweep(x_refs[i], d_ref, registers(in_ref, starts[i], piece), outs[i], piece.sizes)
            copies.append(pltpu.make_async_copy(outs[i], piece.place(o_ref), sem.at[i]))
            copies[i].start()
        wait_all(copies)

    return pl.pallas_call(
        body,
        out_shape=pieces[0].sizes.result(),
        in_specs=[VMEM] * (listed + 2) + [HBM],
        out_specs=HBM,
        scratch_shapes=[pltpu.VMEM((piece.rows, ROWS), jnp.float32) for piece in pieces]
        + [pltpu.SemaphoreType.DMA((listed,))],
        input_output_aliases={listed + 2: 0},
        compiler_params=params(2 * rows),
        cost_estimate=cost(rows),
        name="arrived_result",
    )(*chunks, codes, inflow, result)


def place_chunk(chunk, piece, result):
    def body(x_ref, _, o_ref, sem):
        copy = pltpu.make_async_copy(x_ref, piece.place(o_ref), sem)
        copy.start()
        copy.wait()

    return pl.pallas_call(
        body,
        out_shape=piece.sizes.result(),
        in_specs=[VMEM, HBM],
        out_specs=HBM,
        scratch_shapes=[pltpu.SemaphoreType.DMA],
        input_output_aliases={1: 0},
        compiler_params=params(piece.rows),
        cost_estimate=cost(piece.rows),
        name="place_chunk",
    )(chunk, result)


def local(runoff, directions):
    basins, chain = lax.axis_size("basin"), lax.axis_size("chain")
    _, members, all_tiles, _, cell_count = runoff.shape
    sizes = Sizes(members, directions.shape[0], cell_count // ROWS, basins)
    x = runoff.reshape(members, all_tiles * sizes.columns, ROWS)
    x = pltpu.with_memory_space_constraint(x, pltpu.HBM)
    codes = directions.reshape(sizes.per_member, ROWS)
    pairs = {k: exchange_pairs(basins, k) for k in range(basins)}

    far = basins - 1
    cut = max(SUB // sizes.tiles, members // 4)
    late = Piece(far, cut, members, sizes)
    head = Piece(far, 0, cut, sizes)
    near = [Piece(k, 0, members, sizes) for k in range(1, basins // 2)]
    across = [Piece(k, 0, members, sizes) for k in range(basins // 2, far)]

    first = pack_with_codes(x, head, pltpu.with_memory_space_constraint(codes, pltpu.HBM))
    far_codes = lax.ppermute(first, "basin", pairs[far])
    arrived = {head: far_codes}
    for piece in across + near:
        arrived[piece] = lax.ppermute(pack(x, piece), "basin", pairs[piece.k])

    own = Piece(0, 0, members, sizes)
    source, source_codes, inflow = [late, own], [far_codes, codes], None
    for _ in range(chain - 1):
        inflow = from_behind(source_panels(x, source, source_codes, inflow), "chain")
    if inflow is None:
        inflow = jnp.zeros((panel_starts(source)[-1], ROWS), jnp.float32)
    result = own_result(x, own, codes, inflow, late.count)
    result, inflow = lax.optimization_barrier((result, inflow))
    finished = lax.ppermute(source_chunk(x, late, far_codes, inflow), "basin", pairs[far])
    for group in ([head] + near, across):
        chunks = [arrived[piece] for piece in group]
        result, chunks = lax.optimization_barrier((result, chunks))
        inflow = None
        for _ in range(chain - 1):
            inflow = from_behind(arrived_panels(chunks, group, codes, inflow), "chain")
        if inflow is None:
            inflow = jnp.zeros((panel_starts(group)[-1], ROWS), jnp.float32)
        result = arrived_result(chunks, group, codes, inflow, result)
    result = place_chunk(finished, late, result)
    return result.reshape(basins * members, sizes.tiles, 1, cell_count)


def solution(mesh):
    return jax.shard_map(
        local,
        mesh=mesh,
        in_specs=(P("mem", "basin", "grp", "chain", None), P(("grp", "basin"), "chain", None)),
        out_specs=P("mem", ("grp", "basin"), "chain", None),
        check_vma=False,
    )
```

```python
import jax
import jax.numpy as jnp
from jax import lax
from jax.experimental import pallas as pl
from jax.experimental.pallas import tpu as pltpu
from jax.sharding import PartitionSpec as P

ROWS = 128
SUB = 8
HBM = pl.BlockSpec(memory_space=pltpu.HBM)
VMEM = pl.BlockSpec(memory_space=pltpu.VMEM)


def exchange_pairs(count, k):
    return [(i, i ^ k) for i in range(count)]


def partner(k):
    return lax.axis_index("basin") ^ k


def from_behind(value, axis):
    count = lax.axis_size(axis)
    return lax.ppermute(value, axis, [(i, (i + 1) % count) for i in range(count)])


class Piece:
    def __init__(self, k, first, last, sizes):
        self.k, self.first, self.sizes = k, first, sizes
        self.members = last - first
        self.count = self.members * sizes.tiles
        self.rows = self.members * sizes.per_member
        self.groups = self.count // SUB

    def shape(self):
        return jax.ShapeDtypeStruct((self.rows, ROWS), jnp.float32)

    def panel(self):
        return jax.ShapeDtypeStruct((self.count, ROWS), jnp.float32)

    def gather(self, x_ref, buf_ref, sem):
        size = self.sizes.per_member
        tiles = x_ref.at[pl.ds(self.first, self.members), pl.ds(partner(self.k) * size, size)]
        return [pltpu.make_async_copy(tiles, buf_ref.at[pl.ds(0, self.rows)].reshape(self.members, size, ROWS), sem)]

    def place(self, o_ref):
        sizes = self.sizes
        start = (partner(self.k) * sizes.members + self.first) * sizes.per_member
        return o_ref.at[pl.ds(start, self.rows)]


class Sizes:
    def __init__(self, members, tiles, columns, basins):
        self.members, self.tiles, self.columns, self.basins = members, tiles, columns, basins
        self.per_member = tiles * columns

    def result(self):
        rows = self.basins * self.members * self.per_member
        return jax.ShapeDtypeStruct((rows, ROWS), jnp.float32)


def column_masks(d_ref, col, sizes):
    codes = d_ref[pl.ds(col, sizes.tiles, sizes.columns), :]
    codes = jnp.concatenate([codes] * (SUB // sizes.tiles), axis=0)
    lane = lax.broadcasted_iota(jnp.int32, codes.shape, 1)
    north = (codes == 1) & (lane > 0)
    south = (codes == 2) & (lane < ROWS - 1)
    return north, south


def advance(summed, north, south):
    zero = jnp.zeros_like(summed)
    up = pltpu.roll(jnp.where(north, summed, zero), ROWS - 1, 1)
    down = pltpu.roll(jnp.where(south, summed, zero), 1, 1)
    return jnp.where(north | south, zero, summed) + (up + down)


def sweep(x_ref, d_ref, carried, o_ref, sizes):
    for col in range(sizes.columns):
        north, south = column_masks(d_ref, col, sizes)
        for g in range(len(carried)):
            rows = pl.ds(g * SUB * sizes.columns + col, SUB, sizes.columns)
            summed = x_ref[rows, :]
            if carried[g] is not None:
                summed = summed + carried[g]
            if o_ref is not None:
                o_ref[rows, :] = summed
            if o_ref is None or col < sizes.columns - 1:
                carried[g] = advance(summed, north, south)
    return carried


def registers(in_ref, start, piece):
    if in_ref is None:
        return [None] * piece.groups
    upstream = lax.axis_index("chain") > 0
    values = [in_ref[pl.ds(start + g * SUB, SUB), :] for g in range(piece.groups)]
    return [jnp.where(upstream, value, jnp.zeros_like(value)) for value in values]


def store_registers(o_ref, start, carried):
    for g, value in enumerate(carried):
        o_ref[pl.ds(start + g * SUB, SUB), :] = value


def start_all(copies):
    for copy in copies:
        copy.start()


def wait_all(copies):
    for copy in copies:
        copy.wait()


def params(rows):
    return pltpu.CompilerParams(vmem_limit_bytes=(rows + 4096) * ROWS * 4)


def cost(rows):
    return pl.CostEstimate(flops=rows * ROWS, bytes_accessed=rows * ROWS, transcendentals=0)


def pack(x, piece):
    def body(x_ref, o_ref, sem):
        copies = piece.gather(x_ref, o_ref, sem)
        start_all(copies)
        wait_all(copies)

    return pl.pallas_call(
        body,
        out_shape=piece.shape(),
        in_specs=[HBM],
        out_specs=VMEM,
        scratch_shapes=[pltpu.SemaphoreType.DMA],
        compiler_params=params(piece.rows),
        cost_estimate=cost(piece.rows),
        name="pack",
    )(x)


def pack_with_codes(x, piece, codes):
    code_rows = codes.shape[0]

    def body(x_ref, d_ref, o_ref, buf, sem, code_sem):
        copies = piece.gather(x_ref, o_ref, sem)
        start_all(copies)
        copy = pltpu.make_async_copy(d_ref, buf, code_sem)
        copy.start()
        copy.wait()
        o_ref[pl.ds(piece.rows, code_rows), :] = buf[...].astype(jnp.float32)
        wait_all(copies)

    return pl.pallas_call(
        body,
        out_shape=jax.ShapeDtypeStruct((piece.rows + code_rows, ROWS), jnp.float32),
        in_specs=[HBM, HBM],
        out_specs=VMEM,
        scratch_shapes=[
            pltpu.VMEM(codes.shape, codes.dtype),
            pltpu.SemaphoreType.DMA,
            pltpu.SemaphoreType.DMA,
        ],
        compiler_params=params(piece.rows),
        cost_estimate=cost(piece.rows),
        name="pack_with_codes",
    )(x, codes)


def source_panels(x, pieces, codes, inflow):
    listed, starts = len(pieces), panel_starts(pieces)
    rows = sum(piece.rows for piece in pieces)

    def body(x_ref, *refs):
        d_refs, in_ref = refs[:listed], refs[listed] if inflow is not None else None
        o_ref, bufs, sem = refs[-2 - listed], refs[-1 - listed : -1], refs[-1]
        copies = [piece.gather(x_ref, bufs[i], sem.at[i]) for i, piece in enumerate(pieces)]
        for c in copies:
            start_all(c)
        for i, piece in enumerate(pieces):
            wait_all(copies[i])
            size = piece.sizes.per_member
            codes_ref = d_refs[i].at[pl.ds(codes[i].shape[0] - size, size)]
            carried = registers(in_ref, starts[i], piece)
            store_registers(o_ref, starts[i], sweep(bufs[i], codes_ref, carried, None, piece.sizes))

    return pl.pallas_call(
        body,
        out_shape=jax.ShapeDtypeStruct((starts[-1], ROWS), jnp.float32),
        in_specs=[HBM] + [VMEM] * (listed + (inflow is not None)),
        out_specs=VMEM,
        scratch_shapes=[pltpu.VMEM((piece.rows, ROWS), jnp.float32) for piece in pieces]
        + [pltpu.SemaphoreType.DMA((listed,))],
        compiler_params=params(2 * rows),
        cost_estimate=cost(rows),
        name="source_panels",
    )(x, *codes, *([inflow] if inflow is not None else []))


def source_chunk(x, piece, codes, inflow):
    def body(x_ref, d_ref, in_ref, o_ref, buf, sem):
        copies = piece.gather(x_ref, buf, sem)
        start_all(copies)
        wait_all(copies)
        size = piece.sizes.per_member
        codes_ref = d_ref.at[pl.ds(codes.shape[0] - size, size)]
        sweep(buf, codes_ref, registers(in_ref, 0, piece), o_ref, piece.sizes)

    return pl.pallas_call(
        body,
        out_shape=piece.shape(),
        in_specs=[HBM, VMEM, VMEM],
        out_specs=VMEM,
        scratch_shapes=[
            pltpu.VMEM((piece.rows, ROWS), jnp.float32),
            pltpu.SemaphoreType.DMA,
        ],
        compiler_params=params(3 * piece.rows),
        cost_estimate=cost(piece.rows),
        name="source_chunk",
    )(x, codes, inflow)


def panel_starts(pieces):
    starts = [0]
    for piece in pieces:
        starts.append(starts[-1] + piece.count)
    return starts


def arrived_panels(chunks, pieces, codes, inflow):
    listed, starts = len(pieces), panel_starts(pieces)
    rows = sum(piece.rows for piece in pieces)

    def body(*refs):
        x_refs, d_ref, o_ref = refs[:listed], refs[listed], refs[-1]
        in_ref = refs[listed + 1] if inflow is not None else None
        for x_ref, piece, start in zip(x_refs, pieces, starts):
            carried = registers(in_ref, start, piece)
            store_registers(o_ref, start, sweep(x_ref, d_ref, carried, None, piece.sizes))

    return pl.pallas_call(
        body,
        out_shape=jax.ShapeDtypeStruct((starts[-1], ROWS), jnp.float32),
        in_specs=[VMEM] * (listed + 1 + (inflow is not None)),
        out_specs=VMEM,
        compiler_params=params(2 * rows),
        cost_estimate=cost(rows),
        name="arrived_panels",
    )(*chunks, codes, *([inflow] if inflow is not None else []))


def own_result(x, piece, codes, inflow, start):
    def body(x_ref, d_ref, in_ref, o_ref, buf, out, sem, out_sem):
        copies = piece.gather(x_ref, buf, sem)
        start_all(copies)
        wait_all(copies)
        sweep(buf, d_ref, registers(in_ref, start, piece), out, piece.sizes)
        copy = pltpu.make_async_copy(out, piece.place(o_ref), out_sem)
        copy.start()
        copy.wait()

    return pl.pallas_call(
        body,
        out_shape=piece.sizes.result(),
        in_specs=[HBM, VMEM, VMEM],
        out_specs=HBM,
        scratch_shapes=[pltpu.VMEM((piece.rows, ROWS), jnp.float32)] * 2
        + [pltpu.SemaphoreType.DMA] * 2,
        compiler_params=params(2 * piece.rows),
        cost_estimate=cost(piece.rows),
        name="own_result",
    )(x, codes, inflow)


def arrived_result(chunks, pieces, codes, inflow, result):
    listed, starts = len(pieces), panel_starts(pieces)
    rows = sum(piece.rows for piece in pieces)

    def body(*refs):
        x_refs, d_ref, in_ref, o_ref = refs[:listed], refs[listed], refs[listed + 1], refs[listed + 3]
        outs, sem = refs[listed + 4 : -1], refs[-1]
        copies = []
        for i, piece in enumerate(pieces):
            sweep(x_refs[i], d_ref, registers(in_ref, starts[i], piece), outs[i], piece.sizes)
            copies.append(pltpu.make_async_copy(outs[i], piece.place(o_ref), sem.at[i]))
            copies[i].start()
        wait_all(copies)

    return pl.pallas_call(
        body,
        out_shape=pieces[0].sizes.result(),
        in_specs=[VMEM] * (listed + 2) + [HBM],
        out_specs=HBM,
        scratch_shapes=[pltpu.VMEM((piece.rows, ROWS), jnp.float32) for piece in pieces]
        + [pltpu.SemaphoreType.DMA((listed,))],
        input_output_aliases={listed + 2: 0},
        compiler_params=params(2 * rows),
        cost_estimate=cost(rows),
        name="arrived_result",
    )(*chunks, codes, inflow, result)


def place_chunk(chunk, piece, result):
    def body(x_ref, _, o_ref, sem):
        copy = pltpu.make_async_copy(x_ref, piece.place(o_ref), sem)
        copy.start()
        copy.wait()

    return pl.pallas_call(
        body,
        out_shape=piece.sizes.result(),
        in_specs=[VMEM, HBM],
        out_specs=HBM,
        scratch_shapes=[pltpu.SemaphoreType.DMA],
        input_output_aliases={1: 0},
        compiler_params=params(piece.rows),
        cost_estimate=cost(piece.rows),
        name="place_chunk",
    )(chunk, result)


def local(runoff, directions):
    basins, chain = lax.axis_size("basin"), lax.axis_size("chain")
    _, members, all_tiles, _, cell_count = runoff.shape
    sizes = Sizes(members, directions.shape[0], cell_count // ROWS, basins)
    x = runoff.reshape(members, all_tiles * sizes.columns, ROWS)
    x = pltpu.with_memory_space_constraint(x, pltpu.HBM)
    codes = directions.reshape(sizes.per_member, ROWS)
    pairs = {k: exchange_pairs(basins, k) for k in range(basins)}

    far = basins - 1
    align = SUB // sizes.tiles
    cut = max(align, members // 4)
    late = Piece(far, cut, members, sizes)
    head = Piece(far, 0, cut, sizes)
    near = [Piece(k, 0, members, sizes) for k in range(1, basins // 2)]
    most = members - align
    across = [
        Piece(k, start, stop, sizes)
        for k in range(basins // 2, far)
        for start, stop in ((0, most), (most, members))
    ]

    first = pack_with_codes(x, head, pltpu.with_memory_space_constraint(codes, pltpu.HBM))
    far_codes = lax.ppermute(first, "basin", pairs[far])
    arrived = {head: far_codes}
    for piece in across + near:
        arrived[piece] = lax.ppermute(pack(x, piece), "basin", pairs[piece.k])

    own = Piece(0, 0, members, sizes)
    source, source_codes, inflow = [late, own], [far_codes, codes], None
    for _ in range(chain - 1):
        inflow = from_behind(source_panels(x, source, source_codes, inflow), "chain")
    if inflow is None:
        inflow = jnp.zeros((panel_starts(source)[-1], ROWS), jnp.float32)
    result = own_result(x, own, codes, inflow, late.count)
    result, inflow = lax.optimization_barrier((result, inflow))
    finished = lax.ppermute(source_chunk(x, late, far_codes, inflow), "basin", pairs[far])
    for group in ([head] + near, across):
        chunks = [arrived[piece] for piece in group]
        result, chunks = lax.optimization_barrier((result, chunks))
        inflow = None
        for _ in range(chain - 1):
            inflow = from_behind(arrived_panels(chunks, group, codes, inflow), "chain")
        if inflow is None:
            inflow = jnp.zeros((panel_starts(group)[-1], ROWS), jnp.float32)
        result = arrived_result(chunks, group, codes, inflow, result)
    result = place_chunk(finished, late, result)
    return result.reshape(basins * members, sizes.tiles, 1, cell_count)


def solution(mesh):
    return jax.shard_map(
        local,
        mesh=mesh,
        in_specs=(P("mem", "basin", "grp", "chain", None), P(("grp", "basin"), "chain", None)),
        out_specs=P("mem", ("grp", "basin"), "chain", None),
        check_vma=False,
    )
```

```python
import jax
import jax.numpy as jnp
from jax import lax
from jax.experimental import pallas as pl
from jax.experimental.pallas import tpu as pltpu
from jax.sharding import PartitionSpec as P

ROWS = 128
SUB = 8
HBM = pl.BlockSpec(memory_space=pltpu.HBM)
VMEM = pl.BlockSpec(memory_space=pltpu.VMEM)


def exchange_pairs(count, k):
    return [(i, i ^ k) for i in range(count)]


def partner(k):
    return lax.axis_index("basin") ^ k


def from_behind(value, axis):
    count = lax.axis_size(axis)
    return lax.ppermute(value, axis, [(i, (i + 1) % count) for i in range(count)])


class Piece:
    def __init__(self, k, first, last, sizes):
        self.k, self.first, self.sizes = k, first, sizes
        self.members = last - first
        self.count = self.members * sizes.tiles
        self.rows = self.members * sizes.per_member
        self.groups = self.count // SUB

    def shape(self):
        return jax.ShapeDtypeStruct((self.rows, ROWS), jnp.float32)

    def panel(self):
        return jax.ShapeDtypeStruct((self.count, ROWS), jnp.float32)

    def gather(self, x_ref, buf_ref, sem):
        size = self.sizes.per_member
        tiles = x_ref.at[pl.ds(self.first, self.members), pl.ds(partner(self.k) * size, size)]
        return [pltpu.make_async_copy(tiles, buf_ref.at[pl.ds(0, self.rows)].reshape(self.members, size, ROWS), sem)]

    def place(self, o_ref):
        sizes = self.sizes
        start = (partner(self.k) * sizes.members + self.first) * sizes.tiles
        return o_ref.at[pl.ds(start, self.count)]

    def leave(self, x_ref, o_ref, sem):
        rows = x_ref.reshape(self.count, self.sizes.columns, ROWS)
        return pltpu.make_async_copy(rows, self.place(o_ref), sem)

    def leave_halves(self, x_ref, o_ref, sems):
        rows = x_ref.reshape(self.count, self.sizes.columns, ROWS)
        half = self.sizes.columns // 2
        return [
            pltpu.make_async_copy(
                rows.at[:, pl.ds(i * half, half)],
                self.place(o_ref).at[:, pl.ds(i * half, half)],
                sems.at[i],
            )
            for i in range(2)
        ]


class Sizes:
    def __init__(self, members, tiles, columns, basins):
        self.members, self.tiles, self.columns, self.basins = members, tiles, columns, basins
        self.per_member = tiles * columns

    def result(self):
        count = self.basins * self.members * self.tiles
        return jax.ShapeDtypeStruct((count, self.columns, ROWS), jnp.float32)


def column_offsets(d_ref, col, sizes):
    codes = d_ref[pl.ds(col, sizes.tiles, sizes.columns), :]
    codes = jnp.concatenate([codes] * (SUB // sizes.tiles), axis=0)
    lane = lax.broadcasted_iota(jnp.int32, codes.shape, 1)
    north = (codes == 1) & (lane > 0)
    south = (codes == 2) & (lane < ROWS - 1)
    return jnp.where(north, -1, jnp.where(south, 1, 0))


def composed(first, second):
    above, below = pltpu.roll(second, 1, 1), pltpu.roll(second, ROWS - 1, 1)
    return first + jnp.where(first == 0, second, jnp.where(first < 0, above, below))


def advance(summed, offsets, reach):
    zero = jnp.zeros_like(summed)
    moved = jnp.where(offsets == 0, summed, zero)
    for by in range(1, reach + 1):
        up = pltpu.roll(jnp.where(offsets == -by, summed, zero), ROWS - by, 1)
        down = pltpu.roll(jnp.where(offsets == by, summed, zero), by, 1)
        moved = moved + (up + down)
    return moved


def sweep(x_ref, d_ref, carried, o_ref, sizes, outflow=True, halfway=None):
    carried = list(carried)
    for col in range(0, sizes.columns, 2):
        first, second = (column_offsets(d_ref, c, sizes) for c in (col, col + 1))
        both = composed(first, second)
        last = col + 2 == sizes.columns and not outflow
        for g in range(len(carried)):
            at = g * SUB * sizes.columns + col
            here, after = pl.ds(at, SUB, sizes.columns), pl.ds(at + 1, SUB, sizes.columns)
            summed, water = x_ref[here, :], x_ref[after, :]
            if carried[g] is not None:
                summed = summed + carried[g]
            if not last:
                carried[g] = advance(water, second, 1) + advance(summed, both, 2)
            if o_ref is not None:
                o_ref[here, :] = summed
                o_ref[after, :] = water + advance(summed, first, 1)
        if halfway is not None and col + 2 == sizes.columns // 2:
            halfway()
    return carried


def registers(in_ref, start, piece):
    if in_ref is None:
        return [None] * piece.groups
    upstream = lax.axis_index("chain") > 0
    values = [in_ref[pl.ds(start + g * SUB, SUB), :] for g in range(piece.groups)]
    return [jnp.where(upstream, value, jnp.zeros_like(value)) for value in values]


def store_registers(o_ref, start, carried):
    for g, value in enumerate(carried):
        o_ref[pl.ds(start + g * SUB, SUB), :] = value


def start_all(copies):
    for copy in copies:
        copy.start()


def wait_all(copies):
    for copy in copies:
        copy.wait()


def params(rows):
    return pltpu.CompilerParams(vmem_limit_bytes=(rows + 4096) * ROWS * 4)


def cost(rows):
    return pl.CostEstimate(flops=rows * ROWS, bytes_accessed=rows * ROWS, transcendentals=0)


def pack(x, piece):
    def body(x_ref, o_ref, sem):
        copies = piece.gather(x_ref, o_ref, sem)
        start_all(copies)
        wait_all(copies)

    return pl.pallas_call(
        body,
        out_shape=piece.shape(),
        in_specs=[HBM],
        out_specs=VMEM,
        scratch_shapes=[pltpu.SemaphoreType.DMA],
        compiler_params=params(piece.rows),
        cost_estimate=cost(piece.rows),
        name="pack",
    )(x)


def pack_with_codes(x, piece, codes):
    code_rows = codes.shape[0]

    def body(x_ref, d_ref, o_ref, buf, sem, code_sem):
        copies = piece.gather(x_ref, o_ref, sem)
        start_all(copies)
        copy = pltpu.make_async_copy(d_ref, buf, code_sem)
        copy.start()
        copy.wait()
        o_ref[pl.ds(piece.rows, code_rows), :] = buf[...].astype(jnp.float32)
        wait_all(copies)

    return pl.pallas_call(
        body,
        out_shape=jax.ShapeDtypeStruct((piece.rows + code_rows, ROWS), jnp.float32),
        in_specs=[HBM, HBM],
        out_specs=VMEM,
        scratch_shapes=[
            pltpu.VMEM(codes.shape, codes.dtype),
            pltpu.SemaphoreType.DMA,
            pltpu.SemaphoreType.DMA,
        ],
        compiler_params=params(piece.rows),
        cost_estimate=cost(piece.rows),
        name="pack_with_codes",
    )(x, codes)


def source_panels(x, pieces, codes, inflow):
    listed, starts = len(pieces), panel_starts(pieces)
    rows = sum(piece.rows for piece in pieces)

    def body(x_ref, *refs):
        d_refs, in_ref = refs[:listed], refs[listed] if inflow is not None else None
        o_ref, bufs, sem = refs[-2 - listed], refs[-1 - listed : -1], refs[-1]
        copies = [piece.gather(x_ref, bufs[i], sem.at[i]) for i, piece in enumerate(pieces)]
        for c in copies:
            start_all(c)
        for i, piece in enumerate(pieces):
            wait_all(copies[i])
            size = piece.sizes.per_member
            codes_ref = d_refs[i].at[pl.ds(codes[i].shape[0] - size, size)]
            carried = registers(in_ref, starts[i], piece)
            store_registers(o_ref, starts[i], sweep(bufs[i], codes_ref, carried, None, piece.sizes))

    return pl.pallas_call(
        body,
        out_shape=jax.ShapeDtypeStruct((starts[-1], ROWS), jnp.float32),
        in_specs=[HBM] + [VMEM] * (listed + (inflow is not None)),
        out_specs=VMEM,
        scratch_shapes=[pltpu.VMEM((piece.rows, ROWS), jnp.float32) for piece in pieces]
        + [pltpu.SemaphoreType.DMA((listed,))],
        compiler_params=params(2 * rows),
        cost_estimate=cost(rows),
        name="source_panels",
    )(x, *codes, *([inflow] if inflow is not None else []))


def source_chunk(x, piece, codes, inflow):
    def body(x_ref, d_ref, in_ref, o_ref, buf, sem):
        copies = piece.gather(x_ref, buf, sem)
        start_all(copies)
        wait_all(copies)
        size = piece.sizes.per_member
        codes_ref = d_ref.at[pl.ds(codes.shape[0] - size, size)]
        sweep(buf, codes_ref, registers(in_ref, 0, piece), o_ref, piece.sizes, outflow=False)

    return pl.pallas_call(
        body,
        out_shape=piece.shape(),
        in_specs=[HBM, VMEM, VMEM],
        out_specs=VMEM,
        scratch_shapes=[
            pltpu.VMEM((piece.rows, ROWS), jnp.float32),
            pltpu.SemaphoreType.DMA,
        ],
        compiler_params=params(3 * piece.rows),
        cost_estimate=cost(piece.rows),
        name="source_chunk",
    )(x, codes, inflow)


def panel_starts(pieces):
    starts = [0]
    for piece in pieces:
        starts.append(starts[-1] + piece.count)
    return starts


def arrived_panels(chunks, pieces, codes, inflow):
    listed, starts = len(pieces), panel_starts(pieces)
    rows = sum(piece.rows for piece in pieces)
    kept = inflow is None

    def body(*refs):
        x_refs, d_ref = refs[:listed], refs[listed]
        in_ref = None if kept else refs[listed + 1]
        o_ref = refs[listed + 1 + (not kept)]
        row_refs = refs[listed + 2 :] if kept else [None] * listed
        for x_ref, row_ref, piece, start in zip(x_refs, row_refs, pieces, starts):
            carried = registers(in_ref, start, piece)
            store_registers(o_ref, start, sweep(x_ref, d_ref, carried, row_ref, piece.sizes))

    out = pl.pallas_call(
        body,
        out_shape=[jax.ShapeDtypeStruct((starts[-1], ROWS), jnp.float32)]
        + [piece.shape() for piece in pieces if kept],
        in_specs=[VMEM] * (listed + 1 + (not kept)),
        out_specs=[VMEM] * (1 + listed * kept),
        compiler_params=params(2 * rows),
        cost_estimate=cost(rows),
        name="arrived_panels",
    )(*chunks, codes, *([] if kept else [inflow]))
    return out[0], out[1:]


def head_result(chunks, pieces, result):
    listed = len(pieces)

    def body(*refs):
        x_refs, o_ref, sem = refs[:listed], refs[listed + 1], refs[-1]

        @pl.when(lax.axis_index("chain") == 0)
        def _():
            copies = [piece.leave(x_refs[i], o_ref, sem.at[i]) for i, piece in enumerate(pieces)]
            start_all(copies)
            wait_all(copies)

    return pl.pallas_call(
        body,
        out_shape=pieces[0].sizes.result(),
        in_specs=[VMEM] * listed + [HBM],
        out_specs=HBM,
        scratch_shapes=[pltpu.SemaphoreType.DMA((listed,))],
        input_output_aliases={listed: 0},
        compiler_params=params(sum(piece.rows for piece in pieces)),
        cost_estimate=cost(sum(piece.rows for piece in pieces)),
        name="head_result",
    )(*chunks, result)


def own_result(x, piece, codes, inflow, start):
    def body(x_ref, d_ref, in_ref, o_ref, buf, out, sem, out_sem):
        copies = piece.gather(x_ref, buf, sem)
        start_all(copies)
        wait_all(copies)
        sweep(buf, d_ref, registers(in_ref, start, piece), out, piece.sizes, outflow=False)
        copy = piece.leave(out, o_ref, out_sem)
        copy.start()
        copy.wait()

    return pl.pallas_call(
        body,
        out_shape=piece.sizes.result(),
        in_specs=[HBM, VMEM, VMEM],
        out_specs=HBM,
        scratch_shapes=[pltpu.VMEM((piece.rows, ROWS), jnp.float32)] * 2
        + [pltpu.SemaphoreType.DMA] * 2,
        compiler_params=params(2 * piece.rows),
        cost_estimate=cost(piece.rows),
        name="own_result",
    )(x, codes, inflow)


def arrived_result(chunks, pieces, codes, inflow, result):
    listed, starts = len(pieces), panel_starts(pieces)
    rows = sum(piece.rows for piece in pieces)

    def body(*refs):
        x_refs, d_ref, in_ref, o_ref = refs[:listed], refs[listed], refs[listed + 1], refs[listed + 3]
        outs, sem = refs[listed + 4 : -1], refs[-1]

        @pl.when(lax.axis_index("chain") > 0)
        def _():
            copies = []
            for i, piece in enumerate(pieces):
                halves = piece.leave_halves(outs[i], o_ref, sem.at[i])
                carried = registers(in_ref, starts[i], piece)
                sweep(
                    x_refs[i], d_ref, carried, outs[i], piece.sizes, outflow=False, halfway=halves[0].start
                )
                halves[1].start()
                copies += halves
            wait_all(copies)

    return pl.pallas_call(
        body,
        out_shape=pieces[0].sizes.result(),
        in_specs=[VMEM] * (listed + 2) + [HBM],
        out_specs=HBM,
        scratch_shapes=[pltpu.VMEM((piece.rows, ROWS), jnp.float32) for piece in pieces]
        + [pltpu.SemaphoreType.DMA((listed, 2))],
        input_output_aliases={listed + 2: 0},
        compiler_params=params(2 * rows),
        cost_estimate=cost(rows),
        name="arrived_result",
    )(*chunks, codes, inflow, result)


def place_chunk(chunk, piece, result):
    def body(x_ref, _, o_ref, sem):
        copy = piece.leave(x_ref, o_ref, sem)
        copy.start()
        copy.wait()

    return pl.pallas_call(
        body,
        out_shape=piece.sizes.result(),
        in_specs=[VMEM, HBM],
        out_specs=HBM,
        scratch_shapes=[pltpu.SemaphoreType.DMA],
        input_output_aliases={1: 0},
        compiler_params=params(piece.rows),
        cost_estimate=cost(piece.rows),
        name="place_chunk",
    )(chunk, result)


def local(runoff, directions):
    basins, chain = lax.axis_size("basin"), lax.axis_size("chain")
    _, members, all_tiles, _, cell_count = runoff.shape
    sizes = Sizes(members, directions.shape[0], cell_count // ROWS, basins)
    x = runoff.reshape(members, all_tiles * sizes.columns, ROWS)
    x = pltpu.with_memory_space_constraint(x, pltpu.HBM)
    codes = directions.reshape(sizes.per_member, ROWS)
    pairs = {k: exchange_pairs(basins, k) for k in range(basins)}

    far = basins - 1
    cut = max(SUB // sizes.tiles, members // 4)
    late = Piece(far, cut, members, sizes)
    head = Piece(far, 0, cut, sizes)
    near = [Piece(k, 0, members, sizes) for k in range(1, basins // 2)]
    across = [Piece(k, 0, members, sizes) for k in range(basins // 2, far)]

    first = pack_with_codes(x, head, pltpu.with_memory_space_constraint(codes, pltpu.HBM))
    far_codes = lax.ppermute(first, "basin", pairs[far])
    arrived = {head: far_codes}
    for piece in across + near:
        arrived[piece] = lax.ppermute(pack(x, piece), "basin", pairs[piece.k])

    own = Piece(0, 0, members, sizes)
    source, source_codes, inflow = [late, own], [far_codes, codes], None
    for _ in range(chain - 1):
        inflow = from_behind(source_panels(x, source, source_codes, inflow), "chain")
    if inflow is None:
        inflow = jnp.zeros((panel_starts(source)[-1], ROWS), jnp.float32)
    result = own_result(x, own, codes, inflow, late.count)
    result, inflow = lax.optimization_barrier((result, inflow))
    finished = lax.ppermute(source_chunk(x, late, far_codes, inflow), "basin", pairs[far])
    for group in ([head] + near, across):
        chunks = [arrived[piece] for piece in group]
        result, chunks = lax.optimization_barrier((result, chunks))
        panel, rows = arrived_panels(chunks, group, codes, None)
        inflow = panel
        for step in range(chain - 1):
            inflow = from_behind(panel, "chain")
            if step < chain - 2:
                panel, _ = arrived_panels(chunks, group, codes, inflow)
        result = head_result(rows, group, result)
        result = arrived_result(chunks, group, codes, inflow, result)
    result = place_chunk(finished, late, result)
    return result.reshape(basins * members, sizes.tiles, 1, cell_count)


def solution(mesh):
    return jax.shard_map(
        local,
        mesh=mesh,
        in_specs=(P("mem", "basin", "grp", "chain", None), P(("grp", "basin"), "chain", None)),
        out_specs=P("mem", ("grp", "basin"), "chain", None),
        check_vma=False,
    )
```

```python
import jax
import jax.numpy as jnp
from jax import lax
from jax.experimental import pallas as pl
from jax.experimental.pallas import tpu as pltpu
from jax.sharding import PartitionSpec as P

ROWS = 128
SUB = 8
HBM = pl.BlockSpec(memory_space=pltpu.HBM)
VMEM = pl.BlockSpec(memory_space=pltpu.VMEM)


def exchange_pairs(count, k):
    return [(i, i ^ k) for i in range(count)]


def partner(k):
    return lax.axis_index("basin") ^ k


def from_behind(value, axis):
    count = lax.axis_size(axis)
    return lax.ppermute(value, axis, [(i, (i + 1) % count) for i in range(count)])


class Piece:
    def __init__(self, k, first, last, sizes):
        self.k, self.first, self.sizes = k, first, sizes
        self.members = last - first
        self.count = self.members * sizes.tiles
        self.rows = self.members * sizes.per_member
        self.groups = self.count // SUB

    def shape(self):
        return jax.ShapeDtypeStruct((self.rows, ROWS), jnp.float32)

    def panel(self):
        return jax.ShapeDtypeStruct((self.count, ROWS), jnp.float32)

    def gather(self, x_ref, buf_ref, sem):
        size = self.sizes.per_member
        tiles = x_ref.at[pl.ds(self.first, self.members), pl.ds(partner(self.k) * size, size)]
        return [pltpu.make_async_copy(tiles, buf_ref.at[pl.ds(0, self.rows)].reshape(self.members, size, ROWS), sem)]

    def place(self, o_ref):
        sizes = self.sizes
        start = (partner(self.k) * sizes.members + self.first) * sizes.tiles
        return o_ref.at[pl.ds(start, self.count)]

    def leave(self, x_ref, o_ref, sem):
        rows = x_ref.reshape(self.count, self.sizes.columns, ROWS)
        return pltpu.make_async_copy(rows, self.place(o_ref), sem)

    def leave_halves(self, x_ref, o_ref, sems):
        rows = x_ref.reshape(self.count, self.sizes.columns, ROWS)
        half = self.sizes.columns // 2
        return [
            pltpu.make_async_copy(
                rows.at[:, pl.ds(i * half, half)],
                self.place(o_ref).at[:, pl.ds(i * half, half)],
                sems.at[i],
            )
            for i in range(2)
        ]


class Sizes:
    def __init__(self, members, tiles, columns, basins):
        self.members, self.tiles, self.columns, self.basins = members, tiles, columns, basins
        self.per_member = tiles * columns

    def result(self):
        count = self.basins * self.members * self.tiles
        return jax.ShapeDtypeStruct((count, self.columns, ROWS), jnp.float32)


def column_offsets(d_ref, col, sizes):
    codes = d_ref[pl.ds(col, sizes.tiles, sizes.columns), :]
    codes = jnp.concatenate([codes] * (SUB // sizes.tiles), axis=0)
    lane = lax.broadcasted_iota(jnp.int32, codes.shape, 1)
    north = (codes == 1) & (lane > 0)
    south = (codes == 2) & (lane < ROWS - 1)
    return jnp.where(north, -1, jnp.where(south, 1, 0))


def composed(first, second):
    above, below = pltpu.roll(second, 1, 1), pltpu.roll(second, ROWS - 1, 1)
    return first + jnp.where(first == 0, second, jnp.where(first < 0, above, below))


def advance(summed, offsets, reach):
    zero = jnp.zeros_like(summed)
    moved = jnp.where(offsets == 0, summed, zero)
    for by in range(1, reach + 1):
        up = pltpu.roll(jnp.where(offsets == -by, summed, zero), ROWS - by, 1)
        down = pltpu.roll(jnp.where(offsets == by, summed, zero), by, 1)
        moved = moved + (up + down)
    return moved


def sweep(x_ref, d_ref, carried, o_ref, sizes, outflow=True, halfway=None):
    carried = list(carried)
    for col in range(0, sizes.columns, 2):
        first, second = (column_offsets(d_ref, c, sizes) for c in (col, col + 1))
        both = composed(first, second)
        last = col + 2 == sizes.columns and not outflow
        for g in range(len(carried)):
            at = g * SUB * sizes.columns + col
            here, after = pl.ds(at, SUB, sizes.columns), pl.ds(at + 1, SUB, sizes.columns)
            summed, water = x_ref[here, :], x_ref[after, :]
            if carried[g] is not None:
                summed = summed + carried[g]
            if not last:
                carried[g] = advance(water, second, 1) + advance(summed, both, 2)
            if o_ref is not None:
                o_ref[here, :] = summed
                o_ref[after, :] = water + advance(summed, first, 1)
        if halfway is not None and col + 2 == sizes.columns // 2:
            halfway()
    return carried


def registers(in_ref, start, piece):
    if in_ref is None:
        return [None] * piece.groups
    upstream = lax.axis_index("chain") > 0
    values = [in_ref[pl.ds(start + g * SUB, SUB), :] for g in range(piece.groups)]
    return [jnp.where(upstream, value, jnp.zeros_like(value)) for value in values]


def store_registers(o_ref, start, carried):
    for g, value in enumerate(carried):
        o_ref[pl.ds(start + g * SUB, SUB), :] = value


def start_all(copies):
    for copy in copies:
        copy.start()


def wait_all(copies):
    for copy in copies:
        copy.wait()


def params(rows):
    return pltpu.CompilerParams(vmem_limit_bytes=(rows + 4096) * ROWS * 4)


def cost(rows):
    return pl.CostEstimate(flops=rows * ROWS, bytes_accessed=rows * ROWS, transcendentals=0)


def pack(x, piece):
    def body(x_ref, o_ref, sem):
        copies = piece.gather(x_ref, o_ref, sem)
        start_all(copies)
        wait_all(copies)

    return pl.pallas_call(
        body,
        out_shape=piece.shape(),
        in_specs=[HBM],
        out_specs=VMEM,
        scratch_shapes=[pltpu.SemaphoreType.DMA],
        compiler_params=params(piece.rows),
        cost_estimate=cost(piece.rows),
        name="pack",
    )(x)


def pack_with_codes(x, piece, codes, code_rows):
    def body(x_ref, d_ref, o_ref, buf, sem, code_sem):
        copies = piece.gather(x_ref, o_ref, sem)
        start_all(copies)
        shares = codes.shape[0] // code_rows
        share = lax.axis_index("mem") if shares > 1 else 0
        mine = d_ref.at[pl.ds(pl.multiple_of(share * code_rows, code_rows), code_rows)]
        copy = pltpu.make_async_copy(mine, buf, code_sem)
        copy.start()
        copy.wait()
        o_ref[pl.ds(piece.rows, code_rows), :] = buf[...].astype(jnp.float32)
        wait_all(copies)

    return pl.pallas_call(
        body,
        out_shape=jax.ShapeDtypeStruct((piece.rows + code_rows, ROWS), jnp.float32),
        in_specs=[HBM, HBM],
        out_specs=VMEM,
        scratch_shapes=[
            pltpu.VMEM((code_rows, ROWS), codes.dtype),
            pltpu.SemaphoreType.DMA,
            pltpu.SemaphoreType.DMA,
        ],
        compiler_params=params(piece.rows),
        cost_estimate=cost(piece.rows),
        name="pack_with_codes",
    )(x, codes)


def source_panels(x, pieces, codes, inflow):
    listed, starts = len(pieces), panel_starts(pieces)
    rows = sum(piece.rows for piece in pieces)

    def body(x_ref, *refs):
        d_refs, in_ref = refs[:listed], refs[listed] if inflow is not None else None
        o_ref, bufs, sem = refs[-2 - listed], refs[-1 - listed : -1], refs[-1]
        copies = [piece.gather(x_ref, bufs[i], sem.at[i]) for i, piece in enumerate(pieces)]
        for c in copies:
            start_all(c)
        for i, piece in enumerate(pieces):
            wait_all(copies[i])
            size = piece.sizes.per_member
            codes_ref = d_refs[i].at[pl.ds(codes[i].shape[0] - size, size)]
            carried = registers(in_ref, starts[i], piece)
            store_registers(o_ref, starts[i], sweep(bufs[i], codes_ref, carried, None, piece.sizes))

    return pl.pallas_call(
        body,
        out_shape=jax.ShapeDtypeStruct((starts[-1], ROWS), jnp.float32),
        in_specs=[HBM] + [VMEM] * (listed + (inflow is not None)),
        out_specs=VMEM,
        scratch_shapes=[pltpu.VMEM((piece.rows, ROWS), jnp.float32) for piece in pieces]
        + [pltpu.SemaphoreType.DMA((listed,))],
        compiler_params=params(2 * rows),
        cost_estimate=cost(rows),
        name="source_panels",
    )(x, *codes, *([inflow] if inflow is not None else []))


def source_chunk(x, piece, codes, inflow):
    def body(x_ref, d_ref, in_ref, o_ref, buf, sem):
        copies = piece.gather(x_ref, buf, sem)
        start_all(copies)
        wait_all(copies)
        size = piece.sizes.per_member
        codes_ref = d_ref.at[pl.ds(codes.shape[0] - size, size)]
        sweep(buf, codes_ref, registers(in_ref, 0, piece), o_ref, piece.sizes, outflow=False)

    return pl.pallas_call(
        body,
        out_shape=piece.shape(),
        in_specs=[HBM, VMEM, VMEM],
        out_specs=VMEM,
        scratch_shapes=[
            pltpu.VMEM((piece.rows, ROWS), jnp.float32),
            pltpu.SemaphoreType.DMA,
        ],
        compiler_params=params(3 * piece.rows),
        cost_estimate=cost(piece.rows),
        name="source_chunk",
    )(x, codes, inflow)


def panel_starts(pieces):
    starts = [0]
    for piece in pieces:
        starts.append(starts[-1] + piece.count)
    return starts


def arrived_panels(chunks, pieces, codes, inflow):
    listed, starts = len(pieces), panel_starts(pieces)
    rows = sum(piece.rows for piece in pieces)
    kept = inflow is None

    def body(*refs):
        x_refs, d_ref = refs[:listed], refs[listed]
        in_ref = None if kept else refs[listed + 1]
        o_ref = refs[listed + 1 + (not kept)]
        row_refs = refs[listed + 2 :] if kept else [None] * listed
        for x_ref, row_ref, piece, start in zip(x_refs, row_refs, pieces, starts):
            carried = registers(in_ref, start, piece)
            store_registers(o_ref, start, sweep(x_ref, d_ref, carried, row_ref, piece.sizes))

    out = pl.pallas_call(
        body,
        out_shape=[jax.ShapeDtypeStruct((starts[-1], ROWS), jnp.float32)]
        + [piece.shape() for piece in pieces if kept],
        in_specs=[VMEM] * (listed + 1 + (not kept)),
        out_specs=[VMEM] * (1 + listed * kept),
        compiler_params=params(2 * rows),
        cost_estimate=cost(rows),
        name="arrived_panels",
    )(*chunks, codes, *([] if kept else [inflow]))
    return out[0], out[1:]


def head_result(chunks, pieces, result):
    listed = len(pieces)

    def body(*refs):
        x_refs, o_ref, sem = refs[:listed], refs[listed + 1], refs[-1]

        @pl.when(lax.axis_index("chain") == 0)
        def _():
            copies = [piece.leave(x_refs[i], o_ref, sem.at[i]) for i, piece in enumerate(pieces)]
            start_all(copies)
            wait_all(copies)

    return pl.pallas_call(
        body,
        out_shape=pieces[0].sizes.result(),
        in_specs=[VMEM] * listed + [HBM],
        out_specs=HBM,
        scratch_shapes=[pltpu.SemaphoreType.DMA((listed,))],
        input_output_aliases={listed: 0},
        compiler_params=params(sum(piece.rows for piece in pieces)),
        cost_estimate=cost(sum(piece.rows for piece in pieces)),
        name="head_result",
    )(*chunks, result)


def own_result(x, piece, codes, inflow, start):
    def body(x_ref, d_ref, in_ref, o_ref, buf, out, sem, out_sem):
        copies = piece.gather(x_ref, buf, sem)
        start_all(copies)
        wait_all(copies)
        sweep(buf, d_ref, registers(in_ref, start, piece), out, piece.sizes, outflow=False)
        copy = piece.leave(out, o_ref, out_sem)
        copy.start()
        copy.wait()

    return pl.pallas_call(
        body,
        out_shape=piece.sizes.result(),
        in_specs=[HBM, VMEM, VMEM],
        out_specs=HBM,
        scratch_shapes=[pltpu.VMEM((piece.rows, ROWS), jnp.float32)] * 2
        + [pltpu.SemaphoreType.DMA] * 2,
        compiler_params=params(2 * piece.rows),
        cost_estimate=cost(piece.rows),
        name="own_result",
    )(x, codes, inflow)


def arrived_result(chunks, pieces, codes, inflow, result):
    listed, starts = len(pieces), panel_starts(pieces)
    rows = sum(piece.rows for piece in pieces)

    def body(*refs):
        x_refs, d_ref, in_ref, o_ref = refs[:listed], refs[listed], refs[listed + 1], refs[listed + 3]
        outs, sem = refs[listed + 4 : -1], refs[-1]

        @pl.when(lax.axis_index("chain") > 0)
        def _():
            copies = []
            for i, piece in enumerate(pieces):
                halves = piece.leave_halves(outs[i], o_ref, sem.at[i])
                carried = registers(in_ref, starts[i], piece)
                sweep(
                    x_refs[i], d_ref, carried, outs[i], piece.sizes, outflow=False, halfway=halves[0].start
                )
                halves[1].start()
                copies += halves
            wait_all(copies)

    return pl.pallas_call(
        body,
        out_shape=pieces[0].sizes.result(),
        in_specs=[VMEM] * (listed + 2) + [HBM],
        out_specs=HBM,
        scratch_shapes=[pltpu.VMEM((piece.rows, ROWS), jnp.float32) for piece in pieces]
        + [pltpu.SemaphoreType.DMA((listed, 2))],
        input_output_aliases={listed + 2: 0},
        compiler_params=params(2 * rows),
        cost_estimate=cost(rows),
        name="arrived_result",
    )(*chunks, codes, inflow, result)


def place_chunk(chunk, piece, result):
    def body(x_ref, _, o_ref, sem):
        copy = piece.leave(x_ref, o_ref, sem)
        copy.start()
        copy.wait()

    return pl.pallas_call(
        body,
        out_shape=piece.sizes.result(),
        in_specs=[VMEM, HBM],
        out_specs=HBM,
        scratch_shapes=[pltpu.SemaphoreType.DMA],
        input_output_aliases={1: 0},
        compiler_params=params(piece.rows),
        cost_estimate=cost(piece.rows),
        name="place_chunk",
    )(chunk, result)


def local(runoff, directions):
    basins, chain = lax.axis_size("basin"), lax.axis_size("chain")
    _, members, all_tiles, _, cell_count = runoff.shape
    sizes = Sizes(members, directions.shape[0], cell_count // ROWS, basins)
    x = runoff.reshape(members, all_tiles * sizes.columns, ROWS)
    x = pltpu.with_memory_space_constraint(x, pltpu.HBM)
    codes = directions.reshape(sizes.per_member, ROWS)
    pairs = {k: exchange_pairs(basins, k) for k in range(basins)}

    far = basins - 1
    cut = max(SUB // sizes.tiles, members // 4)
    late = Piece(far, cut, members, sizes)
    head = Piece(far, 0, cut, sizes)
    near = [Piece(k, 0, members, sizes) for k in range(1, basins // 2)]
    across = [Piece(k, 0, members, sizes) for k in range(basins // 2, far)]

    code_rows = sizes.per_member // lax.axis_size("mem")
    pinned = pltpu.with_memory_space_constraint(codes, pltpu.HBM)
    first = lax.ppermute(pack_with_codes(x, head, pinned, code_rows), "basin", pairs[far])
    arrived = {head: first}
    far_codes = lax.all_gather(first[head.rows :], "mem", axis=0, tiled=True)
    for piece in across + near:
        arrived[piece] = lax.ppermute(pack(x, piece), "basin", pairs[piece.k])

    own = Piece(0, 0, members, sizes)
    source, source_codes, inflow = [late, own], [far_codes, codes], None
    for _ in range(chain - 1):
        inflow = from_behind(source_panels(x, source, source_codes, inflow), "chain")
    if inflow is None:
        inflow = jnp.zeros((panel_starts(source)[-1], ROWS), jnp.float32)
    result = own_result(x, own, codes, inflow, late.count)
    result, inflow = lax.optimization_barrier((result, inflow))
    finished = lax.ppermute(source_chunk(x, late, far_codes, inflow), "basin", pairs[far])
    for group in ([head] + near, across):
        chunks = [arrived[piece] for piece in group]
        result, chunks = lax.optimization_barrier((result, chunks))
        panel, rows = arrived_panels(chunks, group, codes, None)
        inflow = panel
        for step in range(chain - 1):
            inflow = from_behind(panel, "chain")
            if step < chain - 2:
                panel, _ = arrived_panels(chunks, group, codes, inflow)
        result = head_result(rows, group, result)
        result = arrived_result(chunks, group, codes, inflow, result)
    result = place_chunk(finished, late, result)
    return result.reshape(basins * members, sizes.tiles, 1, cell_count)


def solution(mesh):
    return jax.shard_map(
        local,
        mesh=mesh,
        in_specs=(P("mem", "basin", "grp", "chain", None), P(("grp", "basin"), "chain", None)),
        out_specs=P("mem", ("grp", "basin"), "chain", None),
        check_vma=False,
    )
```

```python
import jax
import jax.numpy as jnp
from jax import lax
from jax.experimental import pallas as pl
from jax.experimental.pallas import tpu as pltpu
from jax.sharding import PartitionSpec as P

ROWS = 128
SUB = 8
HBM = pl.BlockSpec(memory_space=pltpu.HBM)
VMEM = pl.BlockSpec(memory_space=pltpu.VMEM)


def exchange_pairs(count, k):
    return [(i, i ^ k) for i in range(count)]


def partner(k):
    return lax.axis_index("basin") ^ k


def from_behind(value, axis):
    count = lax.axis_size(axis)
    return lax.ppermute(value, axis, [(i, (i + 1) % count) for i in range(count)])


class Piece:
    def __init__(self, k, first, last, sizes):
        self.k, self.first, self.sizes = k, first, sizes
        self.members = last - first
        self.count = self.members * sizes.tiles
        self.rows = self.members * sizes.per_member
        self.groups = self.count // SUB

    def shape(self):
        return jax.ShapeDtypeStruct((self.rows, ROWS), jnp.float32)

    def panel(self):
        return jax.ShapeDtypeStruct((self.count, ROWS), jnp.float32)

    def gather(self, x_ref, buf_ref, sem):
        size = self.sizes.per_member
        tiles = x_ref.at[pl.ds(self.first, self.members), pl.ds(partner(self.k) * size, size)]
        return [pltpu.make_async_copy(tiles, buf_ref.at[pl.ds(0, self.rows)].reshape(self.members, size, ROWS), sem)]

    def place(self, o_ref):
        sizes = self.sizes
        start = (partner(self.k) * sizes.members + self.first) * sizes.tiles
        return o_ref.at[pl.ds(start, self.count)]

    def leave(self, x_ref, o_ref, sem):
        rows = x_ref.reshape(self.count, self.sizes.columns, ROWS)
        return pltpu.make_async_copy(rows, self.place(o_ref), sem)

    def leave_halves(self, x_ref, o_ref, sems):
        rows = x_ref.reshape(self.count, self.sizes.columns, ROWS)
        half = self.sizes.columns // 2
        return [
            pltpu.make_async_copy(
                rows.at[:, pl.ds(i * half, half)],
                self.place(o_ref).at[:, pl.ds(i * half, half)],
                sems.at[i],
            )
            for i in range(2)
        ]


class Sizes:
    def __init__(self, members, tiles, columns, basins):
        self.members, self.tiles, self.columns, self.basins = members, tiles, columns, basins
        self.per_member = tiles * columns

    def result(self):
        count = self.basins * self.members * self.tiles
        return jax.ShapeDtypeStruct((count, self.columns, ROWS), jnp.float32)


def column_offsets(d_ref, col, sizes):
    codes = d_ref[pl.ds(col, sizes.tiles, sizes.columns), :]
    codes = jnp.concatenate([codes] * (SUB // sizes.tiles), axis=0)
    lane = lax.broadcasted_iota(jnp.int32, codes.shape, 1)
    north = (codes == 1) & (lane > 0)
    south = (codes == 2) & (lane < ROWS - 1)
    return jnp.where(north, -1, jnp.where(south, 1, 0))


def composed(first, second):
    above, below = pltpu.roll(second, 1, 1), pltpu.roll(second, ROWS - 1, 1)
    return first + jnp.where(first == 0, second, jnp.where(first < 0, above, below))


def advance(summed, offsets, reach):
    zero = jnp.zeros_like(summed)
    moved = jnp.where(offsets == 0, summed, zero)
    for by in range(1, reach + 1):
        up = pltpu.roll(jnp.where(offsets == -by, summed, zero), ROWS - by, 1)
        down = pltpu.roll(jnp.where(offsets == by, summed, zero), by, 1)
        moved = moved + (up + down)
    return moved


def sweep(x_ref, d_ref, carried, o_ref, sizes, outflow=True, halfway=None):
    carried = list(carried)
    for col in range(0, sizes.columns, 2):
        first, second = (column_offsets(d_ref, c, sizes) for c in (col, col + 1))
        both = composed(first, second)
        last = col + 2 == sizes.columns and not outflow
        for g in range(len(carried)):
            at = g * SUB * sizes.columns + col
            here, after = pl.ds(at, SUB, sizes.columns), pl.ds(at + 1, SUB, sizes.columns)
            summed, water = x_ref[here, :], x_ref[after, :]
            if carried[g] is not None:
                summed = summed + carried[g]
            if not last:
                carried[g] = advance(water, second, 1) + advance(summed, both, 2)
            if o_ref is not None:
                o_ref[here, :] = summed
                o_ref[after, :] = water + advance(summed, first, 1)
        if halfway is not None and col + 2 == sizes.columns // 2:
            halfway()
    return carried


def registers(in_ref, start, piece):
    if in_ref is None:
        return [None] * piece.groups
    upstream = lax.axis_index("chain") > 0
    values = [in_ref[pl.ds(start + g * SUB, SUB), :] for g in range(piece.groups)]
    return [jnp.where(upstream, value, jnp.zeros_like(value)) for value in values]


def store_registers(o_ref, start, carried):
    for g, value in enumerate(carried):
        o_ref[pl.ds(start + g * SUB, SUB), :] = value


def start_all(copies):
    for copy in copies:
        copy.start()


def wait_all(copies):
    for copy in copies:
        copy.wait()


def params(rows):
    return pltpu.CompilerParams(vmem_limit_bytes=(rows + 4096) * ROWS * 4)


def cost(rows):
    return pl.CostEstimate(flops=rows * ROWS, bytes_accessed=rows * ROWS, transcendentals=0)


def pack(x, pieces):
    listed = len(pieces)
    rows = sum(piece.rows for piece in pieces)

    def body(x_ref, *refs):
        o_refs, sem = refs[:-1], refs[-1]
        copies = [piece.gather(x_ref, o_refs[i], sem.at[i]) for i, piece in enumerate(pieces)]
        for c in copies:
            start_all(c)
        for c in copies:
            wait_all(c)

    return pl.pallas_call(
        body,
        out_shape=[piece.shape() for piece in pieces],
        in_specs=[HBM],
        out_specs=[VMEM] * listed,
        scratch_shapes=[pltpu.SemaphoreType.DMA((listed,))],
        compiler_params=params(rows),
        cost_estimate=cost(rows),
        name="pack",
    )(x)


def pack_with_codes(x, piece, codes, code_rows):
    def body(x_ref, d_ref, o_ref, buf, sem, code_sem):
        copies = piece.gather(x_ref, o_ref, sem)
        start_all(copies)
        shares = codes.shape[0] // code_rows
        share = lax.axis_index("mem") if shares > 1 else 0
        mine = d_ref.at[pl.ds(pl.multiple_of(share * code_rows, code_rows), code_rows)]
        copy = pltpu.make_async_copy(mine, buf, code_sem)
        copy.start()
        copy.wait()
        o_ref[pl.ds(piece.rows, code_rows), :] = buf[...].astype(jnp.float32)
        wait_all(copies)

    return pl.pallas_call(
        body,
        out_shape=jax.ShapeDtypeStruct((piece.rows + code_rows, ROWS), jnp.float32),
        in_specs=[HBM, HBM],
        out_specs=VMEM,
        scratch_shapes=[
            pltpu.VMEM((code_rows, ROWS), codes.dtype),
            pltpu.SemaphoreType.DMA,
            pltpu.SemaphoreType.DMA,
        ],
        compiler_params=params(piece.rows),
        cost_estimate=cost(piece.rows),
        name="pack_with_codes",
    )(x, codes)


def source_panels(x, pieces, codes, inflow):
    listed, starts = len(pieces), panel_starts(pieces)
    rows = sum(piece.rows for piece in pieces)

    def body(x_ref, *refs):
        d_refs, in_ref = refs[:listed], refs[listed] if inflow is not None else None
        o_ref, bufs, sem = refs[-2 - listed], refs[-1 - listed : -1], refs[-1]
        copies = [piece.gather(x_ref, bufs[i], sem.at[i]) for i, piece in enumerate(pieces)]
        for c in copies:
            start_all(c)
        for i, piece in enumerate(pieces):
            wait_all(copies[i])
            size = piece.sizes.per_member
            codes_ref = d_refs[i].at[pl.ds(codes[i].shape[0] - size, size)]
            carried = registers(in_ref, starts[i], piece)
            store_registers(o_ref, starts[i], sweep(bufs[i], codes_ref, carried, None, piece.sizes))

    return pl.pallas_call(
        body,
        out_shape=jax.ShapeDtypeStruct((starts[-1], ROWS), jnp.float32),
        in_specs=[HBM] + [VMEM] * (listed + (inflow is not None)),
        out_specs=VMEM,
        scratch_shapes=[pltpu.VMEM((piece.rows, ROWS), jnp.float32) for piece in pieces]
        + [pltpu.SemaphoreType.DMA((listed,))],
        compiler_params=params(2 * rows),
        cost_estimate=cost(rows),
        name="source_panels",
    )(x, *codes, *([inflow] if inflow is not None else []))


def source_chunk(x, piece, codes, inflow):
    def body(x_ref, d_ref, in_ref, o_ref, buf, sem):
        copies = piece.gather(x_ref, buf, sem)
        start_all(copies)
        wait_all(copies)
        size = piece.sizes.per_member
        codes_ref = d_ref.at[pl.ds(codes.shape[0] - size, size)]
        sweep(buf, codes_ref, registers(in_ref, 0, piece), o_ref, piece.sizes, outflow=False)

    return pl.pallas_call(
        body,
        out_shape=piece.shape(),
        in_specs=[HBM, VMEM, VMEM],
        out_specs=VMEM,
        scratch_shapes=[
            pltpu.VMEM((piece.rows, ROWS), jnp.float32),
            pltpu.SemaphoreType.DMA,
        ],
        compiler_params=params(3 * piece.rows),
        cost_estimate=cost(piece.rows),
        name="source_chunk",
    )(x, codes, inflow)


def panel_starts(pieces):
    starts = [0]
    for piece in pieces:
        starts.append(starts[-1] + piece.count)
    return starts


def arrived_panels(chunks, pieces, codes, inflow):
    listed, starts = len(pieces), panel_starts(pieces)
    rows = sum(piece.rows for piece in pieces)
    kept = inflow is None

    def body(*refs):
        x_refs, d_ref = refs[:listed], refs[listed]
        in_ref = None if kept else refs[listed + 1]
        o_ref = refs[listed + 1 + (not kept)]
        row_refs = refs[listed + 2 :] if kept else [None] * listed
        for x_ref, row_ref, piece, start in zip(x_refs, row_refs, pieces, starts):
            carried = registers(in_ref, start, piece)
            store_registers(o_ref, start, sweep(x_ref, d_ref, carried, row_ref, piece.sizes))

    out = pl.pallas_call(
        body,
        out_shape=[jax.ShapeDtypeStruct((starts[-1], ROWS), jnp.float32)]
        + [piece.shape() for piece in pieces if kept],
        in_specs=[VMEM] * (listed + 1 + (not kept)),
        out_specs=[VMEM] * (1 + listed * kept),
        compiler_params=params(2 * rows),
        cost_estimate=cost(rows),
        name="arrived_panels",
    )(*chunks, codes, *([] if kept else [inflow]))
    return out[0], out[1:]


def head_result(chunks, pieces, result):
    listed = len(pieces)

    def body(*refs):
        x_refs, o_ref, sem = refs[:listed], refs[listed + 1], refs[-1]

        @pl.when(lax.axis_index("chain") == 0)
        def _():
            copies = [piece.leave(x_refs[i], o_ref, sem.at[i]) for i, piece in enumerate(pieces)]
            start_all(copies)
            wait_all(copies)

    return pl.pallas_call(
        body,
        out_shape=pieces[0].sizes.result(),
        in_specs=[VMEM] * listed + [HBM],
        out_specs=HBM,
        scratch_shapes=[pltpu.SemaphoreType.DMA((listed,))],
        input_output_aliases={listed: 0},
        compiler_params=params(sum(piece.rows for piece in pieces)),
        cost_estimate=cost(sum(piece.rows for piece in pieces)),
        name="head_result",
    )(*chunks, result)


def own_result(x, piece, codes, inflow, start):
    def body(x_ref, d_ref, in_ref, o_ref, buf, out, sem, out_sem):
        copies = piece.gather(x_ref, buf, sem)
        start_all(copies)
        wait_all(copies)
        sweep(buf, d_ref, registers(in_ref, start, piece), out, piece.sizes, outflow=False)
        copy = piece.leave(out, o_ref, out_sem)
        copy.start()
        copy.wait()

    return pl.pallas_call(
        body,
        out_shape=piece.sizes.result(),
        in_specs=[HBM, VMEM, VMEM],
        out_specs=HBM,
        scratch_shapes=[pltpu.VMEM((piece.rows, ROWS), jnp.float32)] * 2
        + [pltpu.SemaphoreType.DMA] * 2,
        compiler_params=params(2 * piece.rows),
        cost_estimate=cost(piece.rows),
        name="own_result",
    )(x, codes, inflow)


def arrived_result(chunks, pieces, codes, inflow, result):
    listed, starts = len(pieces), panel_starts(pieces)
    rows = sum(piece.rows for piece in pieces)

    def body(*refs):
        x_refs, d_ref, in_ref, o_ref = refs[:listed], refs[listed], refs[listed + 1], refs[listed + 3]
        outs, sem = refs[listed + 4 : -1], refs[-1]

        @pl.when(lax.axis_index("chain") > 0)
        def _():
            copies = []
            for i, piece in enumerate(pieces):
                halves = piece.leave_halves(outs[i], o_ref, sem.at[i])
                carried = registers(in_ref, starts[i], piece)
                sweep(
                    x_refs[i], d_ref, carried, outs[i], piece.sizes, outflow=False, halfway=halves[0].start
                )
                halves[1].start()
                copies += halves
            wait_all(copies)

    return pl.pallas_call(
        body,
        out_shape=pieces[0].sizes.result(),
        in_specs=[VMEM] * (listed + 2) + [HBM],
        out_specs=HBM,
        scratch_shapes=[pltpu.VMEM((piece.rows, ROWS), jnp.float32) for piece in pieces]
        + [pltpu.SemaphoreType.DMA((listed, 2))],
        input_output_aliases={listed + 2: 0},
        compiler_params=params(2 * rows),
        cost_estimate=cost(rows),
        name="arrived_result",
    )(*chunks, codes, inflow, result)


def place_chunk(chunk, piece, result):
    def body(x_ref, _, o_ref, sem):
        copy = piece.leave(x_ref, o_ref, sem)
        copy.start()
        copy.wait()

    return pl.pallas_call(
        body,
        out_shape=piece.sizes.result(),
        in_specs=[VMEM, HBM],
        out_specs=HBM,
        scratch_shapes=[pltpu.SemaphoreType.DMA],
        input_output_aliases={1: 0},
        compiler_params=params(piece.rows),
        cost_estimate=cost(piece.rows),
        name="place_chunk",
    )(chunk, result)


def local(runoff, directions):
    basins, chain = lax.axis_size("basin"), lax.axis_size("chain")
    _, members, all_tiles, _, cell_count = runoff.shape
    sizes = Sizes(members, directions.shape[0], cell_count // ROWS, basins)
    x = runoff.reshape(members, all_tiles * sizes.columns, ROWS)
    x = pltpu.with_memory_space_constraint(x, pltpu.HBM)
    codes = directions.reshape(sizes.per_member, ROWS)
    pairs = {k: exchange_pairs(basins, k) for k in range(basins)}

    far = basins - 1
    cut = max(SUB // sizes.tiles, members // 4)
    late = Piece(far, cut, members, sizes)
    head = Piece(far, 0, cut, sizes)
    near = [Piece(k, 0, members, sizes) for k in range(1, basins // 2)]
    across = [Piece(k, 0, members, sizes) for k in range(basins // 2, far)]

    code_rows = sizes.per_member // lax.axis_size("mem")
    pinned = pltpu.with_memory_space_constraint(codes, pltpu.HBM)
    first = lax.ppermute(pack_with_codes(x, head, pinned, code_rows), "basin", pairs[far])
    arrived = {head: first}
    far_codes = lax.all_gather(first[head.rows :], "mem", axis=0, tiled=True)
    for piece, chunk in zip(across + near, pack(x, across + near)):
        arrived[piece] = lax.ppermute(chunk, "basin", pairs[piece.k])

    own = Piece(0, 0, members, sizes)
    source, source_codes, inflow = [late, own], [far_codes, codes], None
    for _ in range(chain - 1):
        inflow = from_behind(source_panels(x, source, source_codes, inflow), "chain")
    if inflow is None:
        inflow = jnp.zeros((panel_starts(source)[-1], ROWS), jnp.float32)
    result = own_result(x, own, codes, inflow, late.count)
    result, inflow = lax.optimization_barrier((result, inflow))
    finished = lax.ppermute(source_chunk(x, late, far_codes, inflow), "basin", pairs[far])
    for group in ([head] + near, across):
        chunks = [arrived[piece] for piece in group]
        result, chunks = lax.optimization_barrier((result, chunks))
        panel, rows = arrived_panels(chunks, group, codes, None)
        inflow = panel
        for step in range(chain - 1):
            inflow = from_behind(panel, "chain")
            if step < chain - 2:
                panel, _ = arrived_panels(chunks, group, codes, inflow)
        result = head_result(rows, group, result)
        result = arrived_result(chunks, group, codes, inflow, result)
    result = place_chunk(finished, late, result)
    return result.reshape(basins * members, sizes.tiles, 1, cell_count)


def solution(mesh):
    return jax.shard_map(
        local,
        mesh=mesh,
        in_specs=(P("mem", "basin", "grp", "chain", None), P(("grp", "basin"), "chain", None)),
        out_specs=P("mem", ("grp", "basin"), "chain", None),
        check_vma=False,
    )
```

```python
import jax
import jax.numpy as jnp
from jax import lax
from jax.experimental import pallas as pl
from jax.experimental.pallas import tpu as pltpu
from jax.sharding import PartitionSpec as P

ROWS = 128
SUB = 8
HBM = pl.BlockSpec(memory_space=pltpu.HBM)
VMEM = pl.BlockSpec(memory_space=pltpu.VMEM)


def exchange_pairs(count, k):
    return [(i, i ^ k) for i in range(count)]


def partner(k):
    return lax.axis_index("basin") ^ k


def from_behind(value, axis):
    count = lax.axis_size(axis)
    return lax.ppermute(value, axis, [(i, (i + 1) % count) for i in range(count)])


class Piece:
    def __init__(self, k, first, last, sizes):
        self.k, self.first, self.sizes = k, first, sizes
        self.members = last - first
        self.count = self.members * sizes.tiles
        self.rows = self.members * sizes.per_member
        self.groups = self.count // SUB

    def shape(self):
        return jax.ShapeDtypeStruct((self.rows, ROWS), jnp.float32)

    def panel(self):
        return jax.ShapeDtypeStruct((self.count, ROWS), jnp.float32)

    def gather(self, x_ref, buf_ref, sem):
        size = self.sizes.per_member
        tiles = x_ref.at[pl.ds(self.first, self.members), pl.ds(partner(self.k) * size, size)]
        return [pltpu.make_async_copy(tiles, buf_ref.at[pl.ds(0, self.rows)].reshape(self.members, size, ROWS), sem)]

    def place(self, o_ref):
        sizes = self.sizes
        start = (partner(self.k) * sizes.members + self.first) * sizes.tiles
        return o_ref.at[pl.ds(start, self.count)]

    def leave(self, x_ref, o_ref, sem):
        rows = x_ref.reshape(self.count, self.sizes.columns, ROWS)
        return pltpu.make_async_copy(rows, self.place(o_ref), sem)

    def leave_halves(self, x_ref, o_ref, sems):
        rows = x_ref.reshape(self.count, self.sizes.columns, ROWS)
        half = self.sizes.columns // 2
        return [
            pltpu.make_async_copy(
                rows.at[:, pl.ds(i * half, half)],
                self.place(o_ref).at[:, pl.ds(i * half, half)],
                sems.at[i],
            )
            for i in range(2)
        ]


class Sizes:
    def __init__(self, members, tiles, columns, basins):
        self.members, self.tiles, self.columns, self.basins = members, tiles, columns, basins
        self.per_member = tiles * columns

    def result(self):
        count = self.basins * self.members * self.tiles
        return jax.ShapeDtypeStruct((count, self.columns, ROWS), jnp.float32)


def column_offsets(d_ref, col, sizes):
    codes = d_ref[pl.ds(col, sizes.tiles, sizes.columns), :]
    codes = jnp.concatenate([codes] * (SUB // sizes.tiles), axis=0)
    lane = lax.broadcasted_iota(jnp.int32, codes.shape, 1)
    north = (codes == 1) & (lane > 0)
    south = (codes == 2) & (lane < ROWS - 1)
    return jnp.where(north, -1, jnp.where(south, 1, 0))


def composed(first, second):
    above, below = pltpu.roll(second, 1, 1), pltpu.roll(second, ROWS - 1, 1)
    return first + jnp.where(first == 0, second, jnp.where(first < 0, above, below))


def advance(summed, offsets, reach):
    zero = jnp.zeros_like(summed)
    moved = jnp.where(offsets == 0, summed, zero)
    for by in range(1, reach + 1):
        up = pltpu.roll(jnp.where(offsets == -by, summed, zero), ROWS - by, 1)
        down = pltpu.roll(jnp.where(offsets == by, summed, zero), by, 1)
        moved = moved + (up + down)
    return moved


def sweep(x_ref, d_ref, carried, o_ref, sizes, outflow=True, halfway=None):
    carried = list(carried)
    for col in range(0, sizes.columns, 2):
        first, second = (column_offsets(d_ref, c, sizes) for c in (col, col + 1))
        both = composed(first, second)
        last = col + 2 == sizes.columns and not outflow
        for g in range(len(carried)):
            at = g * SUB * sizes.columns + col
            here, after = pl.ds(at, SUB, sizes.columns), pl.ds(at + 1, SUB, sizes.columns)
            summed, water = x_ref[here, :], x_ref[after, :]
            if carried[g] is not None:
                summed = summed + carried[g]
            if not last:
                carried[g] = advance(water, second, 1) + advance(summed, both, 2)
            if o_ref is not None:
                o_ref[here, :] = summed
                o_ref[after, :] = water + advance(summed, first, 1)
        if halfway is not None and col + 2 == sizes.columns // 2:
            halfway()
    return carried


def registers(in_ref, start, piece):
    if in_ref is None:
        return [None] * piece.groups
    upstream = lax.axis_index("chain") > 0
    values = [in_ref[pl.ds(start + g * SUB, SUB), :] for g in range(piece.groups)]
    return [jnp.where(upstream, value, jnp.zeros_like(value)) for value in values]


def store_registers(o_ref, start, carried):
    for g, value in enumerate(carried):
        o_ref[pl.ds(start + g * SUB, SUB), :] = value


def start_all(copies):
    for copy in copies:
        copy.start()


def wait_all(copies):
    for copy in copies:
        copy.wait()


def params(rows):
    return pltpu.CompilerParams(vmem_limit_bytes=(rows + 4096) * ROWS * 4)


def cost(rows):
    return pl.CostEstimate(flops=rows * ROWS, bytes_accessed=rows * ROWS, transcendentals=0)


def pack(x, piece):
    def body(x_ref, o_ref, sem):
        copies = piece.gather(x_ref, o_ref, sem)
        start_all(copies)
        wait_all(copies)

    return pl.pallas_call(
        body,
        out_shape=piece.shape(),
        in_specs=[HBM],
        out_specs=VMEM,
        scratch_shapes=[pltpu.SemaphoreType.DMA],
        compiler_params=params(piece.rows),
        cost_estimate=cost(piece.rows),
        name="pack",
    )(x)


def pack_with_codes(x, piece, codes, code_rows):
    def body(x_ref, d_ref, o_ref, buf, sem, code_sem):
        shares = codes.shape[0] // code_rows
        share = lax.axis_index("mem") if shares > 1 else 0
        mine = d_ref.at[pl.ds(pl.multiple_of(share * code_rows, code_rows), code_rows)]
        copy = pltpu.make_async_copy(mine, buf, code_sem)
        copy.start()
        copies = piece.gather(x_ref, o_ref, sem)
        start_all(copies)
        copy.wait()
        o_ref[pl.ds(piece.rows, code_rows), :] = buf[...].astype(jnp.float32)
        wait_all(copies)

    return pl.pallas_call(
        body,
        out_shape=jax.ShapeDtypeStruct((piece.rows + code_rows, ROWS), jnp.float32),
        in_specs=[HBM, HBM],
        out_specs=VMEM,
        scratch_shapes=[
            pltpu.VMEM((code_rows, ROWS), codes.dtype),
            pltpu.SemaphoreType.DMA,
            pltpu.SemaphoreType.DMA,
        ],
        compiler_params=params(piece.rows),
        cost_estimate=cost(piece.rows),
        name="pack_with_codes",
    )(x, codes)


def source_panels(x, pieces, codes, inflow):
    listed, starts = len(pieces), panel_starts(pieces)
    rows = sum(piece.rows for piece in pieces)

    def body(x_ref, *refs):
        d_refs, in_ref = refs[:listed], refs[listed] if inflow is not None else None
        o_ref, bufs, sem = refs[-2 - listed], refs[-1 - listed : -1], refs[-1]
        copies = [piece.gather(x_ref, bufs[i], sem.at[i]) for i, piece in enumerate(pieces)]
        for c in copies:
            start_all(c)
        for i, piece in enumerate(pieces):
            wait_all(copies[i])
            size = piece.sizes.per_member
            codes_ref = d_refs[i].at[pl.ds(codes[i].shape[0] - size, size)]
            carried = registers(in_ref, starts[i], piece)
            store_registers(o_ref, starts[i], sweep(bufs[i], codes_ref, carried, None, piece.sizes))

    return pl.pallas_call(
        body,
        out_shape=jax.ShapeDtypeStruct((starts[-1], ROWS), jnp.float32),
        in_specs=[HBM] + [VMEM] * (listed + (inflow is not None)),
        out_specs=VMEM,
        scratch_shapes=[pltpu.VMEM((piece.rows, ROWS), jnp.float32) for piece in pieces]
        + [pltpu.SemaphoreType.DMA((listed,))],
        compiler_params=params(2 * rows),
        cost_estimate=cost(rows),
        name="source_panels",
    )(x, *codes, *([inflow] if inflow is not None else []))


def source_chunk(x, piece, codes, inflow):
    def body(x_ref, d_ref, in_ref, o_ref, buf, sem):
        copies = piece.gather(x_ref, buf, sem)
        start_all(copies)
        wait_all(copies)
        size = piece.sizes.per_member
        codes_ref = d_ref.at[pl.ds(codes.shape[0] - size, size)]
        sweep(buf, codes_ref, registers(in_ref, 0, piece), o_ref, piece.sizes, outflow=False)

    return pl.pallas_call(
        body,
        out_shape=piece.shape(),
        in_specs=[HBM, VMEM, VMEM],
        out_specs=VMEM,
        scratch_shapes=[
            pltpu.VMEM((piece.rows, ROWS), jnp.float32),
            pltpu.SemaphoreType.DMA,
        ],
        compiler_params=params(3 * piece.rows),
        cost_estimate=cost(piece.rows),
        name="source_chunk",
    )(x, codes, inflow)


def panel_starts(pieces):
    starts = [0]
    for piece in pieces:
        starts.append(starts[-1] + piece.count)
    return starts


def arrived_panels(chunks, pieces, codes, inflow):
    listed, starts = len(pieces), panel_starts(pieces)
    rows = sum(piece.rows for piece in pieces)
    kept = inflow is None

    def body(*refs):
        x_refs, d_ref = refs[:listed], refs[listed]
        in_ref = None if kept else refs[listed + 1]
        o_ref = refs[listed + 1 + (not kept)]
        row_refs = refs[listed + 2 :] if kept else [None] * listed
        for x_ref, row_ref, piece, start in zip(x_refs, row_refs, pieces, starts):
            carried = registers(in_ref, start, piece)
            store_registers(o_ref, start, sweep(x_ref, d_ref, carried, row_ref, piece.sizes))

    out = pl.pallas_call(
        body,
        out_shape=[jax.ShapeDtypeStruct((starts[-1], ROWS), jnp.float32)]
        + [piece.shape() for piece in pieces if kept],
        in_specs=[VMEM] * (listed + 1 + (not kept)),
        out_specs=[VMEM] * (1 + listed * kept),
        compiler_params=params(2 * rows),
        cost_estimate=cost(rows),
        name="arrived_panels",
    )(*chunks, codes, *([] if kept else [inflow]))
    return out[0], out[1:]


def head_result(chunks, pieces, result):
    listed = len(pieces)

    def body(*refs):
        x_refs, o_ref, sem = refs[:listed], refs[listed + 1], refs[-1]

        @pl.when(lax.axis_index("chain") == 0)
        def _():
            copies = [piece.leave(x_refs[i], o_ref, sem.at[i]) for i, piece in enumerate(pieces)]
            start_all(copies)
            wait_all(copies)

    return pl.pallas_call(
        body,
        out_shape=pieces[0].sizes.result(),
        in_specs=[VMEM] * listed + [HBM],
        out_specs=HBM,
        scratch_shapes=[pltpu.SemaphoreType.DMA((listed,))],
        input_output_aliases={listed: 0},
        compiler_params=params(sum(piece.rows for piece in pieces)),
        cost_estimate=cost(sum(piece.rows for piece in pieces)),
        name="head_result",
    )(*chunks, result)


def own_result(x, piece, codes, inflow, start):
    def body(x_ref, d_ref, in_ref, o_ref, buf, out, sem, out_sem):
        copies = piece.gather(x_ref, buf, sem)
        start_all(copies)
        wait_all(copies)
        sweep(buf, d_ref, registers(in_ref, start, piece), out, piece.sizes, outflow=False)
        copy = piece.leave(out, o_ref, out_sem)
        copy.start()
        copy.wait()

    return pl.pallas_call(
        body,
        out_shape=piece.sizes.result(),
        in_specs=[HBM, VMEM, VMEM],
        out_specs=HBM,
        scratch_shapes=[pltpu.VMEM((piece.rows, ROWS), jnp.float32)] * 2
        + [pltpu.SemaphoreType.DMA] * 2,
        compiler_params=params(2 * piece.rows),
        cost_estimate=cost(piece.rows),
        name="own_result",
    )(x, codes, inflow)


def arrived_result(chunks, pieces, codes, inflow, result):
    listed, starts = len(pieces), panel_starts(pieces)
    rows = sum(piece.rows for piece in pieces)

    def body(*refs):
        x_refs, d_ref, in_ref, o_ref = refs[:listed], refs[listed], refs[listed + 1], refs[listed + 3]
        outs, sem = refs[listed + 4 : -1], refs[-1]

        @pl.when(lax.axis_index("chain") > 0)
        def _():
            copies = []
            for i, piece in enumerate(pieces):
                halves = piece.leave_halves(outs[i], o_ref, sem.at[i])
                carried = registers(in_ref, starts[i], piece)
                sweep(
                    x_refs[i], d_ref, carried, outs[i], piece.sizes, outflow=False, halfway=halves[0].start
                )
                halves[1].start()
                copies += halves
            wait_all(copies)

    return pl.pallas_call(
        body,
        out_shape=pieces[0].sizes.result(),
        in_specs=[VMEM] * (listed + 2) + [HBM],
        out_specs=HBM,
        scratch_shapes=[pltpu.VMEM((piece.rows, ROWS), jnp.float32) for piece in pieces]
        + [pltpu.SemaphoreType.DMA((listed, 2))],
        input_output_aliases={listed + 2: 0},
        compiler_params=params(2 * rows),
        cost_estimate=cost(rows),
        name="arrived_result",
    )(*chunks, codes, inflow, result)


def place_chunk(chunk, piece, result):
    def body(x_ref, _, o_ref, sem):
        copy = piece.leave(x_ref, o_ref, sem)
        copy.start()
        copy.wait()

    return pl.pallas_call(
        body,
        out_shape=piece.sizes.result(),
        in_specs=[VMEM, HBM],
        out_specs=HBM,
        scratch_shapes=[pltpu.SemaphoreType.DMA],
        input_output_aliases={1: 0},
        compiler_params=params(piece.rows),
        cost_estimate=cost(piece.rows),
        name="place_chunk",
    )(chunk, result)


def local(runoff, directions):
    basins, chain = lax.axis_size("basin"), lax.axis_size("chain")
    _, members, all_tiles, _, cell_count = runoff.shape
    sizes = Sizes(members, directions.shape[0], cell_count // ROWS, basins)
    x = runoff.reshape(members, all_tiles * sizes.columns, ROWS)
    x = pltpu.with_memory_space_constraint(x, pltpu.HBM)
    codes = directions.reshape(sizes.per_member, ROWS)
    pairs = {k: exchange_pairs(basins, k) for k in range(basins)}

    far = basins - 1
    cut = max(SUB // sizes.tiles, members // 4)
    late = Piece(far, cut, members, sizes)
    head = Piece(far, 0, cut, sizes)
    near = [Piece(k, 0, members, sizes) for k in range(1, basins // 2)]
    across = [Piece(k, 0, members, sizes) for k in range(basins // 2, far)]

    code_rows = sizes.per_member // lax.axis_size("mem")
    pinned = pltpu.with_memory_space_constraint(codes, pltpu.HBM)
    first = lax.ppermute(pack_with_codes(x, head, pinned, code_rows), "basin", pairs[far])
    arrived = {head: first}
    far_codes = lax.all_gather(first[head.rows :], "mem", axis=0, tiled=True)
    for piece in across + near:
        arrived[piece] = lax.ppermute(pack(x, piece), "basin", pairs[piece.k])

    own = Piece(0, 0, members, sizes)
    source, source_codes, inflow = [late, own], [far_codes, codes], None
    for _ in range(chain - 1):
        inflow = from_behind(source_panels(x, source, source_codes, inflow), "chain")
    if inflow is None:
        inflow = jnp.zeros((panel_starts(source)[-1], ROWS), jnp.float32)
    result = own_result(x, own, codes, inflow, late.count)
    result, inflow = lax.optimization_barrier((result, inflow))
    finished = lax.ppermute(source_chunk(x, late, far_codes, inflow), "basin", pairs[far])
    for group in ([head] + near, across):
        chunks = [arrived[piece] for piece in group]
        result, chunks = lax.optimization_barrier((result, chunks))
        panel, rows = arrived_panels(chunks, group, codes, None)
        inflow = panel
        for step in range(chain - 1):
            inflow = from_behind(panel, "chain")
            if step < chain - 2:
                panel, _ = arrived_panels(chunks, group, codes, inflow)
        result = head_result(rows, group, result)
        result = arrived_result(chunks, group, codes, inflow, result)
    result = place_chunk(finished, late, result)
    return result.reshape(basins * members, sizes.tiles, 1, cell_count)


def solution(mesh):
    return jax.shard_map(
        local,
        mesh=mesh,
        in_specs=(P("mem", "basin", "grp", "chain", None), P(("grp", "basin"), "chain", None)),
        out_specs=P("mem", ("grp", "basin"), "chain", None),
        check_vma=False,
    )
```
